32 devices in a mesh: enc: 2 (over x), dp: 16 (over z, y, core).
Axes of the slice: x: 2, y: 2, z: 4, core: 2. Of those that a mesh axis runs over, the one named last changes fastest.
Arguments:
- hidden_in: bfloat16 [2, 48, 256, 768], P('enc', 'dp'), may hold values from -6 to 6
- starts: int32 [2, 48, 4], P('enc', 'dp'), may hold values from 0 to 192, as said below
- positives: int32 [192], replicated, may hold values from 0 to 191, each once
- qkv_weight: bfloat16 [2, 768, 2304], P('enc'), may hold values from -0.21875 to 0.21875
- query_bias: float32 [2, 768], P('enc'), may hold values from -3 to 3
- value_bias: float32 [2, 768], P('enc'), may hold values from -3 to 3
- out_weight: bfloat16 [2, 768, 768], P('enc'), may hold values from -0.625 to 0.625
- out_bias: float32 [2, 768], P('enc'), may hold values from -3 to 3
- first_gain: float32 [2, 768], P('enc'), may hold values from 0.5 to 1.5
- first_shift: float32 [2, 768], P('enc'), may hold values from -3 to 3
- up_weight: bfloat16 [2, 768, 3072], P('enc'), may hold values from -0.21875 to 0.21875
- up_bias: float32 [2, 3072], P('enc'), may hold values from -3 to 3
- down_weight: bfloat16 [2, 3072, 768], P('enc'), may hold values from -0.109375 to 0.109375
- down_bias: float32 [2, 768], P('enc'), may hold values from -3 to 3
- second_gain: float32 [2, 768], P('enc'), may hold values from 0.5 to 1.5
- second_shift: float32 [2, 768], P('enc'), may hold values from -3 to 3
Outputs:
- loss_mean: float32 [], replicated
- hidden_out: bfloat16 [2, 48, 256, 768], P('enc', 'dp')
- hidden_grad: bfloat16 [2, 48, 256, 768], P('enc', 'dp')
- grad_qkv: float32 [2, 768, 2304], P('enc')
- grad_query_bias: float32 [2, 768], P('enc')
- grad_value_bias: float32 [2, 768], P('enc')
- grad_out_weight: float32 [2, 768, 768], P('enc')
- grad_out_bias: float32 [2, 768], P('enc')
- grad_first_gain: float32 [2, 768], P('enc')
- grad_first_shift: float32 [2, 768], P('enc')
- grad_up_weight: float32 [2, 768, 3072], P('enc')
- grad_up_bias: float32 [2, 3072], P('enc')
- grad_down_weight: float32 [2, 3072, 768], P('enc')
- grad_down_bias: float32 [2, 768], P('enc')
- grad_second_gain: float32 [2, 768], P('enc')
- grad_second_shift: float32 [2, 768], P('enc')
The draws below stay inside these ranges and needn't reach their ends.
Inputs may be any that keep to these rules, and one draw needn't show every extreme that they name: starts[e, r] are the first positions of the 4 documents packed into row r of encoder e, rising, the first 0; a document's CLS token stands at its start. For the questions (e = 0) they are 0, 64, 128 and 192; of the passages of a row one is exactly 128 long and the last is 64 long or longer. `positives`: the passage, numbered r * 4 + k over packed rows r and slots k, that answers question q (numbered alike); every passage answers exactly one question.
All inputs are finite; a program needn't handle non-finite values.
Results may differ from the reference program's by a relative error of at most 0.025.
Values may be sent and summed in bfloat16 or wider, within the bound.
A program may use at most 192 MiB of HBM per device.

```python
import math
import jax
import jax.numpy as jnp
from jax import lax

D = 768
H = 12
HD = 64
FF = 3072
L = 256
DOCS = 4
ROWS_DEV = 3
ROWS = 48
NQ = 192
N_DP = 16


def draw_starts(key, part):
    half = L // 2
    keys = jax.random.split(key, 4)
    first = jax.random.randint(keys[0], (ROWS,), L // 16, L // 8 + 1)
    second = jax.random.randint(keys[1], (ROWS,), L // 16, L // 8 + 1)
    third = half - first - second
    coin = jax.random.randint(keys[2], (ROWS,), 0, 2)
    ending = jnp.where(coin == 1, half, third)
    spared = jnp.where(coin == 1, third, half)
    trio = jnp.stack([first, second, spared], -1)
    offset = jax.random.randint(keys[3], (ROWS, 1), 0, 3)
    order = (jnp.arange(3, dtype=jnp.int32)[None, :] + offset) % 3
    trio = jnp.take_along_axis(trio, order, axis=1)
    lengths = jnp.concatenate([trio, ending[:, None]], -1)
    passage_starts = jnp.cumsum(lengths, -1) - lengths
    question_starts = jnp.broadcast_to(jnp.arange(4, dtype=jnp.int32) * (L // 4), (ROWS, 4))
    return jnp.stack([question_starts.astype(jnp.int32), passage_starts.astype(jnp.int32)]).astype(jnp.int32)


def block_scale(key, shape, pieces, low, largest):
    loudness, own = 1.0, jax.random.fold_in(key, 6)
    for dim, parts in pieces:
        draws = jnp.exp(jax.random.uniform(jax.random.fold_in(own, dim), (parts,), jnp.float32, low / len(pieces), largest / len(pieces)))
        loudness = loudness * jnp.repeat(draws, shape[dim] // parts).reshape([-1 if axis == dim else 1 for axis in range(len(shape))])
    return loudness


def normal_values(rng, shape, deviation, reach, pieces=(), kind=jnp.bfloat16):
    values = jax.random.normal(rng, shape, jnp.float32) * deviation
    if len(pieces) > 0:
        values = block_scale(rng, shape, pieces, -0.22, 0.18) * values
    return jnp.clip(values, min=-reach, max=reach).astype(kind)


def setup_inputs(seed: int = 0) -> dict:
    key_list = jax.random.split(jax.random.key(seed), 17)
    return {
        "hidden_in": normal_values(key_list[0], (2, ROWS, L, D), 1.0, 6.0, ((0, 2), (1, 16))),
        "starts": draw_starts(jax.random.fold_in(key_list[16], 71), 0),
        "positives": jax.random.permutation(key_list[2], NQ).astype(jnp.int32),
        "qkv_weight": normal_values(key_list[3], (2, D, 3 * D), D ** -0.5, 0.21875, ((0, 2),)),
        "query_bias": normal_values(key_list[4], (2, D), 0.5, 3.0, ((0, 2),), jnp.float32),
        "value_bias": normal_values(key_list[5], (2, D), 0.5, 3.0, ((0, 2),), jnp.float32),
        "out_weight": normal_values(key_list[6], (2, D, D), (D // 8) ** -0.5, 0.625, ((0, 2),)),
        "out_bias": normal_values(key_list[7], (2, D), 0.5, 3.0, ((0, 2),), jnp.float32),
        "first_gain": jnp.clip(1.0 + 0.1 * jax.random.normal(key_list[8], (2, D), jnp.float32), 0.5, 1.5),
        "first_shift": normal_values(key_list[9], (2, D), 0.5, 3.0, ((0, 2),), jnp.float32),
        "up_weight": normal_values(key_list[10], (2, D, FF), D ** -0.5, 0.21875, ((0, 2),)),
        "up_bias": normal_values(key_list[11], (2, FF), 0.5, 3.0, ((0, 2),), jnp.float32),
        "down_weight": normal_values(key_list[12], (2, FF, D), FF ** -0.5, 0.109375, ((0, 2),)),
        "down_bias": normal_values(key_list[13], (2, D), 0.5, 3.0, ((0, 2),), jnp.float32),
        "second_gain": jnp.clip(1.0 + 0.1 * jax.random.normal(key_list[14], (2, D), jnp.float32), 0.5, 1.5),
        "second_shift": normal_values(key_list[15], (2, D), 0.5, 3.0, ((0, 2),), jnp.float32),
    }


EPS_NORM = 1e-12
HIGH = lax.Precision.HIGHEST

@jax.custom_vjp
def low(v):
    return lax.optimization_barrier(v.astype(jnp.bfloat16)).astype(jnp.float32)

@jax.custom_vjp
def low_back(v):
    return v

def low_keep(v):
    return (low(v), None)

def low_pass(kept, grad):
    return (grad,)

def back_keep(v):
    return (v, None)

def back_low(kept, grad):
    return (low(grad),)
low.defvjp(low_keep, low_pass)
low_back.defvjp(back_keep, back_low)

def product(left, right):
    return jnp.dot(left, right, precision=HIGH, preferred_element_type=jnp.float32)

def layer_norm(hidden, gain, shift):
    centred = hidden - lax.optimization_barrier(jnp.mean(hidden, -1, keepdims=True))
    variance = lax.optimization_barrier(jnp.mean(centred * centred, -1, keepdims=True))
    return centred * lax.rsqrt(variance + EPS_NORM) * gain + shift

def encoder_rows(hidden, starts, params):
    qkv_weight, query_bias, value_bias, out_weight, out_bias, first_gain, first_shift, up_weight, up_bias, down_weight, down_bias, second_gain, second_shift = params
    groups = hidden.shape[0]
    flat = hidden.reshape(groups * L, D)
    qkv_shift = jnp.concatenate([query_bias, jnp.zeros_like(query_bias), value_bias])
    qkv = low(low_back(product(flat, qkv_weight) + qkv_shift))
    qkv = qkv.reshape(groups, L, 3, H, HD)
    query, key, value = (qkv[:, :, 0], qkv[:, :, 1], qkv[:, :, 2])
    places = jnp.arange(L, dtype=jnp.int32)
    segment = lax.optimization_barrier(jnp.sum((places[None, :, None] >= starts[:, None, :]).astype(jnp.int32), -1))
    allowed = (segment[:, :, None] == segment[:, None, :])[:, None]
    raw = jnp.einsum('gqhe,gkhe->ghqk', query, key, precision=HIGH)
    scores = jnp.where(allowed, HD ** (-0.5) * low_back(raw), -1e+30)
    probs = jax.nn.softmax(scores, axis=-1)
    mixed = jnp.einsum('ghqk,gkhe->gqhe', low(probs), value, precision=HIGH)
    mixed = low(low_back(mixed)).reshape(groups * L, D)
    attended = low_back(product(mixed, out_weight) + out_bias)
    normed = layer_norm(flat + attended, first_gain, first_shift)
    inner = low_back(product(low(normed), up_weight) + up_bias)
    activated = low(jax.nn.gelu(inner, approximate=False))
    outer = low_back(product(activated, down_weight) + down_bias)
    encoded = layer_norm(normed + outer, second_gain, second_shift)
    return encoded.reshape(groups, L, D)

def encode_half(hidden, starts, params):
    group = math.gcd(ROWS, max(1, 4096 // L))
    blocks = hidden.reshape(ROWS // group, group, L, D)
    start_blocks = starts.reshape(ROWS // group, group, DOCS)
    block_fn = jax.checkpoint(lambda pair: encoder_rows(pair[0], pair[1], params))
    return lax.map(block_fn, (blocks, start_blocks)).reshape(ROWS, L, D)

def forward(hidden, starts, positives, params):
    encoded = jnp.stack([encode_half(hidden[half], starts[half], tuple((p[half] for p in params))) for half in range(2)])
    places = jnp.arange(L, dtype=jnp.int32)
    picker = (places[None, None, None, :] == starts[:, :, :, None]).astype(jnp.float32)
    cls = jnp.einsum('erdl,erlw->erdw', picker, encoded, precision=HIGH)
    cls = low(cls.reshape(2, NQ, D))
    sims = D ** (-0.5) * low_back(product(cls[0], cls[1].T))
    log_total = jax.nn.logsumexp(sims, axis=-1)
    target = (jnp.arange(NQ, dtype=jnp.int32)[None, :] == positives[:, None]).astype(jnp.float32)
    total = jnp.sum(log_total - lax.optimization_barrier(jnp.sum(sims * target, -1))) / (DOCS * ROWS_DEV)
    return (total, encoded)

def reference(hidden_in, starts, positives, qkv_weight, query_bias, value_bias, out_weight, out_bias, first_gain, first_shift, up_weight, up_bias, down_weight, down_bias, second_gain, second_shift):
    floats = tuple((a.astype(jnp.float32) for a in (hidden_in, qkv_weight, query_bias, value_bias, out_weight, out_bias, first_gain, first_shift, up_weight, up_bias, down_weight, down_bias, second_gain, second_shift)))

    def objective(hidden, *params):
        return forward(hidden, starts, positives, params)
    total, pullback, encoded = jax.vjp(objective, *floats, has_aux=True)
    grads = pullback(jnp.ones_like(total))
    return (total / N_DP, encoded.astype(jnp.bfloat16), grads[0].astype(jnp.bfloat16), grads[1], grads[2], grads[3], grads[4], grads[5], grads[6], grads[7], grads[8], grads[9], grads[10], grads[11], grads[12], grads[13])
```

```python
import functools

import jax
import jax.numpy as jnp
from jax import lax
from jax.experimental import pallas as pl
from jax.experimental.pallas import tpu as pltpu
from jax.sharding import PartitionSpec as P

OWNERS = 16
H = 12
DOCS = 4


EPS_NORM = 1e-12


def partner(value, axis, distance):
    mask = 2**distance
    pairs = [(source, source ^ mask) for source in range(lax.axis_size(axis))]
    return lax.ppermute(value, axis, pairs)


def product(left, right):
    return jnp.dot(left, right, preferred_element_type=jnp.float32)


def layer_stats(hidden):
    centred = hidden - jnp.mean(hidden, -1, keepdims=True)
    inverse = lax.rsqrt(jnp.mean(centred * centred, -1, keepdims=True) + EPS_NORM)
    return (centred * inverse, inverse)


def norm_back(upstream, normal, inverse, gain):
    scaled = upstream * gain
    return inverse * (
        scaled
        - jnp.mean(scaled, -1, keepdims=True)
        - normal * jnp.mean(scaled * normal, -1, keepdims=True)
    )


def on_device(
    hidden_in,
    starts,
    positives,
    qkv_weight,
    query_bias,
    value_bias,
    out_weight,
    out_bias,
    first_gain,
    first_shift,
    up_weight,
    up_bias,
    down_weight,
    down_bias,
    second_gain,
    second_shift,
):
    rows, length, width = (hidden_in.shape[1], hidden_in.shape[2], hidden_in.shape[3])
    heads = H
    head_size = width // heads
    tokens = rows * length
    flat = hidden_in.reshape(tokens, width)
    w_qkv = qkv_weight[0]
    w_out = out_weight[0]
    w_up = up_weight[0]
    w_down = down_weight[0]
    row_starts = starts[0]
    qkv_shift = jnp.concatenate([query_bias[0], jnp.zeros_like(query_bias[0]), value_bias[0]])
    qkv = (product(flat, w_qkv) + qkv_shift).astype(jnp.bfloat16)
    split = qkv.reshape(rows, length, 3, heads, head_size)
    query, key, value = (split[:, :, 0], split[:, :, 1], split[:, :, 2])
    places = jnp.arange(length, dtype=jnp.int32)
    segment = jnp.sum((places[None, :, None] >= row_starts[:, None, :]).astype(jnp.int32), -1)
    allowed = (segment[:, :, None] == segment[:, None, :])[:, None]
    head_scale = head_size ** (-0.5)

    def attention_scores(left, right):
        raw = jnp.einsum("rqhe,rkhe->rhqk", left, right, preferred_element_type=jnp.float32)
        return jnp.where(allowed, head_scale * raw, -1e30)

    scores = attention_scores(query, key)
    peak = jnp.max(scores, -1, keepdims=True)
    log_total = peak + jnp.log(jnp.sum(jnp.exp(scores - peak), -1, keepdims=True))
    weights_low = jnp.exp(scores - log_total).astype(jnp.bfloat16)
    mixed = jnp.einsum("rhqk,rkhe->rqhe", weights_low, value, preferred_element_type=jnp.float32)
    mixed = mixed.astype(jnp.bfloat16).reshape(tokens, width)
    attended = product(mixed, w_out) + out_bias[0]
    first_normal, first_inverse = layer_stats(flat.astype(jnp.float32) + attended)
    normed = first_normal * first_gain[0] + first_shift[0]
    normed_low = normed.astype(jnp.bfloat16)
    inner = product(normed_low, w_up) + up_bias[0]
    activated_low = jax.nn.gelu(inner, approximate=False).astype(jnp.bfloat16)
    outer = product(activated_low, w_down) + down_bias[0]
    second_normal, second_inverse = layer_stats(normed + outer)
    encoded = second_normal * second_gain[0] + second_shift[0]
    hidden_out = encoded.astype(jnp.bfloat16).reshape(1, rows, length, width)
    picker = (places[None, None, :] == row_starts[:, :, None]).astype(jnp.float32)
    cls = jnp.einsum(
        "rdl,rlw->rdw",
        picker,
        encoded.reshape(rows, length, width),
        precision=lax.Precision.HIGHEST,
    )
    local_count = rows * DOCS
    cls_low = cls.reshape(local_count, width).astype(jnp.bfloat16)
    first_half = lax.axis_index("enc") == 0
    mine = lax.all_gather(cls_low, "dp", axis=0, tiled=True)
    other = partner(mine, "enc", 0)
    questions = jnp.where(first_half, mine, other)
    passages = jnp.where(first_half, other, mine)
    count = questions.shape[0]
    sim_scale = width ** (-0.5)
    sims = sim_scale * jnp.einsum(
        "qw,pw->qp", questions, passages, preferred_element_type=jnp.float32
    )
    sim_peak = jnp.max(sims, -1, keepdims=True)
    sim_total = sim_peak + jnp.log(jnp.sum(jnp.exp(sims - sim_peak), -1, keepdims=True))
    target = (jnp.arange(count, dtype=jnp.int32)[None, :] == positives[:, None]).astype(jnp.float32)
    total = jnp.sum(sim_total[:, 0] - jnp.sum(sims * target, -1)) / local_count
    loss_mean = total / lax.axis_size("dp")
    d_sims_low = (sim_scale * (jnp.exp(sims - sim_total) - target) / local_count).astype(
        jnp.bfloat16
    )
    own_start = lax.axis_index("dp") * local_count
    own_rows = lax.dynamic_slice_in_dim(d_sims_low, own_start, local_count, 0)
    own_columns = lax.dynamic_slice_in_dim(d_sims_low, own_start, local_count, 1)
    d_questions = jnp.einsum("qp,pw->qw", own_rows, passages, preferred_element_type=jnp.float32)
    d_passages = jnp.einsum("qp,qw->pw", own_columns, questions, preferred_element_type=jnp.float32)
    d_cls = jnp.where(first_half, d_questions, d_passages).reshape(rows, DOCS, width)
    d_encoded = jnp.einsum("rdl,rdw->rlw", picker, d_cls, precision=lax.Precision.HIGHEST).reshape(
        tokens, width
    )
    grad_second_gain = jnp.sum(d_encoded * second_normal, 0)
    grad_second_shift = jnp.sum(d_encoded, 0)
    d_second = norm_back(d_encoded, second_normal, second_inverse, second_gain[0])
    d_outer_low = d_second.astype(jnp.bfloat16)
    grad_down_bias = jnp.sum(d_outer_low.astype(jnp.float32), 0)
    grad_down_weight = jnp.einsum(
        "tf,tw->fw", activated_low, d_outer_low, preferred_element_type=jnp.float32
    )
    d_activated = jnp.einsum("tw,fw->tf", d_outer_low, w_down, preferred_element_type=jnp.float32)
    normal_cdf = 0.5 * (1.0 + lax.erf(inner * 0.7071067811865476))
    slope = normal_cdf + inner * jnp.exp(-0.5 * inner * inner) * 0.3989422804014327
    d_inner_low = (d_activated * slope).astype(jnp.bfloat16)
    grad_up_bias = jnp.sum(d_inner_low.astype(jnp.float32), 0)
    grad_up_weight = jnp.einsum(
        "tw,tf->wf", normed_low, d_inner_low, preferred_element_type=jnp.float32
    )
    d_normed = d_second + jnp.einsum(
        "tf,wf->tw", d_inner_low, w_up, preferred_element_type=jnp.float32
    )
    grad_first_gain = jnp.sum(d_normed * first_normal, 0)
    grad_first_shift = jnp.sum(d_normed, 0)
    d_first = norm_back(d_normed, first_normal, first_inverse, first_gain[0])
    d_attended_low = d_first.astype(jnp.bfloat16)
    grad_out_bias = jnp.sum(d_attended_low.astype(jnp.float32), 0)
    grad_out_weight = jnp.einsum(
        "tv,tw->vw", mixed, d_attended_low, preferred_element_type=jnp.float32
    )
    d_mixed_low = jnp.einsum(
        "tw,vw->tv", d_attended_low, w_out, preferred_element_type=jnp.float32
    ).astype(jnp.bfloat16)
    d_mixed_heads = d_mixed_low.reshape(rows, length, heads, head_size)
    probs_again = jnp.exp(attention_scores(query, key) - log_total)
    weights_again = probs_again.astype(jnp.bfloat16)
    grad_value = jnp.einsum(
        "rhqk,rqhe->rkhe", weights_again, d_mixed_heads, preferred_element_type=jnp.float32
    )
    d_weights = jnp.einsum(
        "rqhe,rkhe->rhqk", d_mixed_heads, value, preferred_element_type=jnp.float32
    )
    d_scores = probs_again * (d_weights - jnp.sum(d_weights * probs_again, -1, keepdims=True))
    d_raw_low = (head_scale * d_scores).astype(jnp.bfloat16)
    grad_query = jnp.einsum("rhqk,rkhe->rqhe", d_raw_low, key, preferred_element_type=jnp.float32)
    grad_key = jnp.einsum("rhqk,rqhe->rkhe", d_raw_low, query, preferred_element_type=jnp.float32)
    d_qkv_low = (
        jnp.stack([grad_query, grad_key, grad_value], 2)
        .reshape(tokens, 3 * width)
        .astype(jnp.bfloat16)
    )
    grad_qkv_local = jnp.einsum("tw,tv->wv", flat, d_qkv_low, preferred_element_type=jnp.float32)
    bias_sums = jnp.sum(d_qkv_low.astype(jnp.float32), 0)
    grad_query_local = bias_sums[:width]
    grad_value_local = bias_sums[2 * width :]
    d_input = d_first + jnp.einsum(
        "tv,wv->tw", d_qkv_low, w_qkv, preferred_element_type=jnp.float32
    )
    hidden_grad = d_input.astype(jnp.bfloat16).reshape(1, rows, length, width)
    (
        share_qkv,
        share_query_bias,
        share_value_bias,
        share_out_weight,
        share_out_bias,
        share_first_gain,
        share_first_shift,
        share_up_weight,
        share_up_bias,
        share_down_weight,
        share_down_bias,
        share_second_gain,
        share_second_shift,
    ) = (
        lax.psum_scatter(grad_qkv_local[None], "dp", scatter_dimension=1, tiled=True),
        lax.psum_scatter(grad_query_local[None], "dp", scatter_dimension=1, tiled=True),
        lax.psum_scatter(grad_value_local[None], "dp", scatter_dimension=1, tiled=True),
        lax.psum_scatter(grad_out_weight[None], "dp", scatter_dimension=1, tiled=True),
        lax.psum_scatter(grad_out_bias[None], "dp", scatter_dimension=1, tiled=True),
        lax.psum_scatter(grad_first_gain[None], "dp", scatter_dimension=1, tiled=True),
        lax.psum_scatter(grad_first_shift[None], "dp", scatter_dimension=1, tiled=True),
        lax.psum_scatter(grad_up_weight[None], "dp", scatter_dimension=1, tiled=True),
        lax.psum_scatter(grad_up_bias[None], "dp", scatter_dimension=1, tiled=True),
        lax.psum_scatter(grad_down_weight[None], "dp", scatter_dimension=1, tiled=True),
        lax.psum_scatter(grad_down_bias[None], "dp", scatter_dimension=1, tiled=True),
        lax.psum_scatter(grad_second_gain[None], "dp", scatter_dimension=1, tiled=True),
        lax.psum_scatter(grad_second_shift[None], "dp", scatter_dimension=1, tiled=True),
    )
    summed = (
        lax.all_gather(share_qkv.astype(jnp.bfloat16), "dp", axis=1, tiled=True).astype(
            share_qkv.dtype
        ),
        lax.all_gather(share_query_bias.astype(jnp.bfloat16), "dp", axis=1, tiled=True).astype(
            share_query_bias.dtype
        ),
        lax.all_gather(share_value_bias.astype(jnp.bfloat16), "dp", axis=1, tiled=True).astype(
            share_value_bias.dtype
        ),
        lax.all_gather(share_out_weight.astype(jnp.bfloat16), "dp", axis=1, tiled=True).astype(
            share_out_weight.dtype
        ),
        lax.all_gather(share_out_bias.astype(jnp.bfloat16), "dp", axis=1, tiled=True).astype(
            share_out_bias.dtype
        ),
        lax.all_gather(share_first_gain.astype(jnp.bfloat16), "dp", axis=1, tiled=True).astype(
            share_first_gain.dtype
        ),
        lax.all_gather(share_first_shift.astype(jnp.bfloat16), "dp", axis=1, tiled=True).astype(
            share_first_shift.dtype
        ),
        lax.all_gather(share_up_weight.astype(jnp.bfloat16), "dp", axis=1, tiled=True).astype(
            share_up_weight.dtype
        ),
        lax.all_gather(share_up_bias.astype(jnp.bfloat16), "dp", axis=1, tiled=True).astype(
            share_up_bias.dtype
        ),
        lax.all_gather(share_down_weight.astype(jnp.bfloat16), "dp", axis=1, tiled=True).astype(
            share_down_weight.dtype
        ),
        lax.all_gather(share_down_bias.astype(jnp.bfloat16), "dp", axis=1, tiled=True).astype(
            share_down_bias.dtype
        ),
        lax.all_gather(share_second_gain.astype(jnp.bfloat16), "dp", axis=1, tiled=True).astype(
            share_second_gain.dtype
        ),
        lax.all_gather(share_second_shift.astype(jnp.bfloat16), "dp", axis=1, tiled=True).astype(
            share_second_shift.dtype
        ),
    )
    return (
        loss_mean,
        hidden_out,
        hidden_grad,
        summed[0],
        summed[1],
        summed[2],
        summed[3],
        summed[4],
        summed[5],
        summed[6],
        summed[7],
        summed[8],
        summed[9],
        summed[10],
        summed[11],
        summed[12],
    )


PAD = 16
BF = jnp.bfloat16
F32 = jnp.float32
MESH = pl.DeviceIdType.MESH
NEG = -1e30
ROOT_HALF = 0.7071067811865476
PEAK = 0.3989422804014327


def nn(left, right):
    return jnp.dot(left, right, preferred_element_type=F32)


def nt(left, right):
    return lax.dot_general(left, right, (((1,), (1,)), ((), ())), preferred_element_type=F32)


def tn(left, right):
    return lax.dot_general(left, right, (((0,), (0,)), ((), ())), preferred_element_type=F32)


def iota(shape, dim):
    return lax.broadcasted_iota(jnp.int32, shape, dim)


def gelu_parts(inner):
    cdf = 0.5 * (1.0 + lax.erf(inner * ROOT_HALF))
    return cdf, jnp.exp(-0.5 * inner * inner) * PEAK


def chunk(index, size):
    return pl.ds(pl.multiple_of(index * size, size), size)


def loop(count, body):
    def step(index, carry):
        body(index)
        return carry

    lax.fori_loop(0, count, step, 0)


def main_kernel(
    n,
    starts,
    positives,
    x_hbm,
    qkv_hbm,
    q_bias,
    v_bias,
    out_hbm,
    o_bias,
    gain1,
    shift1,
    up_hbm,
    u_bias,
    down_hbm,
    d_bias,
    gain2,
    shift2,
    hidden_out,
    hidden_grad,
    xcls_o,
    mixed_o,
    normed_o,
    act_o,
    douter_o,
    dinner_o,
    datt_o,
    dq_o,
    kv_o,
    vecs,
    up_sum,
    x,
    w_qkv,
    w_out,
    w_up,
    w_down,
    kv,
    q,
    mix,
    seg_bias,
    qbd,
    dbd,
    probs,
    p_low,
    ds_low,
    spread,
    xcls,
    mixed,
    cls,
    normed,
    norm1,
    inv1,
    norm2,
    inv2,
    act,
    slope,
    dinner,
    douter,
    datt,
    dmix,
    d_cls,
    dfirst,
    acc,
    turned,
    recv,
    piece,
    dq_own,
    normed_t,
    low_t,
    acc_t,
    hout,
    hgrad,
    load_sem,
    save_sem,
    xs_sem,
    xr_sem,
    ms_sem,
    mr_sem,
    vs_sem,
    ks_sem,
    pr_sem,
    cs_sem,
    cr_sem,
    qs_sem,
    qr_sem,
    gs_sem,
    gr_sem,
):
    enc = lax.axis_index("enc")
    me = lax.axis_index("dp")
    other = 1 - enc
    core = lax.rem(me, 2)
    sibling = me + 1 - 2 * core
    width = x.shape[1]
    tokens = x.shape[0]
    ff = w_up.shape[1]
    wide = n * PAD
    rows = starts.shape[0] // DOCS
    length = tokens // rows
    local = rows * DOCS
    head = width // H
    pairs = H // 2
    head_scale = head ** (-0.5)
    group_cols = width // 4
    half_feats = width // 2
    group_rows = H // 4 * PAD

    loads = [
        pltpu.make_async_copy(x_hbm, x, load_sem.at[0]),
        pltpu.make_async_copy(
            qkv_hbm.at[:, pl.ds(width, 2 * width)], w_qkv.at[:, pl.ds(width, 2 * width)], load_sem.at[1]
        ),
        pltpu.make_async_copy(
            qkv_hbm.at[:, pl.ds(0, width)], w_qkv.at[:, pl.ds(0, width)], load_sem.at[2]
        ),
        pltpu.make_async_copy(out_hbm, w_out, load_sem.at[3]),
        pltpu.make_async_copy(up_hbm, w_up, load_sem.at[4]),
        pltpu.make_async_copy(down_hbm, w_down, load_sem.at[5]),
    ]
    for copy in loads:
        copy.start()

    barrier = pltpu.get_barrier_semaphore()

    def greet(j):
        peer = lax.rem(me + j + 1, n)
        pl.semaphore_signal(barrier, inc=1, device_id=(enc, peer), device_id_type=MESH)

    loop(n - 1, greet)
    pl.semaphore_signal(barrier, inc=1, device_id=(other, me), device_id_type=MESH)

    def to_all(source, target, send, receive):
        def go(j):
            peer = lax.rem(me + j + 1, n)
            pltpu.make_async_remote_copy(
                src_ref=source,
                dst_ref=target,
                send_sem=send.at[j],
                recv_sem=receive.at[me],
                device_id=(enc, peer),
                device_id_type=MESH,
            ).start()

        loop(n - 1, go)

    def from_all(source, target_of, send, receive):
        def wait(j):
            peer = lax.rem(me + j + 1, n)
            copy = pltpu.make_async_remote_copy(
                src_ref=source,
                dst_ref=target_of(peer),
                send_sem=send.at[j],
                recv_sem=receive.at[peer],
                device_id=(enc, peer),
                device_id_type=MESH,
            )
            copy.wait_send()
            copy.wait_recv()

        loop(n - 1, wait)

    first_col = jnp.full((PAD, 1), -1, jnp.int32)
    seg_col = jnp.full((PAD, 1), -1, jnp.int32)
    place_col = iota((PAD, 1), 0)
    segs = []
    for r in range(rows):
        place = iota((1, length), 1)
        count = jnp.zeros((1, length), jnp.int32)
        for k in range(DOCS):
            start = starts[r * DOCS + k]
            count = count + (place >= start).astype(jnp.int32)
            order = jnp.int32(0)
            for m in range(DOCS):
                order = order + jnp.where(starts[r * DOCS + m] <= start, 1, 0)
            here = place_col == r * DOCS + k
            first_col = jnp.where(here, r * length + start, first_col)
            seg_col = jnp.where(here, r * 8 + order, seg_col)
        segs.append(count + r * 8)
    seg_row = jnp.concatenate(segs, axis=1)
    pick = (iota((PAD, tokens), 1) == first_col).astype(F32).astype(BF)
    allowed = seg_row == seg_col

    own_rows = pl.ds(pl.multiple_of(me * PAD, PAD), PAD)

    def rows_of(ref):
        return lambda peer: ref.at[pl.ds(pl.multiple_of(peer * PAD, PAD), PAD)]

    loads[0].wait()
    xcls[own_rows, :] = nn(pick, x[...]).astype(BF)
    pl.semaphore_wait(barrier, n)
    to_all(xcls.at[own_rows], xcls.at[own_rows], xs_sem, xr_sem)

    loads[1].wait()

    def kv_step(j):
        cols = chunk(j, 256)
        y = nn(x[...], w_qkv[:, pl.ds(pl.multiple_of(width + j * 256, 256), 256)])
        kv[:, cols] = y.astype(BF)

    loop(width // 256, kv_step)

    def v_step(j):
        cols = chunk(j, 256)
        y = nn(x[...], w_qkv[:, pl.ds(pl.multiple_of(2 * width + j * 256, 256), 256)])
        kv[:, pl.ds(pl.multiple_of(width + j * 256, 256), 256)] = (y + v_bias[:, cols]).astype(BF)

    loop(width // 256, v_step)

    low_half = iota((1, 128), 1) < head

    def block_diagonal(target, rows16):
        for p in range(pairs):
            part = rows16[:, p * 128 : (p + 1) * 128]
            even = jnp.where(low_half, part, 0.0).astype(BF)
            odd = jnp.where(low_half, 0.0, part).astype(BF)
            target[pl.ds(2 * p * PAD, PAD), pl.ds(p * 128, 128)] = even
            target[pl.ds((2 * p + 1) * PAD, PAD), pl.ds(p * 128, 128)] = odd

    def own_lanes(full):
        parts = []
        for p in range(pairs):
            lanes = slice(p * 128, (p + 1) * 128)
            even = full[2 * p * PAD : (2 * p + 1) * PAD, lanes]
            odd = full[(2 * p + 1) * PAD : (2 * p + 2) * PAD, lanes]
            parts.append(jnp.where(low_half, even, odd))
        return jnp.concatenate(parts, axis=1)

    loads[2].wait()
    q_own = (nn(xcls[own_rows, :], w_qkv[:, pl.ds(0, width)]) + q_bias[...]).astype(BF).astype(F32)
    qbd[...] = jnp.zeros_like(qbd)
    dbd[...] = jnp.zeros_like(dbd)
    block_diagonal(qbd, q_own)
    allowed_all = jnp.concatenate([allowed] * H, axis=0)
    scores = jnp.where(allowed_all, head_scale * nt(qbd[...], kv[:, pl.ds(0, width)]), NEG)
    peak = jnp.max(scores, -1, keepdims=True)
    raw = jnp.where(allowed_all, jnp.exp(scores - peak), 0.0)
    total = jnp.sum(raw, -1, keepdims=True)
    weights = raw / jnp.where(total > 0.0, total, 1.0)
    probs[...] = weights
    p_low[...] = weights.astype(BF)
    mixed[own_rows, :] = own_lanes(nn(p_low[...], kv[:, pl.ds(width, width)])).astype(BF)
    to_all(mixed.at[own_rows], mixed.at[own_rows], ms_sem, mr_sem)

    def send_pieces(side, send, slot):
        for i in range(8):
            owner = 2 * i + side
            source = spread.at[
                slot,
                pl.ds((i % 4) * group_rows, group_rows),
                pl.ds((i // 4) * half_feats, half_feats),
            ]

            @pl.when(me != owner)
            def _():
                pltpu.make_async_remote_copy(
                    src_ref=source,
                    dst_ref=recv.at[me],
                    send_sem=send.at[i],
                    recv_sem=pr_sem.at[me],
                    device_id=(enc, owner),
                    device_id_type=MESH,
                ).start()

            @pl.when(me == owner)
            def _():
                recv[me] = source[...]

    def sent_pieces(side, send, slot):
        for i in range(8):
            owner = 2 * i + side
            source = spread.at[
                slot,
                pl.ds((i % 4) * group_rows, group_rows),
                pl.ds((i // 4) * half_feats, half_feats),
            ]

            @pl.when(me != owner)
            def _():
                pltpu.make_async_remote_copy(
                    src_ref=source,
                    dst_ref=recv.at[me],
                    send_sem=send.at[i],
                    recv_sem=pr_sem.at[me],
                    device_id=(enc, owner),
                    device_id_type=MESH,
                ).wait_send()

    spread[0] = nn(p_low[...], x[...]).astype(BF)
    send_pieces(1, vs_sem, 0)

    def q_step(j):
        cols = chunk(j, 256)
        y = nn(x[...], w_qkv[:, cols]) + q_bias[:, cols]
        q[:, cols] = (y.astype(BF).astype(F32) * head_scale).astype(BF)

    loop(width // 256, q_step)

    def attend_row(r):
        place0 = iota((length, 1), 0)
        place1 = iota((1, length), 1)
        count0 = jnp.zeros((length, 1), jnp.int32)
        count1 = jnp.zeros((1, length), jnp.int32)
        for k in range(DOCS):
            start = starts[r * DOCS + k]
            count0 = count0 + (place0 >= start).astype(jnp.int32)
            count1 = count1 + (place1 >= start).astype(jnp.int32)
        seg_bias[...] = jnp.where(count0 == count1, 0.0, NEG)
        these = chunk(r, length)
        mask_even = jnp.where(low_half, 1.0, 0.0).astype(BF)
        mask_odd = jnp.where(low_half, 0.0, 1.0).astype(BF)

        def attend_pair(p):
            lanes = chunk(p, 128)
            query = q[these, lanes]
            key = kv[these, lanes]
            value = kv[these, pl.ds(pl.multiple_of(width + p * 128, 128), 128)]
            ext = jnp.concatenate([value, jnp.ones_like(value)], axis=1)
            outs = []
            for mask in (mask_even, mask_odd):
                s = nt(query * mask, key) + seg_bias[...]
                e = jnp.exp(s - jnp.max(s, -1, keepdims=True)).astype(BF)
                outs.append(nn(e, ext))
            even, odd = outs
            top = jnp.where(low_half, even[:, :128], odd[:, :128])
            low = jnp.where(low_half, even[:, 128:], odd[:, 128:])
            mix[these, lanes] = (top / low).astype(BF)

        loop(pairs, attend_pair)

    loop(rows, attend_row)

    def saver(source, target, index):
        return pltpu.make_async_copy(source, target, save_sem.at[index])

    saves = []

    def save(source, target, index):
        copy = saver(source, target, index)
        copy.start()
        saves.append(copy)

    from_all(xcls.at[own_rows], rows_of(xcls), xs_sem, xr_sem)
    save(xcls, xcls_o, 0)
    from_all(mixed.at[own_rows], rows_of(mixed), ms_sem, mr_sem)
    save(mixed, mixed_o, 1)
    loads[3].wait()

    def out_step(j):
        cols = chunk(j, 256)
        acc[:, cols] = nn(mixed[...], w_out[:, cols]) + o_bias[:, cols] + xcls[:, cols].astype(F32)

    loop(width // 256, out_step)

    def stats(h):
        centred = h - jnp.mean(h, -1, keepdims=True)
        inverse = lax.rsqrt(jnp.mean(centred * centred, -1, keepdims=True) + EPS_NORM)
        return centred * inverse, inverse

    unit, inverse = stats(acc[...])
    norm1[...] = unit
    inv1[...] = jnp.broadcast_to(inverse, inv1.shape)
    level = unit * gain1[...] + shift1[...]
    normed[...] = level
    low_t[...] = level.astype(BF)
    loads[4].wait()
    loads[5].wait()
    acc[...] = level + d_bias[...]

    def ff_step(j):
        cols = chunk(j, 512)
        inner = nn(low_t[...], w_up[:, cols]) + u_bias[:, cols]
        cdf, pdf = gelu_parts(inner)
        slope[:, cols] = cdf + inner * pdf
        active = (inner * cdf).astype(BF)
        act[:, cols] = active
        acc[...] += nn(active, w_down[cols, :])

    loop(ff // 512, ff_step)
    normed_keep = saver(low_t, normed_o, 2)
    normed_keep.start()
    save(act, act_o, 3)
    unit, inverse = stats(acc[...])
    norm2[...] = unit
    inv2[...] = jnp.broadcast_to(inverse, inv2.shape)
    cls[enc] = (unit * gain2[...] + shift2[...]).astype(BF)
    half = wide // 2
    mine = pl.ds(pl.multiple_of(core * half, half), half)
    theirs = pl.ds(pl.multiple_of((1 - core) * half, half), half)
    cross = pltpu.make_async_remote_copy(
        src_ref=cls.at[enc, mine],
        dst_ref=cls.at[enc, mine],
        send_sem=cs_sem.at[0],
        recv_sem=cr_sem.at[0],
        device_id=(other, me),
        device_id_type=MESH,
    )
    cross.start()
    cross_in = pltpu.make_async_remote_copy(
        src_ref=cls.at[enc, mine],
        dst_ref=cls.at[other, mine],
        send_sem=cs_sem.at[0],
        recv_sem=cr_sem.at[0],
        device_id=(other, me),
        device_id_type=MESH,
    )
    pass_on = pltpu.make_async_remote_copy(
        src_ref=cls.at[other, mine],
        dst_ref=cls.at[other, mine],
        send_sem=cs_sem.at[1],
        recv_sem=cr_sem.at[1],
        device_id=(enc, sibling),
        device_id_type=MESH,
    )
    pass_in = pltpu.make_async_remote_copy(
        src_ref=cls.at[other, mine],
        dst_ref=cls.at[other, theirs],
        send_sem=cs_sem.at[1],
        recv_sem=cr_sem.at[1],
        device_id=(enc, sibling),
        device_id_type=MESH,
    )

    place_row = iota((1, wide), 1)

    def place_step(device, row):
        for k in range(local):
            target = positives[device * local + k]
            padded = target + (PAD - local) * lax.div(target, local)
            row = jnp.where(place_row == device * PAD + k, padded, row)
        return row

    pos_row = lax.fori_loop(0, n, place_step, jnp.full((1, wide), -1, jnp.int32))

    @pl.when(core == 0)
    def _():
        for j in range(width // 256):
            cols = pl.ds(j * 256, 256)
            y = (nn(xcls[...], w_qkv[:, cols]) + q_bias[:, cols]).astype(BF).astype(F32)
            turned[pl.ds(j * 256, 256), :] = y.T.astype(BF)

    normed_keep.wait()

    def layer_tile(r):
        these = chunk(r, length)

        def tile_out(j):
            cols = chunk(j, 256)
            y = nn(mix[these, :], w_out[:, cols]) + o_bias[:, cols]
            acc_t[:, cols] = y + x[these, cols].astype(F32)

        loop(width // 256, tile_out)
        unit, _ = stats(acc_t[...])
        level = unit * gain1[...] + shift1[...]
        normed_t[...] = level
        low_t[...] = level.astype(BF)
        acc_t[...] = level + d_bias[...]

        def tile_ff(j):
            cols = chunk(j, 512)
            inner = nn(low_t[...], w_up[:, cols]) + u_bias[:, cols]
            active = 0.5 * inner * (1.0 + lax.erf(inner * ROOT_HALF))
            acc_t[...] += nn(active.astype(BF), w_down[cols, :])

        loop(ff // 512, tile_ff)
        unit, _ = stats(acc_t[...])
        hout[these, :] = (unit * gain2[...] + shift2[...]).astype(BF)

    def save_tile(r):
        these = pl.ds(r * length, length)
        save(hout.at[these], hidden_out.at[these], 8 + r)

    layer_tile(0)
    save_tile(0)

    cross.wait_send()
    cross_in.wait_recv()
    pass_on.start()
    pass_on.wait_send()
    pass_in.wait_recv()

    sim_scale = width ** (-0.5)
    good_col = lax.rem(iota((wide, 1), 0), PAD) < local
    good_row = lax.rem(iota((1, wide), 1), PAD) < local
    raw_sims = sim_scale * nt(cls[1], cls[0])
    sims = jnp.where(good_col, raw_sims, NEG)
    sim_peak = jnp.max(sims, 0, keepdims=True)
    sim_total = sim_peak + jnp.log(jnp.sum(jnp.exp(sims - sim_peak), 0, keepdims=True))
    target = (iota((wide, wide), 0) == pos_row).astype(F32)
    losses = sim_total - jnp.sum(raw_sims * target, 0, keepdims=True)
    loss = jnp.sum(jnp.where(good_row, losses, 0.0), -1, keepdims=True) / (local * n)
    d_sims = sim_scale * (jnp.exp(sims - sim_total) - target) / local
    d_sims = jnp.where(good_row, d_sims, 0.0).astype(BF)

    @pl.when(enc == 0)
    def _():
        d_cls[...] = tn(d_sims, cls[1])

    @pl.when(enc == 1)
    def _():
        d_cls[...] = nn(d_sims, cls[0])

    def column_sum(value):
        return jnp.sum(value, 0, keepdims=True)

    def back(upstream, unit, inverse, gain):
        scaled = upstream * gain
        return inverse[:, :1] * (
            scaled
            - jnp.mean(scaled, -1, keepdims=True)
            - unit * jnp.mean(scaled * unit, -1, keepdims=True)
        )

    vecs[pl.ds(0, 1), :] = column_sum(d_cls[...] * norm2[...])
    vecs[pl.ds(1, 1), :] = column_sum(d_cls[...])
    d_second = back(d_cls[...], norm2[...], inv2[...], gain2[...])
    acc[...] = d_second
    d_outer = d_second.astype(BF)
    douter[...] = d_outer
    save(douter, douter_o, 4)
    vecs[pl.ds(2, 1), :] = column_sum(d_outer.astype(F32))

    def ff_back(j):
        cols = chunk(j, 512)
        d_active = nt(douter[...], w_down[cols, :])
        d_low = (d_active * slope[:, cols]).astype(BF)
        dinner[:, cols] = d_low
        up_sum[:, cols] = column_sum(d_low.astype(F32))
        acc[...] += nt(d_low, w_up[:, cols])

    loop(ff // 512, ff_back)
    save(dinner, dinner_o, 5)
    vecs[pl.ds(3, 1), :] = column_sum(acc[...] * norm1[...])
    vecs[pl.ds(4, 1), :] = column_sum(acc[...])
    d_first = back(acc[...], norm1[...], inv1[...], gain1[...])
    dfirst[...] = d_first
    d_low = d_first.astype(BF)
    datt[...] = d_low
    save(datt, datt_o, 6)
    vecs[pl.ds(5, 1), :] = column_sum(d_low.astype(F32))

    def mix_back(j):
        cols = chunk(j, 256)
        dmix[:, cols] = nt(datt[...], w_out[cols, :]).astype(BF)

    loop(width // 256, mix_back)
    vecs[pl.ds(6, 1), :] = column_sum(dmix[...].astype(F32))
    vecs[pl.ds(7, 1), :] = jnp.broadcast_to(loss, (1, width))

    which = lax.div(me, 2)
    group = lax.rem(which, 4)
    part = lax.div(which, 4)
    piece_cols = pl.ds(pl.multiple_of(group * group_cols, group_cols), group_cols)
    piece_feats = pl.ds(pl.multiple_of(part * half_feats, half_feats), half_feats)

    def sum_pieces():
        def wait(j):
            peer = lax.rem(me + j + 1, n)
            pltpu.make_async_remote_copy(
                src_ref=recv.at[peer],
                dst_ref=recv.at[peer],
                send_sem=vs_sem.at[0],
                recv_sem=pr_sem.at[peer],
                device_id=(enc, peer),
                device_id_type=MESH,
            ).wait_recv()

        loop(n - 1, wait)
        for a in range(H // 4):
            right = recv[:, pl.ds(a * PAD, PAD), :].reshape(wide, half_feats)
            left = turned[pl.ds(pl.multiple_of(group * group_cols + a * head, head), head), :]
            piece[pl.ds(a * head, head), :] = nn(left, right).astype(BF)
        target = kv_o.at[core, piece_cols, piece_feats]
        to_all(piece, target, gs_sem, gr_sem)
        saver(piece, target, 7).start()

    @pl.when(core == 1)
    def _():
        for j in range(width // 256):
            cols = pl.ds(j * 256, 256)
            turned[pl.ds(j * 256, 256), :] = dmix[:, cols].astype(F32).T.astype(BF)
        sum_pieces()

    d_own = dmix[own_rows, :].astype(F32)
    block_diagonal(dbd, d_own)
    d_weights = nt(dbd[...], kv[:, pl.ds(width, width)])
    weights = probs[...]
    inner_sum = jnp.sum(d_weights * weights, -1, keepdims=True)
    ds_low[...] = (head_scale * weights * (d_weights - inner_sum)).astype(BF)
    spread[1] = nn(ds_low[...], x[...]).astype(BF)
    send_pieces(0, ks_sem, 1)
    d_query = own_lanes(nn(ds_low[...], kv[:, pl.ds(0, width)])).astype(BF)
    dq_own[...] = d_query
    to_all(dq_own, dq_o.at[own_rows], qs_sem, qr_sem)
    save(dq_own, dq_o.at[own_rows], 11)

    layer_tile(1)
    save_tile(1)

    @pl.when(core == 0)
    def _():
        sum_pieces()

    layer_tile(2)
    save_tile(2)

    spread_q = nt(qbd[...], w_qkv[:, pl.ds(width, width)]).astype(BF)
    spread_v = nt(dbd[...], w_qkv[:, pl.ds(2 * width, width)]).astype(BF)
    base = dfirst[own_rows, :] + nt(dq_own[...], w_qkv[:, pl.ds(0, width)])
    base = base.astype(BF)
    for r in range(rows):
        these = slice(r * length, (r + 1) * length)
        y = tn(ds_low[:, these], spread_q) + tn(p_low[:, these], spread_v) + tn(pick[:, these], base)
        hgrad[pl.ds(r * length, length), :] = y.astype(BF)
    save(hgrad, hidden_grad, 12)

    sent_pieces(1, vs_sem, 0)
    sent_pieces(0, ks_sem, 1)
    from_all(dq_own, rows_of(dq_o), qs_sem, qr_sem)

    def grad_of(peer):
        other_which = lax.div(peer, 2)
        return kv_o.at[
            lax.rem(peer, 2),
            pl.ds(pl.multiple_of(lax.rem(other_which, 4) * group_cols, group_cols), group_cols),
            pl.ds(pl.multiple_of(lax.div(other_which, 4) * half_feats, half_feats), half_feats),
        ]

    from_all(piece, grad_of, gs_sem, gr_sem)
    saver(piece, kv_o.at[core, piece_cols, piece_feats], 7).wait()
    for copy in saves:
        copy.wait()


def grad_kernel(
    xcls_i,
    mixed_i,
    normed_i,
    act_i,
    douter_i,
    dinner_i,
    datt_i,
    dq_i,
    kv_i,
    hidden_out_i,
    hidden_grad_i,
    vecs,
    up_sum,
    loss,
    hidden_out,
    hidden_grad,
    grad_qkv,
    grad_query_bias,
    grad_value_bias,
    grad_out,
    grad_out_bias,
    grad_first_gain,
    grad_first_shift,
    grad_up,
    grad_up_bias,
    grad_down,
    grad_down_bias,
    grad_second_gain,
    grad_second_shift,
    xcls,
    mixed,
    normed,
    act,
    douter,
    dinner,
    datt,
    dq,
    kv,
    g_qkv,
    g_out,
    g_up,
    g_down,
    in_sem,
    out_sem,
):
    width = xcls.shape[1]
    ff = act.shape[1]
    pairs = [
        (act_i, act),
        (douter_i, douter),
        (normed_i, normed),
        (dinner_i, dinner),
        (mixed_i, mixed),
        (datt_i, datt),
        (xcls_i, xcls),
        (dq_i, dq),
        (kv_i, kv),
    ]
    ins = [pltpu.make_async_copy(a, b, in_sem.at[i]) for i, (a, b) in enumerate(pairs)]
    for copy in ins:
        copy.start()
    through = [
        pltpu.make_async_copy(hidden_out_i, hidden_out, out_sem.at[0]),
        pltpu.make_async_copy(hidden_grad_i, hidden_grad, out_sem.at[1]),
    ]
    for copy in through:
        copy.start()

    loss[...] = vecs[pl.ds(7, 1), pl.ds(0, 1)]
    grad_second_gain[...] = vecs[pl.ds(0, 1), :]
    grad_second_shift[...] = vecs[pl.ds(1, 1), :]
    grad_down_bias[...] = vecs[pl.ds(2, 1), :]
    grad_first_gain[...] = vecs[pl.ds(3, 1), :]
    grad_first_shift[...] = vecs[pl.ds(4, 1), :]
    grad_out_bias[...] = vecs[pl.ds(5, 1), :]
    grad_value_bias[...] = vecs[pl.ds(6, 1), :]
    grad_up_bias[...] = up_sum[...]

    ins[0].wait()
    ins[1].wait()

    def down_step(j):
        these = chunk(j, 256)
        g_down[these, :] = tn(act[:, these], douter[...])
        pltpu.make_async_copy(g_down.at[these], grad_down.at[0, these], out_sem.at[2]).start()

    loop(ff // 256, down_step)
    ins[2].wait()
    ins[3].wait()

    def up_step(j):
        these = chunk(j, 128)
        g_up[these, :] = tn(normed[:, these], dinner[...])
        pltpu.make_async_copy(g_up.at[these], grad_up.at[0, these], out_sem.at[3]).start()

    loop(width // 128, up_step)
    ins[4].wait()
    ins[5].wait()

    def out_step(j):
        these = chunk(j, 128)
        g_out[these, :] = tn(mixed[:, these], datt[...])
        pltpu.make_async_copy(g_out.at[these], grad_out.at[0, these], out_sem.at[4]).start()

    loop(width // 128, out_step)
    ins[6].wait()
    ins[7].wait()
    ins[8].wait()
    grad_query_bias[...] = jnp.sum(dq[...].astype(F32), 0, keepdims=True)

    def qkv_step(j):
        these = chunk(j, 128)
        g_qkv[these, pl.ds(0, width)] = tn(xcls[:, these], dq[...])
        for m in range(2):
            g_qkv[these, pl.ds((m + 1) * width, width)] = kv[m, :, these].astype(F32).T
        pltpu.make_async_copy(g_qkv.at[these], grad_qkv.at[0, these], out_sem.at[5]).start()

    loop(width // 128, qkv_step)
    pltpu.make_async_copy(g_down, grad_down.at[0], out_sem.at[2]).wait()
    pltpu.make_async_copy(g_up, grad_up.at[0], out_sem.at[3]).wait()
    pltpu.make_async_copy(g_out, grad_out.at[0], out_sem.at[4]).wait()
    pltpu.make_async_copy(g_qkv, grad_qkv.at[0], out_sem.at[5]).wait()
    for copy in through:
        copy.wait()


def fused_on_device(n, *args):
    (
        hidden_in,
        starts,
        positives,
        qkv_weight,
        query_bias,
        value_bias,
        out_weight,
        out_bias,
        first_gain,
        first_shift,
        up_weight,
        up_bias,
        down_weight,
        down_bias,
        second_gain,
        second_shift,
    ) = args
    rows, length, width = hidden_in.shape[1:]
    tokens = rows * length
    ff = up_weight.shape[-1]
    wide = n * PAD
    spreads = H * PAD
    shape = jax.ShapeDtypeStruct
    hbm = pl.BlockSpec(memory_space=pl.ANY)
    vmem = pl.BlockSpec(memory_space=pltpu.VMEM)
    smem = pl.BlockSpec(memory_space=pltpu.SMEM)
    dma = pltpu.SemaphoreType.DMA
    limit = 60 * 1024 * 1024
    outs = pl.pallas_call(
        functools.partial(main_kernel, n),
        out_shape=[
            shape((tokens, width), BF),
            shape((tokens, width), BF),
            shape((wide, width), BF),
            shape((wide, width), BF),
            shape((wide, width), BF),
            shape((wide, ff), BF),
            shape((wide, width), BF),
            shape((wide, ff), BF),
            shape((wide, width), BF),
            shape((wide, width), BF),
            shape((2, width, width), BF),
            shape((8, width), F32),
            shape((1, ff), F32),
        ],
        in_specs=[smem, smem, hbm, hbm, vmem, vmem, hbm, vmem, vmem, vmem, hbm, vmem, hbm, vmem, vmem, vmem],
        out_specs=[hbm] * 11 + [vmem] * 2,
        scratch_shapes=[
            pltpu.VMEM((tokens, width), BF),
            pltpu.VMEM((width, 3 * width), BF),
            pltpu.VMEM((width, width), BF),
            pltpu.VMEM((width, ff), BF),
            pltpu.VMEM((ff, width), BF),
            pltpu.VMEM((tokens, 2 * width), BF),
            pltpu.VMEM((tokens, width), BF),
            pltpu.VMEM((tokens, width), BF),
            pltpu.VMEM((length, length), F32),
            pltpu.VMEM((spreads, width), BF),
            pltpu.VMEM((spreads, width), BF),
            pltpu.VMEM((spreads, tokens), F32),
            pltpu.VMEM((spreads, tokens), BF),
            pltpu.VMEM((spreads, tokens), BF),
            pltpu.VMEM((2, spreads, width), BF),
            pltpu.VMEM((wide, width), BF),
            pltpu.VMEM((wide, width), BF),
            pltpu.VMEM((2, wide, width), BF),
            pltpu.VMEM((wide, width), F32),
            pltpu.VMEM((wide, width), F32),
            pltpu.VMEM((wide, 128), F32),
            pltpu.VMEM((wide, width), F32),
            pltpu.VMEM((wide, 128), F32),
            pltpu.VMEM((wide, ff), BF),
            pltpu.VMEM((wide, ff), F32),
            pltpu.VMEM((wide, ff), BF),
            pltpu.VMEM((wide, width), BF),
            pltpu.VMEM((wide, width), BF),
            pltpu.VMEM((wide, width), BF),
            pltpu.VMEM((wide, width), F32),
            pltpu.VMEM((wide, width), F32),
            pltpu.VMEM((wide, width), F32),
            pltpu.VMEM((width, wide), BF),
            pltpu.VMEM((n, H // 4 * PAD, width // 2), BF),
            pltpu.VMEM((width // 4, width // 2), BF),
            pltpu.VMEM((PAD, width), BF),
            pltpu.VMEM((length, width), F32),
            pltpu.VMEM((length, width), BF),
            pltpu.VMEM((length, width), F32),
            pltpu.VMEM((tokens, width), BF),
            pltpu.VMEM((tokens, width), BF),
            dma((6,)),
            dma((13,)),
            dma((n,)),
            dma((n,)),
            dma((n,)),
            dma((n,)),
            dma((8,)),
            dma((8,)),
            dma((n,)),
            dma((2,)),
            dma((2,)),
            dma((n,)),
            dma((n,)),
            dma((n,)),
            dma((n,)),
        ],
        compiler_params=pltpu.CompilerParams(
            collective_id=0, has_side_effects=True, vmem_limit_bytes=limit
        ),
        name="layer",
    )(
        starts.reshape(rows * DOCS),
        positives,
        hidden_in.reshape(tokens, width),
        qkv_weight.reshape(width, 3 * width),
        query_bias,
        value_bias,
        out_weight.reshape(width, width),
        out_bias,
        first_gain,
        first_shift,
        up_weight.reshape(width, ff),
        up_bias,
        down_weight.reshape(ff, width),
        down_bias,
        second_gain,
        second_shift,
    )
    (h_out, h_grad, xcls, mixed, normed, act, douter, dinner, datt, dq, kv, vecs, up_sum) = outs
    row = shape((1, width), F32)
    grads = pl.pallas_call(
        grad_kernel,
        out_shape=[
            shape((1, 1), F32),
            shape((tokens, width), BF),
            shape((tokens, width), BF),
            shape((1, width, 3 * width), F32),
            row,
            row,
            shape((1, width, width), F32),
            row,
            row,
            row,
            shape((1, width, ff), F32),
            shape((1, ff), F32),
            shape((1, ff, width), F32),
            row,
            row,
            row,
        ],
        in_specs=[hbm] * 11 + [vmem] * 2,
        out_specs=[vmem, hbm, hbm, hbm, vmem, vmem, hbm, vmem, vmem, vmem, hbm, vmem, hbm, vmem, vmem, vmem],
        scratch_shapes=[
            pltpu.VMEM((wide, width), BF),
            pltpu.VMEM((wide, width), BF),
            pltpu.VMEM((wide, width), BF),
            pltpu.VMEM((wide, ff), BF),
            pltpu.VMEM((wide, width), BF),
            pltpu.VMEM((wide, ff), BF),
            pltpu.VMEM((wide, width), BF),
            pltpu.VMEM((wide, width), BF),
            pltpu.VMEM((2, width, width), BF),
            pltpu.VMEM((width, 3 * width), F32),
            pltpu.VMEM((width, width), F32),
            pltpu.VMEM((width, ff), F32),
            pltpu.VMEM((ff, width), F32),
            dma((9,)),
            dma((6,)),
        ],
        compiler_params=pltpu.CompilerParams(vmem_limit_bytes=limit),
        name="gradients",
    )(xcls, mixed, normed, act, douter, dinner, datt, dq, kv, h_out, h_grad, vecs, up_sum)
    block = (1, rows, length, width)
    return (
        grads[0].reshape(()),
        grads[1].reshape(block),
        grads[2].reshape(block),
        *grads[3:],
    )


def solution(mesh):
    placed = (
        P("enc", "dp", None, None),
        P("enc", "dp", None),
        P(),
        P("enc", None, None),
        P("enc", None),
        P("enc", None),
        P("enc", None, None),
        P("enc", None),
        P("enc", None),
        P("enc", None),
        P("enc", None, None),
        P("enc", None),
        P("enc", None, None),
        P("enc", None),
        P("enc", None),
        P("enc", None),
    )
    n = mesh.shape["dp"]
    body = functools.partial(fused_on_device, n) if n == OWNERS else on_device
    return jax.shard_map(
        body,
        mesh=mesh,
        in_specs=placed,
        out_specs=(
            P(),
            P("enc", "dp", None, None),
            P("enc", "dp", None, None),
            P("enc", None, None),
            P("enc", None),
            P("enc", None),
            P("enc", None, None),
            P("enc", None),
            P("enc", None),
            P("enc", None),
            P("enc", None, None),
            P("enc", None),
            P("enc", None, None),
            P("enc", None),
            P("enc", None),
            P("enc", None),
        ),
        check_vma=False,
    )
```

```python
import functools

import jax
import jax.numpy as jnp
from jax import lax
from jax.experimental import pallas as pl
from jax.experimental.pallas import tpu as pltpu
from jax.sharding import PartitionSpec as P

OWNERS = 16
H = 12
DOCS = 4


EPS_NORM = 1e-12


def partner(value, axis, distance):
    mask = 2**distance
    pairs = [(source, source ^ mask) for source in range(lax.axis_size(axis))]
    return lax.ppermute(value, axis, pairs)


def product(left, right):
    return jnp.dot(left, right, preferred_element_type=jnp.float32)


def layer_stats(hidden):
    centred = hidden - jnp.mean(hidden, -1, keepdims=True)
    inverse = lax.rsqrt(jnp.mean(centred * centred, -1, keepdims=True) + EPS_NORM)
    return (centred * inverse, inverse)


def norm_back(upstream, normal, inverse, gain):
    scaled = upstream * gain
    return inverse * (
        scaled
        - jnp.mean(scaled, -1, keepdims=True)
        - normal * jnp.mean(scaled * normal, -1, keepdims=True)
    )


def on_device(
    hidden_in,
    starts,
    positives,
    qkv_weight,
    query_bias,
    value_bias,
    out_weight,
    out_bias,
    first_gain,
    first_shift,
    up_weight,
    up_bias,
    down_weight,
    down_bias,
    second_gain,
    second_shift,
):
    rows, length, width = (hidden_in.shape[1], hidden_in.shape[2], hidden_in.shape[3])
    heads = H
    head_size = width // heads
    tokens = rows * length
    flat = hidden_in.reshape(tokens, width)
    w_qkv = qkv_weight[0]
    w_out = out_weight[0]
    w_up = up_weight[0]
    w_down = down_weight[0]
    row_starts = starts[0]
    qkv_shift = jnp.concatenate([query_bias[0], jnp.zeros_like(query_bias[0]), value_bias[0]])
    qkv = (product(flat, w_qkv) + qkv_shift).astype(jnp.bfloat16)
    split = qkv.reshape(rows, length, 3, heads, head_size)
    query, key, value = (split[:, :, 0], split[:, :, 1], split[:, :, 2])
    places = jnp.arange(length, dtype=jnp.int32)
    segment = jnp.sum((places[None, :, None] >= row_starts[:, None, :]).astype(jnp.int32), -1)
    allowed = (segment[:, :, None] == segment[:, None, :])[:, None]
    head_scale = head_size ** (-0.5)

    def attention_scores(left, right):
        raw = jnp.einsum("rqhe,rkhe->rhqk", left, right, preferred_element_type=jnp.float32)
        return jnp.where(allowed, head_scale * raw, -1e30)

    scores = attention_scores(query, key)
    peak = jnp.max(scores, -1, keepdims=True)
    log_total = peak + jnp.log(jnp.sum(jnp.exp(scores - peak), -1, keepdims=True))
    weights_low = jnp.exp(scores - log_total).astype(jnp.bfloat16)
    mixed = jnp.einsum("rhqk,rkhe->rqhe", weights_low, value, preferred_element_type=jnp.float32)
    mixed = mixed.astype(jnp.bfloat16).reshape(tokens, width)
    attended = product(mixed, w_out) + out_bias[0]
    first_normal, first_inverse = layer_stats(flat.astype(jnp.float32) + attended)
    normed = first_normal * first_gain[0] + first_shift[0]
    normed_low = normed.astype(jnp.bfloat16)
    inner = product(normed_low, w_up) + up_bias[0]
    activated_low = jax.nn.gelu(inner, approximate=False).astype(jnp.bfloat16)
    outer = product(activated_low, w_down) + down_bias[0]
    second_normal, second_inverse = layer_stats(normed + outer)
    encoded = second_normal * second_gain[0] + second_shift[0]
    hidden_out = encoded.astype(jnp.bfloat16).reshape(1, rows, length, width)
    picker = (places[None, None, :] == row_starts[:, :, None]).astype(jnp.float32)
    cls = jnp.einsum(
        "rdl,rlw->rdw",
        picker,
        encoded.reshape(rows, length, width),
        precision=lax.Precision.HIGHEST,
    )
    local_count = rows * DOCS
    cls_low = cls.reshape(local_count, width).astype(jnp.bfloat16)
    first_half = lax.axis_index("enc") == 0
    mine = lax.all_gather(cls_low, "dp", axis=0, tiled=True)
    other = partner(mine, "enc", 0)
    questions = jnp.where(first_half, mine, other)
    passages = jnp.where(first_half, other, mine)
    count = questions.shape[0]
    sim_scale = width ** (-0.5)
    sims = sim_scale * jnp.einsum(
        "qw,pw->qp", questions, passages, preferred_element_type=jnp.float32
    )
    sim_peak = jnp.max(sims, -1, keepdims=True)
    sim_total = sim_peak + jnp.log(jnp.sum(jnp.exp(sims - sim_peak), -1, keepdims=True))
    target = (jnp.arange(count, dtype=jnp.int32)[None, :] == positives[:, None]).astype(jnp.float32)
    total = jnp.sum(sim_total[:, 0] - jnp.sum(sims * target, -1)) / local_count
    loss_mean = total / lax.axis_size("dp")
    d_sims_low = (sim_scale * (jnp.exp(sims - sim_total) - target) / local_count).astype(
        jnp.bfloat16
    )
    own_start = lax.axis_index("dp") * local_count
    own_rows = lax.dynamic_slice_in_dim(d_sims_low, own_start, local_count, 0)
    own_columns = lax.dynamic_slice_in_dim(d_sims_low, own_start, local_count, 1)
    d_questions = jnp.einsum("qp,pw->qw", own_rows, passages, preferred_element_type=jnp.float32)
    d_passages = jnp.einsum("qp,qw->pw", own_columns, questions, preferred_element_type=jnp.float32)
    d_cls = jnp.where(first_half, d_questions, d_passages).reshape(rows, DOCS, width)
    d_encoded = jnp.einsum("rdl,rdw->rlw", picker, d_cls, precision=lax.Precision.HIGHEST).reshape(
        tokens, width
    )
    grad_second_gain = jnp.sum(d_encoded * second_normal, 0)
    grad_second_shift = jnp.sum(d_encoded, 0)
    d_second = norm_back(d_encoded, second_normal, second_inverse, second_gain[0])
    d_outer_low = d_second.astype(jnp.bfloat16)
    grad_down_bias = jnp.sum(d_outer_low.astype(jnp.float32), 0)
    grad_down_weight = jnp.einsum(
        "tf,tw->fw", activated_low, d_outer_low, preferred_element_type=jnp.float32
    )
    d_activated = jnp.einsum("tw,fw->tf", d_outer_low, w_down, preferred_element_type=jnp.float32)
    normal_cdf = 0.5 * (1.0 + lax.erf(inner * 0.7071067811865476))
    slope = normal_cdf + inner * jnp.exp(-0.5 * inner * inner) * 0.3989422804014327
    d_inner_low = (d_activated * slope).astype(jnp.bfloat16)
    grad_up_bias = jnp.sum(d_inner_low.astype(jnp.float32), 0)
    grad_up_weight = jnp.einsum(
        "tw,tf->wf", normed_low, d_inner_low, preferred_element_type=jnp.float32
    )
    d_normed = d_second + jnp.einsum(
        "tf,wf->tw", d_inner_low, w_up, preferred_element_type=jnp.float32
    )
    grad_first_gain = jnp.sum(d_normed * first_normal, 0)
    grad_first_shift = jnp.sum(d_normed, 0)
    d_first = norm_back(d_normed, first_normal, first_inverse, first_gain[0])
    d_attended_low = d_first.astype(jnp.bfloat16)
    grad_out_bias = jnp.sum(d_attended_low.astype(jnp.float32), 0)
    grad_out_weight = jnp.einsum(
        "tv,tw->vw", mixed, d_attended_low, preferred_element_type=jnp.float32
    )
    d_mixed_low = jnp.einsum(
        "tw,vw->tv", d_attended_low, w_out, preferred_element_type=jnp.float32
    ).astype(jnp.bfloat16)
    d_mixed_heads = d_mixed_low.reshape(rows, length, heads, head_size)
    probs_again = jnp.exp(attention_scores(query, key) - log_total)
    weights_again = probs_again.astype(jnp.bfloat16)
    grad_value = jnp.einsum(
        "rhqk,rqhe->rkhe", weights_again, d_mixed_heads, preferred_element_type=jnp.float32
    )
    d_weights = jnp.einsum(
        "rqhe,rkhe->rhqk", d_mixed_heads, value, preferred_element_type=jnp.float32
    )
    d_scores = probs_again * (d_weights - jnp.sum(d_weights * probs_again, -1, keepdims=True))
    d_raw_low = (head_scale * d_scores).astype(jnp.bfloat16)
    grad_query = jnp.einsum("rhqk,rkhe->rqhe", d_raw_low, key, preferred_element_type=jnp.float32)
    grad_key = jnp.einsum("rhqk,rqhe->rkhe", d_raw_low, query, preferred_element_type=jnp.float32)
    d_qkv_low = (
        jnp.stack([grad_query, grad_key, grad_value], 2)
        .reshape(tokens, 3 * width)
        .astype(jnp.bfloat16)
    )
    grad_qkv_local = jnp.einsum("tw,tv->wv", flat, d_qkv_low, preferred_element_type=jnp.float32)
    bias_sums = jnp.sum(d_qkv_low.astype(jnp.float32), 0)
    grad_query_local = bias_sums[:width]
    grad_value_local = bias_sums[2 * width :]
    d_input = d_first + jnp.einsum(
        "tv,wv->tw", d_qkv_low, w_qkv, preferred_element_type=jnp.float32
    )
    hidden_grad = d_input.astype(jnp.bfloat16).reshape(1, rows, length, width)
    (
        share_qkv,
        share_query_bias,
        share_value_bias,
        share_out_weight,
        share_out_bias,
        share_first_gain,
        share_first_shift,
        share_up_weight,
        share_up_bias,
        share_down_weight,
        share_down_bias,
        share_second_gain,
        share_second_shift,
    ) = (
        lax.psum_scatter(grad_qkv_local[None], "dp", scatter_dimension=1, tiled=True),
        lax.psum_scatter(grad_query_local[None], "dp", scatter_dimension=1, tiled=True),
        lax.psum_scatter(grad_value_local[None], "dp", scatter_dimension=1, tiled=True),
        lax.psum_scatter(grad_out_weight[None], "dp", scatter_dimension=1, tiled=True),
        lax.psum_scatter(grad_out_bias[None], "dp", scatter_dimension=1, tiled=True),
        lax.psum_scatter(grad_first_gain[None], "dp", scatter_dimension=1, tiled=True),
        lax.psum_scatter(grad_first_shift[None], "dp", scatter_dimension=1, tiled=True),
        lax.psum_scatter(grad_up_weight[None], "dp", scatter_dimension=1, tiled=True),
        lax.psum_scatter(grad_up_bias[None], "dp", scatter_dimension=1, tiled=True),
        lax.psum_scatter(grad_down_weight[None], "dp", scatter_dimension=1, tiled=True),
        lax.psum_scatter(grad_down_bias[None], "dp", scatter_dimension=1, tiled=True),
        lax.psum_scatter(grad_second_gain[None], "dp", scatter_dimension=1, tiled=True),
        lax.psum_scatter(grad_second_shift[None], "dp", scatter_dimension=1, tiled=True),
    )
    summed = (
        lax.all_gather(share_qkv.astype(jnp.bfloat16), "dp", axis=1, tiled=True).astype(
            share_qkv.dtype
        ),
        lax.all_gather(share_query_bias.astype(jnp.bfloat16), "dp", axis=1, tiled=True).astype(
            share_query_bias.dtype
        ),
        lax.all_gather(share_value_bias.astype(jnp.bfloat16), "dp", axis=1, tiled=True).astype(
            share_value_bias.dtype
        ),
        lax.all_gather(share_out_weight.astype(jnp.bfloat16), "dp", axis=1, tiled=True).astype(
            share_out_weight.dtype
        ),
        lax.all_gather(share_out_bias.astype(jnp.bfloat16), "dp", axis=1, tiled=True).astype(
            share_out_bias.dtype
        ),
        lax.all_gather(share_first_gain.astype(jnp.bfloat16), "dp", axis=1, tiled=True).astype(
            share_first_gain.dtype
        ),
        lax.all_gather(share_first_shift.astype(jnp.bfloat16), "dp", axis=1, tiled=True).astype(
            share_first_shift.dtype
        ),
        lax.all_gather(share_up_weight.astype(jnp.bfloat16), "dp", axis=1, tiled=True).astype(
            share_up_weight.dtype
        ),
        lax.all_gather(share_up_bias.astype(jnp.bfloat16), "dp", axis=1, tiled=True).astype(
            share_up_bias.dtype
        ),
        lax.all_gather(share_down_weight.astype(jnp.bfloat16), "dp", axis=1, tiled=True).astype(
            share_down_weight.dtype
        ),
        lax.all_gather(share_down_bias.astype(jnp.bfloat16), "dp", axis=1, tiled=True).astype(
            share_down_bias.dtype
        ),
        lax.all_gather(share_second_gain.astype(jnp.bfloat16), "dp", axis=1, tiled=True).astype(
            share_second_gain.dtype
        ),
        lax.all_gather(share_second_shift.astype(jnp.bfloat16), "dp", axis=1, tiled=True).astype(
            share_second_shift.dtype
        ),
    )
    return (
        loss_mean,
        hidden_out,
        hidden_grad,
        summed[0],
        summed[1],
        summed[2],
        summed[3],
        summed[4],
        summed[5],
        summed[6],
        summed[7],
        summed[8],
        summed[9],
        summed[10],
        summed[11],
        summed[12],
    )


PAD = 16
BF = jnp.bfloat16
F32 = jnp.float32
MESH = pl.DeviceIdType.MESH
NEG = -1e30
ROOT_HALF = 0.7071067811865476
PEAK = 0.3989422804014327


def nn(left, right):
    return jnp.dot(left, right, preferred_element_type=F32)


def nt(left, right):
    return lax.dot_general(left, right, (((1,), (1,)), ((), ())), preferred_element_type=F32)


def tn(left, right):
    return lax.dot_general(left, right, (((0,), (0,)), ((), ())), preferred_element_type=F32)


def iota(shape, dim):
    return lax.broadcasted_iota(jnp.int32, shape, dim)


def gelu_parts(inner):
    cdf = 0.5 * (1.0 + lax.erf(inner * ROOT_HALF))
    return cdf, jnp.exp(-0.5 * inner * inner) * PEAK


def chunk(index, size):
    return pl.ds(pl.multiple_of(index * size, size), size)


def loop(count, body):
    def step(index, carry):
        body(index)
        return carry

    lax.fori_loop(0, count, step, 0)


def main_kernel(
    n,
    starts,
    positives,
    x_hbm,
    qkv_hbm,
    q_bias,
    v_bias,
    out_hbm,
    o_bias,
    gain1,
    shift1,
    up_hbm,
    u_bias,
    down_hbm,
    d_bias,
    gain2,
    shift2,
    hidden_out,
    hidden_grad,
    xcls_o,
    mixed_o,
    normed_o,
    act_o,
    douter_o,
    dinner_o,
    datt_o,
    dq_o,
    kv_o,
    vecs,
    up_sum,
    x,
    w_qkv,
    w_out,
    w_up,
    w_down,
    kv,
    q,
    mix,
    seg_bias,
    qbd,
    dbd,
    probs,
    p_low,
    ds_low,
    spread,
    xcls,
    mixed,
    cls,
    normed,
    norm1,
    inv1,
    norm2,
    inv2,
    act,
    slope,
    dinner,
    douter,
    datt,
    dmix,
    d_cls,
    dfirst,
    acc,
    turned,
    recv,
    piece,
    dq_own,
    normed_t,
    low_t,
    acc_t,
    hout,
    hgrad,
    load_sem,
    save_sem,
    xs_sem,
    xr_sem,
    ms_sem,
    mr_sem,
    vs_sem,
    ks_sem,
    pr_sem,
    cs_sem,
    cr_sem,
    qs_sem,
    qr_sem,
    gs_sem,
    gr_sem,
):
    enc = lax.axis_index("enc")
    me = lax.axis_index("dp")
    other = 1 - enc
    core = lax.rem(me, 2)
    sibling = me + 1 - 2 * core
    width = x.shape[1]
    tokens = x.shape[0]
    ff = w_up.shape[1]
    wide = n * PAD
    rows = starts.shape[0] // DOCS
    length = tokens // rows
    local = rows * DOCS
    head = width // H
    pairs = H // 2
    head_scale = head ** (-0.5)
    group_cols = width // 4
    half_feats = width // 2
    group_rows = H // 4 * PAD

    loads = [
        pltpu.make_async_copy(x_hbm, x, load_sem.at[0]),
        pltpu.make_async_copy(
            qkv_hbm.at[:, pl.ds(width, 2 * width)], w_qkv.at[:, pl.ds(width, 2 * width)], load_sem.at[1]
        ),
        pltpu.make_async_copy(
            qkv_hbm.at[:, pl.ds(0, width)], w_qkv.at[:, pl.ds(0, width)], load_sem.at[2]
        ),
        pltpu.make_async_copy(out_hbm, w_out, load_sem.at[3]),
        pltpu.make_async_copy(up_hbm, w_up, load_sem.at[4]),
        pltpu.make_async_copy(down_hbm, w_down, load_sem.at[5]),
    ]
    for copy in loads:
        copy.start()

    barrier = pltpu.get_barrier_semaphore()

    def greet(j):
        peer = lax.rem(me + j + 1, n)
        pl.semaphore_signal(barrier, inc=1, device_id=(enc, peer), device_id_type=MESH)

    loop(n - 1, greet)
    pl.semaphore_signal(barrier, inc=1, device_id=(other, me), device_id_type=MESH)

    def remote(source, target, send, receive, device):
        return pltpu.make_async_remote_copy(
            src_ref=source,
            dst_ref=target,
            send_sem=send,
            recv_sem=receive,
            device_id=device,
            device_id_type=MESH,
        )

    def same_core(j):
        return lax.rem(me + 2 * j + 2, n)

    def share(source, place, send, receive):
        def go(j):
            remote(source, place(me), send.at[j], receive.at[me], (enc, same_core(j))).start()

        loop(n // 2 - 1, go)
        remote(source, place(me), send.at[n - 2], receive.at[me], (enc, sibling)).start()

    def shared(source, place, send, receive):
        def pass_on(j):
            peer = same_core(j)
            remote(source, place(peer), send.at[j], receive.at[peer], (enc, peer)).wait_recv()
            remote(
                place(peer), place(peer), send.at[n // 2 - 1 + j], receive.at[peer], (enc, sibling)
            ).start()

        loop(n // 2 - 1, pass_on)

        def finish(j):
            peer = lax.rem(same_core(j) + 1 - 2 * core + n, n)
            remote(source, place(peer), send.at[0], receive.at[peer], (enc, sibling)).wait_recv()

        loop(n // 2, finish)

        def sent(j):
            remote(source, place(me), send.at[j], receive.at[me], (enc, sibling)).wait_send()

        loop(n - 1, sent)

    first_col = jnp.full((PAD, 1), -1, jnp.int32)
    seg_col = jnp.full((PAD, 1), -1, jnp.int32)
    place_col = iota((PAD, 1), 0)
    segs = []
    for r in range(rows):
        place = iota((1, length), 1)
        count = jnp.zeros((1, length), jnp.int32)
        for k in range(DOCS):
            start = starts[r * DOCS + k]
            count = count + (place >= start).astype(jnp.int32)
            order = jnp.int32(0)
            for m in range(DOCS):
                order = order + jnp.where(starts[r * DOCS + m] <= start, 1, 0)
            here = place_col == r * DOCS + k
            first_col = jnp.where(here, r * length + start, first_col)
            seg_col = jnp.where(here, r * 8 + order, seg_col)
        segs.append(count + r * 8)
    seg_row = jnp.concatenate(segs, axis=1)
    pick = (iota((PAD, tokens), 1) == first_col).astype(F32).astype(BF)
    allowed = seg_row == seg_col

    own_rows = pl.ds(pl.multiple_of(me * PAD, PAD), PAD)

    def rows_of(ref):
        return lambda peer: ref.at[pl.ds(pl.multiple_of(peer * PAD, PAD), PAD)]

    loads[0].wait()
    xcls[own_rows, :] = nn(pick, x[...]).astype(BF)
    pl.semaphore_wait(barrier, n)
    share(xcls.at[own_rows], rows_of(xcls), xs_sem, xr_sem)

    loads[1].wait()

    def kv_step(j):
        cols = chunk(j, 256)
        y = nn(x[...], w_qkv[:, pl.ds(pl.multiple_of(width + j * 256, 256), 256)])
        kv[:, cols] = y.astype(BF)

    loop(width // 256, kv_step)

    def v_step(j):
        cols = chunk(j, 256)
        y = nn(x[...], w_qkv[:, pl.ds(pl.multiple_of(2 * width + j * 256, 256), 256)])
        kv[:, pl.ds(pl.multiple_of(width + j * 256, 256), 256)] = (y + v_bias[:, cols]).astype(BF)

    loop(width // 256, v_step)

    low_half = iota((1, 128), 1) < head

    def block_diagonal(target, rows16):
        for p in range(pairs):
            part = rows16[:, p * 128 : (p + 1) * 128]
            even = jnp.where(low_half, part, 0.0).astype(BF)
            odd = jnp.where(low_half, 0.0, part).astype(BF)
            target[pl.ds(2 * p * PAD, PAD), pl.ds(p * 128, 128)] = even
            target[pl.ds((2 * p + 1) * PAD, PAD), pl.ds(p * 128, 128)] = odd

    def own_lanes(full):
        parts = []
        for p in range(pairs):
            lanes = slice(p * 128, (p + 1) * 128)
            even = full[2 * p * PAD : (2 * p + 1) * PAD, lanes]
            odd = full[(2 * p + 1) * PAD : (2 * p + 2) * PAD, lanes]
            parts.append(jnp.where(low_half, even, odd))
        return jnp.concatenate(parts, axis=1)

    loads[2].wait()
    q_own = (nn(xcls[own_rows, :], w_qkv[:, pl.ds(0, width)]) + q_bias[...]).astype(BF).astype(F32)
    qbd[...] = jnp.zeros_like(qbd)
    dbd[...] = jnp.zeros_like(dbd)
    block_diagonal(qbd, q_own)
    allowed_all = jnp.concatenate([allowed] * H, axis=0)
    scores = jnp.where(allowed_all, head_scale * nt(qbd[...], kv[:, pl.ds(0, width)]), NEG)
    peak = jnp.max(scores, -1, keepdims=True)
    raw = jnp.where(allowed_all, jnp.exp(scores - peak), 0.0)
    total = jnp.sum(raw, -1, keepdims=True)
    weights = raw / jnp.where(total > 0.0, total, 1.0)
    probs[...] = weights
    p_low[...] = weights.astype(BF)
    mixed[own_rows, :] = own_lanes(nn(p_low[...], kv[:, pl.ds(width, width)])).astype(BF)
    share(mixed.at[own_rows], rows_of(mixed), ms_sem, mr_sem)

    def send_pieces(side, send, slot):
        for i in range(8):
            owner = 2 * i + side
            source = spread.at[
                slot,
                pl.ds((i % 4) * group_rows, group_rows),
                pl.ds((i // 4) * half_feats, half_feats),
            ]

            @pl.when(me != owner)
            def _():
                pltpu.make_async_remote_copy(
                    src_ref=source,
                    dst_ref=recv.at[me],
                    send_sem=send.at[i],
                    recv_sem=pr_sem.at[me],
                    device_id=(enc, owner),
                    device_id_type=MESH,
                ).start()

            @pl.when(me == owner)
            def _():
                recv[me] = source[...]

    def sent_pieces(side, send, slot):
        for i in range(8):
            owner = 2 * i + side
            source = spread.at[
                slot,
                pl.ds((i % 4) * group_rows, group_rows),
                pl.ds((i // 4) * half_feats, half_feats),
            ]

            @pl.when(me != owner)
            def _():
                pltpu.make_async_remote_copy(
                    src_ref=source,
                    dst_ref=recv.at[me],
                    send_sem=send.at[i],
                    recv_sem=pr_sem.at[me],
                    device_id=(enc, owner),
                    device_id_type=MESH,
                ).wait_send()

    spread[0] = nn(p_low[...], x[...]).astype(BF)
    send_pieces(1, vs_sem, 0)

    def q_step(j):
        cols = chunk(j, 256)
        y = nn(x[...], w_qkv[:, cols]) + q_bias[:, cols]
        q[:, cols] = (y.astype(BF).astype(F32) * head_scale).astype(BF)

    loop(width // 256, q_step)

    def attend_row(r):
        place0 = iota((length, 1), 0)
        place1 = iota((1, length), 1)
        count0 = jnp.zeros((length, 1), jnp.int32)
        count1 = jnp.zeros((1, length), jnp.int32)
        for k in range(DOCS):
            start = starts[r * DOCS + k]
            count0 = count0 + (place0 >= start).astype(jnp.int32)
            count1 = count1 + (place1 >= start).astype(jnp.int32)
        seg_bias[...] = jnp.where(count0 == count1, 0.0, NEG)
        these = chunk(r, length)
        mask_even = jnp.where(low_half, 1.0, 0.0).astype(BF)
        mask_odd = jnp.where(low_half, 0.0, 1.0).astype(BF)

        def attend_pair(p):
            lanes = chunk(p, 128)
            query = q[these, lanes]
            key = kv[these, lanes]
            value = kv[these, pl.ds(pl.multiple_of(width + p * 128, 128), 128)]
            ext = jnp.concatenate([value, jnp.ones_like(value)], axis=1)
            outs = []
            for mask in (mask_even, mask_odd):
                s = nt(query * mask, key) + seg_bias[...]
                e = jnp.exp(s - jnp.max(s, -1, keepdims=True)).astype(BF)
                outs.append(nn(e, ext))
            even, odd = outs
            top = jnp.where(low_half, even[:, :128], odd[:, :128])
            low = jnp.where(low_half, even[:, 128:], odd[:, 128:])
            mix[these, lanes] = (top / low).astype(BF)

        loop(pairs, attend_pair)

    loop(rows, attend_row)

    def saver(source, target, index):
        return pltpu.make_async_copy(source, target, save_sem.at[index])

    saves = []

    def save(source, target, index):
        copy = saver(source, target, index)
        copy.start()
        saves.append(copy)

    shared(xcls.at[own_rows], rows_of(xcls), xs_sem, xr_sem)
    save(xcls, xcls_o, 0)
    shared(mixed.at[own_rows], rows_of(mixed), ms_sem, mr_sem)
    save(mixed, mixed_o, 1)
    loads[3].wait()

    def out_step(j):
        cols = chunk(j, 256)
        acc[:, cols] = nn(mixed[...], w_out[:, cols]) + o_bias[:, cols] + xcls[:, cols].astype(F32)

    loop(width // 256, out_step)

    def stats(h):
        centred = h - jnp.mean(h, -1, keepdims=True)
        inverse = lax.rsqrt(jnp.mean(centred * centred, -1, keepdims=True) + EPS_NORM)
        return centred * inverse, inverse

    unit, inverse = stats(acc[...])
    norm1[...] = unit
    inv1[...] = jnp.broadcast_to(inverse, inv1.shape)
    level = unit * gain1[...] + shift1[...]
    normed[...] = level
    low_t[...] = level.astype(BF)
    loads[4].wait()
    loads[5].wait()
    acc[...] = level + d_bias[...]

    def ff_step(j):
        cols = chunk(j, 512)
        inner = nn(low_t[...], w_up[:, cols]) + u_bias[:, cols]
        cdf, pdf = gelu_parts(inner)
        slope[:, cols] = cdf + inner * pdf
        active = (inner * cdf).astype(BF)
        act[:, cols] = active
        acc[...] += nn(active, w_down[cols, :])

    loop(ff // 512, ff_step)
    normed_keep = saver(low_t, normed_o, 2)
    normed_keep.start()
    save(act, act_o, 3)
    unit, inverse = stats(acc[...])
    norm2[...] = unit
    inv2[...] = jnp.broadcast_to(inverse, inv2.shape)
    cls[enc] = (unit * gain2[...] + shift2[...]).astype(BF)
    half = wide // 2
    mine = pl.ds(pl.multiple_of(core * half, half), half)
    theirs = pl.ds(pl.multiple_of((1 - core) * half, half), half)
    cross = pltpu.make_async_remote_copy(
        src_ref=cls.at[enc, mine],
        dst_ref=cls.at[enc, mine],
        send_sem=cs_sem.at[0],
        recv_sem=cr_sem.at[0],
        device_id=(other, me),
        device_id_type=MESH,
    )
    cross.start()
    cross_in = pltpu.make_async_remote_copy(
        src_ref=cls.at[enc, mine],
        dst_ref=cls.at[other, mine],
        send_sem=cs_sem.at[0],
        recv_sem=cr_sem.at[0],
        device_id=(other, me),
        device_id_type=MESH,
    )
    pass_on = pltpu.make_async_remote_copy(
        src_ref=cls.at[other, mine],
        dst_ref=cls.at[other, mine],
        send_sem=cs_sem.at[1],
        recv_sem=cr_sem.at[1],
        device_id=(enc, sibling),
        device_id_type=MESH,
    )
    pass_in = pltpu.make_async_remote_copy(
        src_ref=cls.at[other, mine],
        dst_ref=cls.at[other, theirs],
        send_sem=cs_sem.at[1],
        recv_sem=cr_sem.at[1],
        device_id=(enc, sibling),
        device_id_type=MESH,
    )

    place_row = iota((1, wide), 1)

    def place_step(device, row):
        for k in range(local):
            target = positives[device * local + k]
            padded = target + (PAD - local) * lax.div(target, local)
            row = jnp.where(place_row == device * PAD + k, padded, row)
        return row

    pos_row = lax.fori_loop(0, n, place_step, jnp.full((1, wide), -1, jnp.int32))

    @pl.when(core == 0)
    def _():
        for j in range(width // 256):
            cols = pl.ds(j * 256, 256)
            y = (nn(xcls[...], w_qkv[:, cols]) + q_bias[:, cols]).astype(BF).astype(F32)
            turned[pl.ds(j * 256, 256), :] = y.T.astype(BF)

    normed_keep.wait()

    def layer_tile(r):
        these = chunk(r, length)

        def tile_out(j):
            cols = chunk(j, 256)
            y = nn(mix[these, :], w_out[:, cols]) + o_bias[:, cols]
            acc_t[:, cols] = y + x[these, cols].astype(F32)

        loop(width // 256, tile_out)
        unit, _ = stats(acc_t[...])
        level = unit * gain1[...] + shift1[...]
        normed_t[...] = level
        low_t[...] = level.astype(BF)
        acc_t[...] = level + d_bias[...]

        def tile_ff(j):
            cols = chunk(j, 512)
            inner = nn(low_t[...], w_up[:, cols]) + u_bias[:, cols]
            active = 0.5 * inner * (1.0 + lax.erf(inner * ROOT_HALF))
            acc_t[...] += nn(active.astype(BF), w_down[cols, :])

        loop(ff // 512, tile_ff)
        unit, _ = stats(acc_t[...])
        hout[these, :] = (unit * gain2[...] + shift2[...]).astype(BF)

    def save_tile(r):
        these = pl.ds(r * length, length)
        save(hout.at[these], hidden_out.at[these], 8 + r)

    layer_tile(0)
    save_tile(0)

    cross.wait_send()
    cross_in.wait_recv()
    pass_on.start()
    pass_on.wait_send()
    pass_in.wait_recv()

    sim_scale = width ** (-0.5)
    good_col = lax.rem(iota((wide, 1), 0), PAD) < local
    good_row = lax.rem(iota((1, wide), 1), PAD) < local
    raw_sims = sim_scale * nt(cls[1], cls[0])
    sims = jnp.where(good_col, raw_sims, NEG)
    sim_peak = jnp.max(sims, 0, keepdims=True)
    sim_total = sim_peak + jnp.log(jnp.sum(jnp.exp(sims - sim_peak), 0, keepdims=True))
    target = (iota((wide, wide), 0) == pos_row).astype(F32)
    losses = sim_total - jnp.sum(raw_sims * target, 0, keepdims=True)
    loss = jnp.sum(jnp.where(good_row, losses, 0.0), -1, keepdims=True) / (local * n)
    d_sims = sim_scale * (jnp.exp(sims - sim_total) - target) / local
    d_sims = jnp.where(good_row, d_sims, 0.0).astype(BF)

    @pl.when(enc == 0)
    def _():
        d_cls[...] = tn(d_sims, cls[1])

    @pl.when(enc == 1)
    def _():
        d_cls[...] = nn(d_sims, cls[0])

    def column_sum(value):
        return jnp.sum(value, 0, keepdims=True)

    def back(upstream, unit, inverse, gain):
        scaled = upstream * gain
        return inverse[:, :1] * (
            scaled
            - jnp.mean(scaled, -1, keepdims=True)
            - unit * jnp.mean(scaled * unit, -1, keepdims=True)
        )

    vecs[pl.ds(0, 1), :] = column_sum(d_cls[...] * norm2[...])
    vecs[pl.ds(1, 1), :] = column_sum(d_cls[...])
    d_second = back(d_cls[...], norm2[...], inv2[...], gain2[...])
    acc[...] = d_second
    d_outer = d_second.astype(BF)
    douter[...] = d_outer
    save(douter, douter_o, 4)
    vecs[pl.ds(2, 1), :] = column_sum(d_outer.astype(F32))

    def ff_back(j):
        cols = chunk(j, 512)
        d_active = nt(douter[...], w_down[cols, :])
        d_low = (d_active * slope[:, cols]).astype(BF)
        dinner[:, cols] = d_low
        up_sum[:, cols] = column_sum(d_low.astype(F32))
        acc[...] += nt(d_low, w_up[:, cols])

    loop(ff // 512, ff_back)
    save(dinner, dinner_o, 5)
    vecs[pl.ds(3, 1), :] = column_sum(acc[...] * norm1[...])
    vecs[pl.ds(4, 1), :] = column_sum(acc[...])
    d_first = back(acc[...], norm1[...], inv1[...], gain1[...])
    dfirst[...] = d_first
    d_low = d_first.astype(BF)
    datt[...] = d_low
    save(datt, datt_o, 6)
    vecs[pl.ds(5, 1), :] = column_sum(d_low.astype(F32))

    def mix_back(j):
        cols = chunk(j, 256)
        dmix[:, cols] = nt(datt[...], w_out[cols, :]).astype(BF)

    loop(width // 256, mix_back)
    vecs[pl.ds(6, 1), :] = column_sum(dmix[...].astype(F32))
    vecs[pl.ds(7, 1), :] = jnp.broadcast_to(loss, (1, width))

    which = lax.div(me, 2)
    group = lax.rem(which, 4)

    planes = n // 4
    across = me + 2 - 4 * lax.rem(which, 2)

    def up_down(j):
        return lax.rem(me + 4 * j + 4, n)

    def grad_of(peer):
        index = lax.div(peer, 2)
        return kv_o.at[
            lax.rem(peer, 2),
            pl.ds(pl.multiple_of(lax.rem(index, 4) * group_cols, group_cols), group_cols),
            pl.ds(pl.multiple_of(lax.div(index, 4) * half_feats, half_feats), half_feats),
        ]

    def gradient(slot, source, owner, device):
        return remote(source, grad_of(owner), gs_sem.at[slot], gr_sem.at[owner], (enc, device))

    def sum_pieces():
        def wait(j):
            peer = lax.rem(me + j + 1, n)
            pltpu.make_async_remote_copy(
                src_ref=recv.at[peer],
                dst_ref=recv.at[peer],
                send_sem=vs_sem.at[0],
                recv_sem=pr_sem.at[peer],
                device_id=(enc, peer),
                device_id_type=MESH,
            ).wait_recv()

        loop(n - 1, wait)
        for a in range(H // 4):
            right = recv[:, pl.ds(a * PAD, PAD), :].reshape(wide, half_feats)
            left = turned[pl.ds(pl.multiple_of(group * group_cols + a * head, head), head), :]
            piece[pl.ds(a * head, head), :] = nn(left, right).astype(BF)
        for j in range(planes - 1):
            gradient(j, piece, me, up_down(j)).start()
        gradient(planes - 1, piece, me, across).start()
        gradient(planes, piece, me, sibling).start()
        saver(piece, grad_of(me), 7).start()

    def pass_plane():
        for j in range(planes - 1):
            peer = up_down(j)
            gradient(0, grad_of(peer), peer, peer).wait_recv()
            gradient(planes + 1 + 2 * j, grad_of(peer), peer, across).start()
            gradient(planes + 2 + 2 * j, grad_of(peer), peer, sibling).start()

    def pass_across():
        for j in range(planes):
            peer = across if j == 0 else lax.rem(up_down(j - 1) - me + across + n, n)
            gradient(0, grad_of(peer), peer, across).wait_recv()
            gradient(3 * planes - 1 + j, grad_of(peer), peer, sibling).start()

    def finish_gradients():
        def came(j):
            peer = lax.rem(same_core(j) + 1 - 2 * core + n, n)
            gradient(0, grad_of(peer), peer, sibling).wait_recv()

        loop(n // 2, came)

        def sent(j):
            remote(piece, grad_of(me), gs_sem.at[j], gr_sem.at[me], (enc, sibling)).wait_send()

        loop(4 * planes - 1, sent)
        saver(piece, grad_of(me), 7).wait()

    @pl.when(core == 1)
    def _():
        for j in range(width // 256):
            cols = pl.ds(j * 256, 256)
            turned[pl.ds(j * 256, 256), :] = dmix[:, cols].astype(F32).T.astype(BF)
        sum_pieces()

    d_own = dmix[own_rows, :].astype(F32)
    block_diagonal(dbd, d_own)
    d_weights = nt(dbd[...], kv[:, pl.ds(width, width)])
    weights = probs[...]
    inner_sum = jnp.sum(d_weights * weights, -1, keepdims=True)
    ds_low[...] = (head_scale * weights * (d_weights - inner_sum)).astype(BF)
    spread[1] = nn(ds_low[...], x[...]).astype(BF)
    send_pieces(0, ks_sem, 1)
    d_query = own_lanes(nn(ds_low[...], kv[:, pl.ds(0, width)])).astype(BF)
    dq_own[...] = d_query
    share(dq_own, rows_of(dq_o), qs_sem, qr_sem)
    save(dq_own, dq_o.at[own_rows], 11)

    layer_tile(1)
    save_tile(1)

    @pl.when(core == 0)
    def _():
        sum_pieces()

    layer_tile(2)
    save_tile(2)

    spread_q = nt(qbd[...], w_qkv[:, pl.ds(width, width)]).astype(BF)
    spread_v = nt(dbd[...], w_qkv[:, pl.ds(2 * width, width)]).astype(BF)
    base = dfirst[own_rows, :] + nt(dq_own[...], w_qkv[:, pl.ds(0, width)])
    base = base.astype(BF)
    for r in range(rows):
        these = slice(r * length, (r + 1) * length)
        y = tn(ds_low[:, these], spread_q) + tn(p_low[:, these], spread_v) + tn(pick[:, these], base)
        hgrad[pl.ds(r * length, length), :] = y.astype(BF)
    save(hgrad, hidden_grad, 12)

    sent_pieces(1, vs_sem, 0)
    sent_pieces(0, ks_sem, 1)
    shared(dq_own, rows_of(dq_o), qs_sem, qr_sem)

    pass_plane()
    pass_across()
    finish_gradients()
    for copy in saves:
        copy.wait()


def grad_kernel(
    xcls_i,
    mixed_i,
    normed_i,
    act_i,
    douter_i,
    dinner_i,
    datt_i,
    dq_i,
    kv_i,
    hidden_out_i,
    hidden_grad_i,
    vecs,
    up_sum,
    loss,
    hidden_out,
    hidden_grad,
    grad_qkv,
    grad_query_bias,
    grad_value_bias,
    grad_out,
    grad_out_bias,
    grad_first_gain,
    grad_first_shift,
    grad_up,
    grad_up_bias,
    grad_down,
    grad_down_bias,
    grad_second_gain,
    grad_second_shift,
    xcls,
    mixed,
    normed,
    act,
    douter,
    dinner,
    datt,
    dq,
    kv,
    g_qkv,
    g_out,
    g_up,
    g_down,
    h_out,
    h_grad,
    in_sem,
    out_sem,
):
    width = xcls.shape[1]
    ff = act.shape[1]
    pairs = [
        (act_i, act),
        (douter_i, douter),
        (normed_i, normed),
        (dinner_i, dinner),
        (mixed_i, mixed),
        (datt_i, datt),
        (xcls_i, xcls),
        (dq_i, dq),
        (kv_i, kv),
    ]
    ins = [pltpu.make_async_copy(a, b, in_sem.at[i]) for i, (a, b) in enumerate(pairs)]
    for copy in ins:
        copy.start()
    through_in = [
        pltpu.make_async_copy(hidden_out_i, h_out, in_sem.at[9]),
        pltpu.make_async_copy(hidden_grad_i, h_grad, in_sem.at[10]),
    ]
    for copy in through_in:
        copy.start()

    loss[...] = vecs[pl.ds(7, 1), pl.ds(0, 1)]
    grad_second_gain[...] = vecs[pl.ds(0, 1), :]
    grad_second_shift[...] = vecs[pl.ds(1, 1), :]
    grad_down_bias[...] = vecs[pl.ds(2, 1), :]
    grad_first_gain[...] = vecs[pl.ds(3, 1), :]
    grad_first_shift[...] = vecs[pl.ds(4, 1), :]
    grad_out_bias[...] = vecs[pl.ds(5, 1), :]
    grad_value_bias[...] = vecs[pl.ds(6, 1), :]
    grad_up_bias[...] = up_sum[...]

    ins[0].wait()
    ins[1].wait()

    def down_step(j):
        these = chunk(j, 256)
        g_down[these, :] = tn(act[:, these], douter[...])
        pltpu.make_async_copy(g_down.at[these], grad_down.at[0, these], out_sem.at[2]).start()

    loop(ff // 256, down_step)
    ins[2].wait()
    ins[3].wait()

    def up_step(j):
        these = chunk(j, 128)
        g_up[these, :] = tn(normed[:, these], dinner[...])
        pltpu.make_async_copy(g_up.at[these], grad_up.at[0, these], out_sem.at[3]).start()

    loop(width // 128, up_step)
    through = [
        pltpu.make_async_copy(h_out, hidden_out, out_sem.at[0]),
        pltpu.make_async_copy(h_grad, hidden_grad, out_sem.at[1]),
    ]
    for came, copy in zip(through_in, through):
        came.wait()
        copy.start()
    ins[4].wait()
    ins[5].wait()

    def out_step(j):
        these = chunk(j, 128)
        g_out[these, :] = tn(mixed[:, these], datt[...])
        pltpu.make_async_copy(g_out.at[these], grad_out.at[0, these], out_sem.at[4]).start()

    loop(width // 128, out_step)
    ins[6].wait()
    ins[7].wait()
    ins[8].wait()
    grad_query_bias[...] = jnp.sum(dq[...].astype(F32), 0, keepdims=True)

    def qkv_step(j):
        these = chunk(j, 128)
        g_qkv[these, pl.ds(0, width)] = tn(xcls[:, these], dq[...])
        for m in range(2):
            g_qkv[these, pl.ds((m + 1) * width, width)] = kv[m, :, these].astype(F32).T
        pltpu.make_async_copy(g_qkv.at[these], grad_qkv.at[0, these], out_sem.at[5]).start()

    loop(width // 128, qkv_step)
    pltpu.make_async_copy(g_down, grad_down.at[0], out_sem.at[2]).wait()
    pltpu.make_async_copy(g_up, grad_up.at[0], out_sem.at[3]).wait()
    pltpu.make_async_copy(g_out, grad_out.at[0], out_sem.at[4]).wait()
    pltpu.make_async_copy(g_qkv, grad_qkv.at[0], out_sem.at[5]).wait()
    for copy in through:
        copy.wait()


def fused_on_device(n, *args):
    (
        hidden_in,
        starts,
        positives,
        qkv_weight,
        query_bias,
        value_bias,
        out_weight,
        out_bias,
        first_gain,
        first_shift,
        up_weight,
        up_bias,
        down_weight,
        down_bias,
        second_gain,
        second_shift,
    ) = args
    rows, length, width = hidden_in.shape[1:]
    tokens = rows * length
    ff = up_weight.shape[-1]
    wide = n * PAD
    spreads = H * PAD
    shape = jax.ShapeDtypeStruct
    hbm = pl.BlockSpec(memory_space=pl.ANY)
    vmem = pl.BlockSpec(memory_space=pltpu.VMEM)
    smem = pl.BlockSpec(memory_space=pltpu.SMEM)
    dma = pltpu.SemaphoreType.DMA
    limit = 60 * 1024 * 1024
    outs = pl.pallas_call(
        functools.partial(main_kernel, n),
        out_shape=[
            shape((tokens, width), BF),
            shape((tokens, width), BF),
            shape((wide, width), BF),
            shape((wide, width), BF),
            shape((wide, width), BF),
            shape((wide, ff), BF),
            shape((wide, width), BF),
            shape((wide, ff), BF),
            shape((wide, width), BF),
            shape((wide, width), BF),
            shape((2, width, width), BF),
            shape((8, width), F32),
            shape((1, ff), F32),
        ],
        in_specs=[smem, smem, hbm, hbm, vmem, vmem, hbm, vmem, vmem, vmem, hbm, vmem, hbm, vmem, vmem, vmem],
        out_specs=[hbm] * 11 + [vmem] * 2,
        scratch_shapes=[
            pltpu.VMEM((tokens, width), BF),
            pltpu.VMEM((width, 3 * width), BF),
            pltpu.VMEM((width, width), BF),
            pltpu.VMEM((width, ff), BF),
            pltpu.VMEM((ff, width), BF),
            pltpu.VMEM((tokens, 2 * width), BF),
            pltpu.VMEM((tokens, width), BF),
            pltpu.VMEM((tokens, width), BF),
            pltpu.VMEM((length, length), F32),
            pltpu.VMEM((spreads, width), BF),
            pltpu.VMEM((spreads, width), BF),
            pltpu.VMEM((spreads, tokens), F32),
            pltpu.VMEM((spreads, tokens), BF),
            pltpu.VMEM((spreads, tokens), BF),
            pltpu.VMEM((2, spreads, width), BF),
            pltpu.VMEM((wide, width), BF),
            pltpu.VMEM((wide, width), BF),
            pltpu.VMEM((2, wide, width), BF),
            pltpu.VMEM((wide, width), F32),
            pltpu.VMEM((wide, width), F32),
            pltpu.VMEM((wide, 128), F32),
            pltpu.VMEM((wide, width), F32),
            pltpu.VMEM((wide, 128), F32),
            pltpu.VMEM((wide, ff), BF),
            pltpu.VMEM((wide, ff), F32),
            pltpu.VMEM((wide, ff), BF),
            pltpu.VMEM((wide, width), BF),
            pltpu.VMEM((wide, width), BF),
            pltpu.VMEM((wide, width), BF),
            pltpu.VMEM((wide, width), F32),
            pltpu.VMEM((wide, width), F32),
            pltpu.VMEM((wide, width), F32),
            pltpu.VMEM((width, wide), BF),
            pltpu.VMEM((n, H // 4 * PAD, width // 2), BF),
            pltpu.VMEM((width // 4, width // 2), BF),
            pltpu.VMEM((PAD, width), BF),
            pltpu.VMEM((length, width), F32),
            pltpu.VMEM((length, width), BF),
            pltpu.VMEM((length, width), F32),
            pltpu.VMEM((tokens, width), BF),
            pltpu.VMEM((tokens, width), BF),
            dma((6,)),
            dma((13,)),
            dma((n,)),
            dma((n,)),
            dma((n,)),
            dma((n,)),
            dma((8,)),
            dma((8,)),
            dma((n,)),
            dma((2,)),
            dma((2,)),
            dma((n,)),
            dma((n,)),
            dma((n,)),
            dma((n,)),
        ],
        compiler_params=pltpu.CompilerParams(
            collective_id=0, has_side_effects=True, vmem_limit_bytes=limit
        ),
        name="layer",
    )(
        starts.reshape(rows * DOCS),
        positives,
        hidden_in.reshape(tokens, width),
        qkv_weight.reshape(width, 3 * width),
        query_bias,
        value_bias,
        out_weight.reshape(width, width),
        out_bias,
        first_gain,
        first_shift,
        up_weight.reshape(width, ff),
        up_bias,
        down_weight.reshape(ff, width),
        down_bias,
        second_gain,
        second_shift,
    )
    (h_out, h_grad, xcls, mixed, normed, act, douter, dinner, datt, dq, kv, vecs, up_sum) = outs
    row = shape((1, width), F32)
    grads = pl.pallas_call(
        grad_kernel,
        out_shape=[
            shape((1, 1), F32),
            shape((tokens, width), BF),
            shape((tokens, width), BF),
            shape((1, width, 3 * width), F32),
            row,
            row,
            shape((1, width, width), F32),
            row,
            row,
            row,
            shape((1, width, ff), F32),
            shape((1, ff), F32),
            shape((1, ff, width), F32),
            row,
            row,
            row,
        ],
        in_specs=[hbm] * 11 + [vmem] * 2,
        out_specs=[vmem, hbm, hbm, hbm, vmem, vmem, hbm, vmem, vmem, vmem, hbm, vmem, hbm, vmem, vmem, vmem],
        scratch_shapes=[
            pltpu.VMEM((wide, width), BF),
            pltpu.VMEM((wide, width), BF),
            pltpu.VMEM((wide, width), BF),
            pltpu.VMEM((wide, ff), BF),
            pltpu.VMEM((wide, width), BF),
            pltpu.VMEM((wide, ff), BF),
            pltpu.VMEM((wide, width), BF),
            pltpu.VMEM((wide, width), BF),
            pltpu.VMEM((2, width, width), BF),
            pltpu.VMEM((width, 3 * width), F32),
            pltpu.VMEM((width, width), F32),
            pltpu.VMEM((width, ff), F32),
            pltpu.VMEM((ff, width), F32),
            pltpu.VMEM((tokens, width), BF),
            pltpu.VMEM((tokens, width), BF),
            dma((11,)),
            dma((6,)),
        ],
        compiler_params=pltpu.CompilerParams(vmem_limit_bytes=limit),
        name="gradients",
    )(xcls, mixed, normed, act, douter, dinner, datt, dq, kv, h_out, h_grad, vecs, up_sum)
    block = (1, rows, length, width)
    return (
        grads[0].reshape(()),
        grads[1].reshape(block),
        grads[2].reshape(block),
        *grads[3:],
    )


def solution(mesh):
    placed = (
        P("enc", "dp", None, None),
        P("enc", "dp", None),
        P(),
        P("enc", None, None),
        P("enc", None),
        P("enc", None),
        P("enc", None, None),
        P("enc", None),
        P("enc", None),
        P("enc", None),
        P("enc", None, None),
        P("enc", None),
        P("enc", None, None),
        P("enc", None),
        P("enc", None),
        P("enc", None),
    )
    n = mesh.shape["dp"]
    body = functools.partial(fused_on_device, n) if n == OWNERS else on_device
    return jax.shard_map(
        body,
        mesh=mesh,
        in_specs=placed,
        out_specs=(
            P(),
            P("enc", "dp", None, None),
            P("enc", "dp", None, None),
            P("enc", None, None),
            P("enc", None),
            P("enc", None),
            P("enc", None, None),
            P("enc", None),
            P("enc", None),
            P("enc", None),
            P("enc", None, None),
            P("enc", None),
            P("enc", None, None),
            P("enc", None),
            P("enc", None),
            P("enc", None),
        ),
        check_vma=False,
    )
```

```python
import functools

import jax
import jax.numpy as jnp
from jax import lax
from jax.experimental import pallas as pl
from jax.experimental.pallas import tpu as pltpu
from jax.sharding import PartitionSpec as P

OWNERS = 16
H = 12
DOCS = 4


EPS_NORM = 1e-12


def partner(value, axis, distance):
    mask = 2**distance
    pairs = [(source, source ^ mask) for source in range(lax.axis_size(axis))]
    return lax.ppermute(value, axis, pairs)


def product(left, right):
    return jnp.dot(left, right, preferred_element_type=jnp.float32)


def layer_stats(hidden):
    centred = hidden - jnp.mean(hidden, -1, keepdims=True)
    inverse = lax.rsqrt(jnp.mean(centred * centred, -1, keepdims=True) + EPS_NORM)
    return (centred * inverse, inverse)


def norm_back(upstream, normal, inverse, gain):
    scaled = upstream * gain
    return inverse * (
        scaled
        - jnp.mean(scaled, -1, keepdims=True)
        - normal * jnp.mean(scaled * normal, -1, keepdims=True)
    )


def on_device(
    hidden_in,
    starts,
    positives,
    qkv_weight,
    query_bias,
    value_bias,
    out_weight,
    out_bias,
    first_gain,
    first_shift,
    up_weight,
    up_bias,
    down_weight,
    down_bias,
    second_gain,
    second_shift,
):
    rows, length, width = (hidden_in.shape[1], hidden_in.shape[2], hidden_in.shape[3])
    heads = H
    head_size = width // heads
    tokens = rows * length
    flat = hidden_in.reshape(tokens, width)
    w_qkv = qkv_weight[0]
    w_out = out_weight[0]
    w_up = up_weight[0]
    w_down = down_weight[0]
    row_starts = starts[0]
    qkv_shift = jnp.concatenate([query_bias[0], jnp.zeros_like(query_bias[0]), value_bias[0]])
    qkv = (product(flat, w_qkv) + qkv_shift).astype(jnp.bfloat16)
    split = qkv.reshape(rows, length, 3, heads, head_size)
    query, key, value = (split[:, :, 0], split[:, :, 1], split[:, :, 2])
    places = jnp.arange(length, dtype=jnp.int32)
    segment = jnp.sum((places[None, :, None] >= row_starts[:, None, :]).astype(jnp.int32), -1)
    allowed = (segment[:, :, None] == segment[:, None, :])[:, None]
    head_scale = head_size ** (-0.5)

    def attention_scores(left, right):
        raw = jnp.einsum("rqhe,rkhe->rhqk", left, right, preferred_element_type=jnp.float32)
        return jnp.where(allowed, head_scale * raw, -1e30)

    scores = attention_scores(query, key)
    peak = jnp.max(scores, -1, keepdims=True)
    log_total = peak + jnp.log(jnp.sum(jnp.exp(scores - peak), -1, keepdims=True))
    weights_low = jnp.exp(scores - log_total).astype(jnp.bfloat16)
    mixed = jnp.einsum("rhqk,rkhe->rqhe", weights_low, value, preferred_element_type=jnp.float32)
    mixed = mixed.astype(jnp.bfloat16).reshape(tokens, width)
    attended = product(mixed, w_out) + out_bias[0]
    first_normal, first_inverse = layer_stats(flat.astype(jnp.float32) + attended)
    normed = first_normal * first_gain[0] + first_shift[0]
    normed_low = normed.astype(jnp.bfloat16)
    inner = product(normed_low, w_up) + up_bias[0]
    activated_low = jax.nn.gelu(inner, approximate=False).astype(jnp.bfloat16)
    outer = product(activated_low, w_down) + down_bias[0]
    second_normal, second_inverse = layer_stats(normed + outer)
    encoded = second_normal * second_gain[0] + second_shift[0]
    hidden_out = encoded.astype(jnp.bfloat16).reshape(1, rows, length, width)
    picker = (places[None, None, :] == row_starts[:, :, None]).astype(jnp.float32)
    cls = jnp.einsum(
        "rdl,rlw->rdw",
        picker,
        encoded.reshape(rows, length, width),
        precision=lax.Precision.HIGHEST,
    )
    local_count = rows * DOCS
    cls_low = cls.reshape(local_count, width).astype(jnp.bfloat16)
    first_half = lax.axis_index("enc") == 0
    mine = lax.all_gather(cls_low, "dp", axis=0, tiled=True)
    other = partner(mine, "enc", 0)
    questions = jnp.where(first_half, mine, other)
    passages = jnp.where(first_half, other, mine)
    count = questions.shape[0]
    sim_scale = width ** (-0.5)
    sims = sim_scale * jnp.einsum(
        "qw,pw->qp", questions, passages, preferred_element_type=jnp.float32
    )
    sim_peak = jnp.max(sims, -1, keepdims=True)
    sim_total = sim_peak + jnp.log(jnp.sum(jnp.exp(sims - sim_peak), -1, keepdims=True))
    target = (jnp.arange(count, dtype=jnp.int32)[None, :] == positives[:, None]).astype(jnp.float32)
    total = jnp.sum(sim_total[:, 0] - jnp.sum(sims * target, -1)) / local_count
    loss_mean = total / lax.axis_size("dp")
    d_sims_low = (sim_scale * (jnp.exp(sims - sim_total) - target) / local_count).astype(
        jnp.bfloat16
    )
    own_start = lax.axis_index("dp") * local_count
    own_rows = lax.dynamic_slice_in_dim(d_sims_low, own_start, local_count, 0)
    own_columns = lax.dynamic_slice_in_dim(d_sims_low, own_start, local_count, 1)
    d_questions = jnp.einsum("qp,pw->qw", own_rows, passages, preferred_element_type=jnp.float32)
    d_passages = jnp.einsum("qp,qw->pw", own_columns, questions, preferred_element_type=jnp.float32)
    d_cls = jnp.where(first_half, d_questions, d_passages).reshape(rows, DOCS, width)
    d_encoded = jnp.einsum("rdl,rdw->rlw", picker, d_cls, precision=lax.Precision.HIGHEST).reshape(
        tokens, width
    )
    grad_second_gain = jnp.sum(d_encoded * second_normal, 0)
    grad_second_shift = jnp.sum(d_encoded, 0)
    d_second = norm_back(d_encoded, second_normal, second_inverse, second_gain[0])
    d_outer_low = d_second.astype(jnp.bfloat16)
    grad_down_bias = jnp.sum(d_outer_low.astype(jnp.float32), 0)
    grad_down_weight = jnp.einsum(
        "tf,tw->fw", activated_low, d_outer_low, preferred_element_type=jnp.float32
    )
    d_activated = jnp.einsum("tw,fw->tf", d_outer_low, w_down, preferred_element_type=jnp.float32)
    normal_cdf = 0.5 * (1.0 + lax.erf(inner * 0.7071067811865476))
    slope = normal_cdf + inner * jnp.exp(-0.5 * inner * inner) * 0.3989422804014327
    d_inner_low = (d_activated * slope).astype(jnp.bfloat16)
    grad_up_bias = jnp.sum(d_inner_low.astype(jnp.float32), 0)
    grad_up_weight = jnp.einsum(
        "tw,tf->wf", normed_low, d_inner_low, preferred_element_type=jnp.float32
    )
    d_normed = d_second + jnp.einsum(
        "tf,wf->tw", d_inner_low, w_up, preferred_element_type=jnp.float32
    )
    grad_first_gain = jnp.sum(d_normed * first_normal, 0)
    grad_first_shift = jnp.sum(d_normed, 0)
    d_first = norm_back(d_normed, first_normal, first_inverse, first_gain[0])
    d_attended_low = d_first.astype(jnp.bfloat16)
    grad_out_bias = jnp.sum(d_attended_low.astype(jnp.float32), 0)
    grad_out_weight = jnp.einsum(
        "tv,tw->vw", mixed, d_attended_low, preferred_element_type=jnp.float32
    )
    d_mixed_low = jnp.einsum(
        "tw,vw->tv", d_attended_low, w_out, preferred_element_type=jnp.float32
    ).astype(jnp.bfloat16)
    d_mixed_heads = d_mixed_low.reshape(rows, length, heads, head_size)
    probs_again = jnp.exp(attention_scores(query, key) - log_total)
    weights_again = probs_again.astype(jnp.bfloat16)
    grad_value = jnp.einsum(
        "rhqk,rqhe->rkhe", weights_again, d_mixed_heads, preferred_element_type=jnp.float32
    )
    d_weights = jnp.einsum(
        "rqhe,rkhe->rhqk", d_mixed_heads, value, preferred_element_type=jnp.float32
    )
    d_scores = probs_again * (d_weights - jnp.sum(d_weights * probs_again, -1, keepdims=True))
    d_raw_low = (head_scale * d_scores).astype(jnp.bfloat16)
    grad_query = jnp.einsum("rhqk,rkhe->rqhe", d_raw_low, key, preferred_element_type=jnp.float32)
    grad_key = jnp.einsum("rhqk,rqhe->rkhe", d_raw_low, query, preferred_element_type=jnp.float32)
    d_qkv_low = (
        jnp.stack([grad_query, grad_key, grad_value], 2)
        .reshape(tokens, 3 * width)
        .astype(jnp.bfloat16)
    )
    grad_qkv_local = jnp.einsum("tw,tv->wv", flat, d_qkv_low, preferred_element_type=jnp.float32)
    bias_sums = jnp.sum(d_qkv_low.astype(jnp.float32), 0)
    grad_query_local = bias_sums[:width]
    grad_value_local = bias_sums[2 * width :]
    d_input = d_first + jnp.einsum(
        "tv,wv->tw", d_qkv_low, w_qkv, preferred_element_type=jnp.float32
    )
    hidden_grad = d_input.astype(jnp.bfloat16).reshape(1, rows, length, width)
    (
        share_qkv,
        share_query_bias,
        share_value_bias,
        share_out_weight,
        share_out_bias,
        share_first_gain,
        share_first_shift,
        share_up_weight,
        share_up_bias,
        share_down_weight,
        share_down_bias,
        share_second_gain,
        share_second_shift,
    ) = (
        lax.psum_scatter(grad_qkv_local[None], "dp", scatter_dimension=1, tiled=True),
        lax.psum_scatter(grad_query_local[None], "dp", scatter_dimension=1, tiled=True),
        lax.psum_scatter(grad_value_local[None], "dp", scatter_dimension=1, tiled=True),
        lax.psum_scatter(grad_out_weight[None], "dp", scatter_dimension=1, tiled=True),
        lax.psum_scatter(grad_out_bias[None], "dp", scatter_dimension=1, tiled=True),
        lax.psum_scatter(grad_first_gain[None], "dp", scatter_dimension=1, tiled=True),
        lax.psum_scatter(grad_first_shift[None], "dp", scatter_dimension=1, tiled=True),
        lax.psum_scatter(grad_up_weight[None], "dp", scatter_dimension=1, tiled=True),
        lax.psum_scatter(grad_up_bias[None], "dp", scatter_dimension=1, tiled=True),
        lax.psum_scatter(grad_down_weight[None], "dp", scatter_dimension=1, tiled=True),
        lax.psum_scatter(grad_down_bias[None], "dp", scatter_dimension=1, tiled=True),
        lax.psum_scatter(grad_second_gain[None], "dp", scatter_dimension=1, tiled=True),
        lax.psum_scatter(grad_second_shift[None], "dp", scatter_dimension=1, tiled=True),
    )
    summed = (
        lax.all_gather(share_qkv.astype(jnp.bfloat16), "dp", axis=1, tiled=True).astype(
            share_qkv.dtype
        ),
        lax.all_gather(share_query_bias.astype(jnp.bfloat16), "dp", axis=1, tiled=True).astype(
            share_query_bias.dtype
        ),
        lax.all_gather(share_value_bias.astype(jnp.bfloat16), "dp", axis=1, tiled=True).astype(
            share_value_bias.dtype
        ),
        lax.all_gather(share_out_weight.astype(jnp.bfloat16), "dp", axis=1, tiled=True).astype(
            share_out_weight.dtype
        ),
        lax.all_gather(share_out_bias.astype(jnp.bfloat16), "dp", axis=1, tiled=True).astype(
            share_out_bias.dtype
        ),
        lax.all_gather(share_first_gain.astype(jnp.bfloat16), "dp", axis=1, tiled=True).astype(
            share_first_gain.dtype
        ),
        lax.all_gather(share_first_shift.astype(jnp.bfloat16), "dp", axis=1, tiled=True).astype(
            share_first_shift.dtype
        ),
        lax.all_gather(share_up_weight.astype(jnp.bfloat16), "dp", axis=1, tiled=True).astype(
            share_up_weight.dtype
        ),
        lax.all_gather(share_up_bias.astype(jnp.bfloat16), "dp", axis=1, tiled=True).astype(
            share_up_bias.dtype
        ),
        lax.all_gather(share_down_weight.astype(jnp.bfloat16), "dp", axis=1, tiled=True).astype(
            share_down_weight.dtype
        ),
        lax.all_gather(share_down_bias.astype(jnp.bfloat16), "dp", axis=1, tiled=True).astype(
            share_down_bias.dtype
        ),
        lax.all_gather(share_second_gain.astype(jnp.bfloat16), "dp", axis=1, tiled=True).astype(
            share_second_gain.dtype
        ),
        lax.all_gather(share_second_shift.astype(jnp.bfloat16), "dp", axis=1, tiled=True).astype(
            share_second_shift.dtype
        ),
    )
    return (
        loss_mean,
        hidden_out,
        hidden_grad,
        summed[0],
        summed[1],
        summed[2],
        summed[3],
        summed[4],
        summed[5],
        summed[6],
        summed[7],
        summed[8],
        summed[9],
        summed[10],
        summed[11],
        summed[12],
    )


PAD = 16
BF = jnp.bfloat16
F32 = jnp.float32
MESH = pl.DeviceIdType.MESH
NEG = -1e30
ROOT_HALF = 0.7071067811865476
PEAK = 0.3989422804014327


def nn(left, right):
    return jnp.dot(left, right, preferred_element_type=F32)


def nt(left, right):
    return lax.dot_general(left, right, (((1,), (1,)), ((), ())), preferred_element_type=F32)


def tn(left, right):
    return lax.dot_general(left, right, (((0,), (0,)), ((), ())), preferred_element_type=F32)


def iota(shape, dim):
    return lax.broadcasted_iota(jnp.int32, shape, dim)


def gelu_parts(inner):
    cdf = 0.5 * (1.0 + lax.erf(inner * ROOT_HALF))
    return cdf, jnp.exp(-0.5 * inner * inner) * PEAK


def chunk(index, size):
    return pl.ds(pl.multiple_of(index * size, size), size)


def loop(count, body):
    def step(index, carry):
        body(index)
        return carry

    lax.fori_loop(0, count, step, 0)


def main_kernel(
    n,
    starts,
    positives,
    x_hbm,
    qkv_hbm,
    q_bias,
    v_bias,
    out_hbm,
    o_bias,
    gain1,
    shift1,
    up_hbm,
    u_bias,
    down_hbm,
    d_bias,
    gain2,
    shift2,
    hidden_out,
    hidden_grad,
    xcls_o,
    mixed_o,
    normed_o,
    act_o,
    douter_o,
    dinner_o,
    datt_o,
    dq_o,
    vecs_o,
    kv_o,
    x,
    w_qkv,
    w_out,
    w_up,
    w_down,
    kv,
    q,
    mix,
    seg_bias,
    qbd,
    dbd,
    qk,
    dv,
    probs,
    p_low,
    ds_low,
    px,
    dx,
    xcls,
    mixed,
    cls,
    norm1,
    inv1,
    norm2,
    inv2,
    normed,
    act,
    slope,
    dinner,
    douter,
    datt,
    dmix,
    d_cls,
    dfirst,
    acc,
    vecs,
    turned,
    recv,
    piece,
    dq_own,
    low_t,
    acc_t,
    hout,
    hgrad,
    load_sem,
    save_sem,
    xs_sem,
    xr_sem,
    ms_sem,
    mr_sem,
    ks_sem,
    kr_sem,
    cs_sem,
    cr_sem,
    qs_sem,
    qr_sem,
    vs_sem,
    gs_sem,
    gr_sem,
    fs_sem,
    fr_sem,
):
    enc = lax.axis_index("enc")
    me = lax.axis_index("dp")
    other = 1 - enc
    core = lax.rem(me, 2)
    which = lax.div(me, 2)
    sibling = me + 1 - 2 * core
    across = me + 2 - 4 * lax.rem(which, 2)
    planes = n // 4
    tokens, width = x.shape
    ff = w_up.shape[1]
    side = n // 2 * PAD
    rows = starts.shape[1]
    length = tokens // rows
    local = rows * DOCS
    head = width // H
    pairs = H // 2
    head_scale = head ** (-0.5)
    group_cols = width // 4
    half_feats = width // 2
    group_rows = H // 4 * PAD
    query_w = pl.ds(0, width)
    key_w = pl.ds(width, width)
    value_w = pl.ds(2 * width, width)

    def weight_load(cols, index):
        return pltpu.make_async_copy(qkv_hbm.at[:, cols], w_qkv.at[:, cols], load_sem.at[index])

    loads = [
        pltpu.make_async_copy(x_hbm, x, load_sem.at[0]),
        weight_load(key_w, 1),
        weight_load(query_w, 2),
        weight_load(value_w, 3),
        pltpu.make_async_copy(out_hbm, w_out, load_sem.at[4]),
        pltpu.make_async_copy(up_hbm, w_up, load_sem.at[5]),
        pltpu.make_async_copy(down_hbm, w_down, load_sem.at[6]),
    ]
    for copy in loads:
        copy.start()

    barrier = pltpu.get_barrier_semaphore()

    def greet(j):
        peer = lax.rem(me + j + 1, n)
        pl.semaphore_signal(barrier, inc=1, device_id=(enc, peer), device_id_type=MESH)

    loop(n - 1, greet)
    pl.semaphore_signal(barrier, inc=1, device_id=(other, me), device_id_type=MESH)

    def remote(source, target, send, receive, device):
        return pltpu.make_async_remote_copy(
            src_ref=source,
            dst_ref=target,
            send_sem=send,
            recv_sem=receive,
            device_id=device,
            device_id_type=MESH,
        )

    def same_core(j):
        return lax.rem(me + 2 * j + 2, n)

    def cousin(j):
        return lax.rem(same_core(j) + 1 - 2 * core + n, n)

    def up_down(j):
        return lax.rem(me + 4 * j + 4, n)

    def block(index):
        return pl.ds(pl.multiple_of(index * PAD, PAD), PAD)

    own = block(which)

    def share(source, place, send, receive):
        def go(j):
            remote(source, place(me), send.at[j], receive.at[me], (enc, same_core(j))).start()

        loop(n // 2 - 1, go)

    def shared(source, place, send, receive):
        def came(j):
            peer = same_core(j)
            copy = remote(source, place(peer), send.at[j], receive.at[peer], (enc, peer))
            copy.wait_send()
            copy.wait_recv()

        loop(n // 2 - 1, came)

    class Relay:
        def __init__(self, source, place, send, receive):
            self.source, self.place, self.send, self.receive = source, place, send, receive

        def copy(self, slot, source, owner, device):
            return remote(
                source, self.place(owner), self.send.at[slot], self.receive.at[owner], (enc, device)
            )

        def start(self):
            for j in range(planes - 1):
                self.copy(j, self.source, me, up_down(j)).start()
            self.copy(planes - 1, self.source, me, across).start()
            self.copy(planes, self.source, me, sibling).start()

        def plane(self):
            for j in range(planes - 1):
                peer = up_down(j)
                self.copy(0, self.place(peer), peer, peer).wait_recv()
                self.copy(planes + 1 + 2 * j, self.place(peer), peer, across).start()
                self.copy(planes + 2 + 2 * j, self.place(peer), peer, sibling).start()

        def over(self):
            for j in range(planes):
                peer = across if j == 0 else lax.rem(up_down(j - 1) - me + across + n, n)
                self.copy(0, self.place(peer), peer, across).wait_recv()
                self.copy(3 * planes - 1 + j, self.place(peer), peer, sibling).start()

        def sent(self):
            def wait(j):
                self.copy(j, self.source, me, sibling).wait_send()

            loop(4 * planes - 1, wait)

        def came(self):
            def wait(j):
                peer = cousin(j)
                self.copy(0, self.place(peer), peer, sibling).wait_recv()

            loop(n // 2, wait)

    saves = []

    def save(source, target, index):
        copy = pltpu.make_async_copy(source, target, save_sem.at[index])
        copy.start()
        saves.append(copy)

    halves = [pl.ds(pl.multiple_of(core * side, side), side)]
    halves.append(pl.ds(pl.multiple_of((1 - core) * side, side), side))
    given = []

    def give(source, target, index):
        save(source, target.at[halves[0]], index)
        copy = remote(source, target.at[halves[0]], fs_sem.at[index], fr_sem.at[index], (enc, sibling))
        copy.start()
        given.append(
            remote(source, target.at[halves[1]], fs_sem.at[index], fr_sem.at[index], (enc, sibling))
        )

    first_col = jnp.full((PAD, 1), -1, jnp.int32)
    seg_col = jnp.full((PAD, 1), -1, jnp.int32)
    place_col = iota((PAD, 1), 0)
    segs = []
    for r in range(rows):
        place = iota((1, length), 1)
        count = jnp.zeros((1, length), jnp.int32)
        for k in range(DOCS):
            start = starts[0, r, k]
            count = count + (place >= start).astype(jnp.int32)
            order = jnp.int32(0)
            for m in range(DOCS):
                order = order + jnp.where(starts[0, r, m] <= start, 1, 0)
            here = place_col == r * DOCS + k
            first_col = jnp.where(here, r * length + start, first_col)
            seg_col = jnp.where(here, r * 8 + order, seg_col)
        segs.append(count + r * 8)
    seg_row = jnp.concatenate(segs, axis=1)
    pick = (iota((PAD, tokens), 1) == first_col).astype(F32).astype(BF)
    allowed = seg_row == seg_col

    low_half = iota((1, 128), 1) < head

    def block_diagonal(target, block_rows):
        for p in range(pairs):
            part = block_rows[:, p * 128 : (p + 1) * 128]
            even = jnp.where(low_half, part, 0.0).astype(BF)
            odd = jnp.where(low_half, 0.0, part).astype(BF)
            target[pl.ds(2 * p * PAD, PAD), pl.ds(p * 128, 128)] = even
            target[pl.ds((2 * p + 1) * PAD, PAD), pl.ds(p * 128, 128)] = odd

    def own_lanes(full):
        parts = []
        for p in range(pairs):
            lanes = slice(p * 128, (p + 1) * 128)
            even = full[2 * p * PAD : (2 * p + 1) * PAD, lanes]
            odd = full[(2 * p + 1) * PAD : (2 * p + 2) * PAD, lanes]
            parts.append(jnp.where(low_half, even, odd))
        return jnp.concatenate(parts, axis=1)

    qbd[...] = jnp.zeros_like(qbd)
    dbd[...] = jnp.zeros_like(dbd)
    loads[0].wait()
    xcls[core, own, :] = nn(pick, x[...]).astype(BF)
    pl.semaphore_wait(barrier, n)

    def xcls_place(peer):
        return xcls.at[core, block(lax.div(peer, 2))]

    share(xcls.at[core, own], xcls_place, xs_sem, xr_sem)

    loads[1].wait()
    kv[:, pl.ds(0, width)] = nn(x[...], w_qkv[:, key_w]).astype(BF)
    loads[2].wait()
    q_own = (nn(xcls[core, own, :], w_qkv[:, query_w]) + q_bias[...]).astype(BF).astype(F32)
    block_diagonal(qbd, q_own)
    loads[3].wait()
    kv[:, pl.ds(width, width)] = (nn(x[...], w_qkv[:, value_w]) + v_bias[...]).astype(BF)
    allowed_all = jnp.concatenate([allowed] * H, axis=0)
    scores = jnp.where(allowed_all, head_scale * nt(qbd[...], kv[:, pl.ds(0, width)]), NEG)
    peak = jnp.max(scores, -1, keepdims=True)
    raw = jnp.where(allowed_all, jnp.exp(scores - peak), 0.0)
    total = jnp.sum(raw, -1, keepdims=True)
    weights = raw / jnp.where(total > 0.0, total, 1.0)
    probs[...] = weights
    p_low[...] = weights.astype(BF)
    mixed[own, :] = own_lanes(nn(p_low[...], kv[:, pl.ds(width, width)])).astype(BF)

    def mixed_place(peer):
        return mixed.at[block(lax.div(peer, 2))]

    share(mixed.at[own], mixed_place, ms_sem, mr_sem)

    def slot_of(peer):
        return lax.rem(peer, 2) * (n // 2) + lax.div(peer, 2)

    def piece_of(source, i):
        return source.at[
            pl.ds((i % 4) * group_rows, group_rows), pl.ds((i // 4) * half_feats, half_feats)
        ]

    def piece_copy(source, side_of, i, send):
        target = recv.at[slot_of(me)]
        owner = (enc, 2 * i + side_of)
        return remote(piece_of(source, i), target, send.at[i], kr_sem.at[me], owner)

    def send_pieces(source, side_of, send):
        for i in range(n // 2):

            @pl.when(me != 2 * i + side_of)
            def _():
                piece_copy(source, side_of, i, send).start()

            @pl.when(me == 2 * i + side_of)
            def _():
                recv[slot_of(me)] = piece_of(source, i)[...]

    def sent_pieces(source, side_of, send):
        for i in range(n // 2):

            @pl.when(me != 2 * i + side_of)
            def _():
                piece_copy(source, side_of, i, send).wait_send()

    px[...] = nn(p_low[...], x[...]).astype(BF)
    send_pieces(px, 1, vs_sem)

    y = nn(x[...], w_qkv[:, query_w]) + q_bias[...]
    q[...] = (y.astype(BF).astype(F32) * head_scale).astype(BF)

    def attend_row(r):
        place0 = iota((length, 1), 0)
        place1 = iota((1, length), 1)
        count0 = jnp.zeros((length, 1), jnp.int32)
        count1 = jnp.zeros((1, length), jnp.int32)
        for k in range(DOCS):
            start = starts[0, r, k]
            count0 = count0 + (place0 >= start).astype(jnp.int32)
            count1 = count1 + (place1 >= start).astype(jnp.int32)
        seg_bias[...] = jnp.where(count0 == count1, 0.0, NEG)
        these = pl.ds(r * length, length)
        mask_even = jnp.where(low_half, 1.0, 0.0).astype(BF)
        mask_odd = jnp.where(low_half, 0.0, 1.0).astype(BF)

        for p in range(pairs):
            lanes = pl.ds(p * 128, 128)
            query = q[these, lanes]
            key = kv[these, lanes]
            value = kv[these, pl.ds(width + p * 128, 128)]
            ext = jnp.concatenate([value, jnp.ones_like(value)], axis=1)
            outs = []
            for mask in (mask_even, mask_odd):
                s = nt(query * mask, key) + seg_bias[...]
                e = jnp.exp(s - jnp.max(s, -1, keepdims=True)).astype(BF)
                outs.append(nn(e, ext))
            even, odd = outs
            top = jnp.where(low_half, even[:, :128], odd[:, :128])
            low = jnp.where(low_half, even[:, 128:], odd[:, 128:])
            mix[these, lanes] = (top / low).astype(BF)

    attend_row(0)

    shared(xcls.at[core, own], xcls_place, xs_sem, xr_sem)
    xcls_over = remote(xcls.at[core], xcls.at[core], fs_sem.at[10], fr_sem.at[10], (enc, sibling))
    xcls_over.start()
    xcls_back = remote(xcls.at[core], xcls.at[1 - core], fs_sem.at[10], fr_sem.at[10], (enc, sibling))
    shared(mixed.at[own], mixed_place, ms_sem, mr_sem)
    loads[4].wait()

    acc[...] = nn(mixed[...], w_out[...]) + o_bias[...] + xcls[core].astype(F32)

    def stats(h):
        centred = h - jnp.mean(h, -1, keepdims=True)
        inverse = lax.rsqrt(jnp.mean(centred * centred, -1, keepdims=True) + EPS_NORM)
        return centred * inverse, inverse

    unit, inverse = stats(acc[...])
    norm1[...] = unit
    inv1[...] = jnp.broadcast_to(inverse, inv1.shape)
    level = unit * gain1[...] + shift1[...]
    normed[...] = level.astype(BF)
    loads[5].wait()
    loads[6].wait()
    inner = nn(normed[...], w_up[...]) + u_bias[...]
    cdf, pdf = gelu_parts(inner)
    slope[...] = cdf + inner * pdf
    act[...] = (inner * cdf).astype(BF)
    unit, inverse = stats(level + d_bias[...] + nn(act[...], w_down[...]))
    norm2[...] = unit
    inv2[...] = jnp.broadcast_to(inverse, inv2.shape)
    cls[enc, core] = (unit * gain2[...] + shift2[...]).astype(BF)

    def cls_copy(half_of, to_core, index, device):
        return remote(
            cls.at[half_of, core], cls.at[half_of, to_core], cs_sem.at[index], cr_sem.at[index], device
        )

    cls_copy(enc, core, 0, (other, me)).start()
    cls_copy(enc, core, 1, (enc, sibling)).start()
    give(mixed, mixed_o, 1)
    give(normed, normed_o, 2)
    give(act, act_o, 3)

    def padded(question):
        device = lax.div(question, local)
        place = lax.rem(device, 2) * side + lax.div(device, 2) * PAD
        return place + question - device * local

    place_row = iota((1, 2 * side), 1)

    def place_step(device, row):
        for k in range(local):
            question = device * local + k
            row = jnp.where(place_row == padded(question), padded(positives[question]), row)
        return row

    pos_row = lax.fori_loop(0, n, place_step, jnp.full((1, 2 * side), -1, jnp.int32))

    xcls_back.wait_recv()

    @pl.when(core == 0)
    def _():
        for c in range(2):
            y = (nn(xcls[c], w_qkv[:, query_w]) + q_bias[...]).astype(BF).astype(F32)
            turned[:, pl.ds(c * side, side)] = y.T.astype(BF)

    save(xcls.at[0], xcls_o.at[pl.ds(0, side)], 4)
    save(xcls.at[1], xcls_o.at[pl.ds(side, side)], 5)

    attend_row(1)
    attend_row(2)

    cls_copy(enc, core, 0, (other, me)).wait_send()
    cls_in = remote(cls.at[enc, core], cls.at[other, core], cs_sem.at[0], cr_sem.at[0], (other, me))
    cls_in.wait_recv()
    cls_pass = cls_copy(other, core, 2, (enc, sibling))
    cls_pass.start()
    cls_copy(enc, core, 1, (enc, sibling)).wait_send()
    remote(
        cls.at[enc, core], cls.at[enc, 1 - core], cs_sem.at[1], cr_sem.at[1], (enc, sibling)
    ).wait_recv()
    cls_pass.wait_send()
    remote(
        cls.at[other, core], cls.at[other, 1 - core], cs_sem.at[2], cr_sem.at[2], (enc, sibling)
    ).wait_recv()

    sim_scale = width ** (-0.5)
    good_col = lax.rem(iota((2 * side, 1), 0), PAD) < local
    good_row = lax.rem(iota((1, 2 * side), 1), PAD) < local
    questions = cls[0].reshape(2 * side, width)
    passages = cls[1].reshape(2 * side, width)
    raw_sims = sim_scale * nt(passages, questions)
    sims = jnp.where(good_col, raw_sims, NEG)
    sim_peak = jnp.max(sims, 0, keepdims=True)
    sim_total = sim_peak + jnp.log(jnp.sum(jnp.exp(sims - sim_peak), 0, keepdims=True))
    target = (iota((2 * side, 2 * side), 0) == pos_row).astype(F32)
    losses = sim_total - jnp.sum(raw_sims * target, 0, keepdims=True)
    loss = jnp.sum(jnp.where(good_row, losses, 0.0), -1, keepdims=True) / (local * n)
    d_sims = sim_scale * (jnp.exp(sims - sim_total) - target) / local
    d_sims = jnp.where(good_row, d_sims, 0.0).astype(BF)

    for c in range(2):
        these = slice(c * side, (c + 1) * side)

        @pl.when((enc == 0) & (core == c))
        def _():
            d_cls[...] = tn(d_sims[:, these], passages)

        @pl.when((enc == 1) & (core == c))
        def _():
            d_cls[...] = nn(d_sims[these, :], questions)

    def column_sum(value):
        return jnp.sum(value, 0, keepdims=True)

    def back(upstream, unit, inverse, gain):
        scaled = upstream * gain
        return inverse[:, :1] * (
            scaled
            - jnp.mean(scaled, -1, keepdims=True)
            - unit * jnp.mean(scaled * unit, -1, keepdims=True)
        )

    vecs[pl.ds(0, 1), :] = column_sum(d_cls[...] * norm2[...])
    vecs[pl.ds(1, 1), :] = column_sum(d_cls[...])
    d_second = back(d_cls[...], norm2[...], inv2[...], gain2[...])
    douter[...] = d_second.astype(BF)
    d_active = nt(douter[...], w_down[...])
    dinner[...] = (d_active * slope[...]).astype(BF)
    acc[...] = d_second + nt(dinner[...], w_up[...])
    vecs[pl.ds(2, 1), :] = column_sum(acc[...] * norm1[...])
    vecs[pl.ds(3, 1), :] = column_sum(acc[...])
    vecs[pl.ds(4, 1), :] = jnp.broadcast_to(loss, (1, width))
    vecs[pl.ds(6, 2), :] = jnp.zeros((2, width), F32)
    d_first = back(acc[...], norm1[...], inv1[...], gain1[...])
    dfirst[...] = d_first
    datt[...] = d_first.astype(BF)

    dmix[core] = nt(datt[...], w_out[...]).astype(BF)
    dmix_over = remote(dmix.at[core], dmix.at[core], fs_sem.at[11], fr_sem.at[11], (enc, sibling))
    dmix_back = remote(dmix.at[core], dmix.at[1 - core], fs_sem.at[11], fr_sem.at[11], (enc, sibling))

    @pl.when(core == 0)
    def _():
        dmix_over.start()

    block_diagonal(dbd, dmix[core, own, :].astype(F32))
    d_weights = nt(dbd[...], kv[:, pl.ds(width, width)])
    weights = probs[...]
    inner_sum = jnp.sum(d_weights * weights, -1, keepdims=True)
    ds_low[...] = (head_scale * weights * (d_weights - inner_sum)).astype(BF)
    dx[...] = nn(ds_low[...], x[...]).astype(BF)
    send_pieces(dx, 0, ks_sem)
    dq_own[...] = own_lanes(nn(ds_low[...], kv[:, pl.ds(0, width)])).astype(BF)

    def dq_place(peer):
        return dq_o.at[block(slot_of(peer))]

    queries = Relay(dq_own, dq_place, qs_sem, qr_sem)
    queries.start()
    save(dq_own, dq_place(me), 6)
    give(douter, douter_o, 7)
    give(dinner, dinner_o, 8)
    give(datt, datt_o, 9)
    vecs[pl.ds(5, 1), :] = column_sum(dmix[core].astype(F32))

    def layer_tile(r):
        these = pl.ds(r * length, length)

        acc_t[...] = nn(mix[these, :], w_out[...]) + o_bias[...] + x[these, :].astype(F32)
        unit, _ = stats(acc_t[...])
        level = unit * gain1[...] + shift1[...]
        low_t[...] = level.astype(BF)
        inner = nn(low_t[...], w_up[...]) + u_bias[...]
        active = (0.5 * inner * (1.0 + lax.erf(inner * ROOT_HALF))).astype(BF)
        unit, _ = stats(level + d_bias[...] + nn(active, w_down[...]))
        hout[these, :] = (unit * gain2[...] + shift2[...]).astype(BF)
        save(hout.at[these], hidden_out.at[these], 13 + r)

    group = lax.rem(which, 4)

    def grad_place(peer):
        index = lax.div(peer, 2)
        return kv_o.at[
            lax.rem(peer, 2),
            pl.ds(pl.multiple_of(lax.rem(index, 4) * group_cols, group_cols), group_cols),
            pl.ds(pl.multiple_of(lax.div(index, 4) * half_feats, half_feats), half_feats),
        ]

    summed = Relay(piece, grad_place, gs_sem, gr_sem)
    piece_save = pltpu.make_async_copy(piece, grad_place(me), save_sem.at[16])

    def sum_pieces():
        def came(j):
            peer = lax.rem(me + j + 1, n)
            place = recv.at[slot_of(peer)]
            remote(place, place, ks_sem.at[0], kr_sem.at[peer], (enc, peer)).wait_recv()

        loop(n - 1, came)
        for a in range(H // 4):
            right = recv[:, pl.ds(a * PAD, PAD), :].reshape(2 * side, half_feats)
            left = turned[pl.ds(pl.multiple_of(group * group_cols + a * head, head), head), :]
            piece[pl.ds(a * head, head), :] = nn(left, right).astype(BF)
        summed.start()
        piece_save.start()

    @pl.when(core == 1)
    def _():
        dmix_back.wait_recv()
        for c in range(2):
            turned[:, pl.ds(c * side, side)] = dmix[c].astype(F32).T.astype(BF)
        sum_pieces()

    layer_tile(0)
    layer_tile(1)
    queries.plane()

    @pl.when(core == 0)
    def _():
        sum_pieces()

    layer_tile(2)
    queries.over()
    summed.plane()

    base = dfirst[own, :] + nt(dq_own[...], w_qkv[:, query_w])
    base = base.astype(BF)
    qk[...] = nt(qbd[...], w_qkv[:, key_w]).astype(BF)
    dv[...] = nt(dbd[...], w_qkv[:, value_w]).astype(BF)
    y = tn(ds_low[...], qk[...]) + tn(p_low[...], dv[...]) + tn(pick, base)
    hgrad[...] = y.astype(BF)
    save(hgrad, hidden_grad, 17)
    vecs_give = remote(vecs, vecs_o.at[core], fs_sem.at[12], fr_sem.at[12], (enc, sibling))
    vecs_give.start()
    vecs_take = remote(vecs, vecs_o.at[1 - core], fs_sem.at[12], fr_sem.at[12], (enc, sibling))
    save(vecs, vecs_o.at[core], 12)

    summed.over()
    sent_pieces(px, 1, vs_sem)
    sent_pieces(dx, 0, ks_sem)
    queries.sent()
    queries.came()
    xcls_back.wait_send()

    @pl.when(core == 0)
    def _():
        dmix_over.wait_send()

    for copy in [*given, vecs_take]:
        copy.wait_send()
        copy.wait_recv()
    summed.sent()
    piece_save.wait()
    summed.came()
    for copy in saves:
        copy.wait()


def grad_kernel(
    xcls_i,
    mixed_i,
    normed_i,
    act_i,
    douter_i,
    dinner_i,
    datt_i,
    dq_i,
    kv_i,
    hidden_out_i,
    hidden_grad_i,
    vecs,
    loss,
    hidden_out,
    hidden_grad,
    grad_qkv,
    grad_query_bias,
    grad_value_bias,
    grad_out,
    grad_out_bias,
    grad_first_gain,
    grad_first_shift,
    grad_up,
    grad_up_bias,
    grad_down,
    grad_down_bias,
    grad_second_gain,
    grad_second_shift,
    xcls,
    mixed,
    normed,
    act,
    douter,
    dinner,
    datt,
    dq,
    kv,
    g_qkv,
    g_out,
    g_up,
    g_down,
    h_out,
    h_grad,
    in_sem,
    out_sem,
):
    width = xcls.shape[1]
    ins = {}
    loads = [
        ("mixed", mixed_i, mixed),
        ("datt", datt_i, datt),
        ("act", act_i, act),
        ("douter", douter_i, douter),
        ("normed", normed_i, normed),
        ("dinner", dinner_i, dinner),
        ("xcls", xcls_i, xcls),
        ("dq", dq_i, dq),
        ("kv", kv_i, kv),
        ("h_out", hidden_out_i, h_out),
        ("h_grad", hidden_grad_i, h_grad),
    ]
    for index, (name, source, target) in enumerate(loads):
        ins[name] = pltpu.make_async_copy(source, target, in_sem.at[index])
        ins[name].start()

    def column_sum(value):
        return jnp.sum(value.astype(F32), 0, keepdims=True)

    def vector(row):
        return vecs[0, pl.ds(row, 1), :] + vecs[1, pl.ds(row, 1), :]

    def put(source, target, rows, index):
        pltpu.make_async_copy(source.at[rows], target.at[0, rows], out_sem.at[index]).start()

    loss[...] = vecs[0, pl.ds(4, 1), pl.ds(0, 1)]
    grad_second_gain[...] = vector(0)
    grad_second_shift[...] = vector(1)
    grad_first_gain[...] = vector(2)
    grad_first_shift[...] = vector(3)
    grad_value_bias[...] = vector(5)

    ins["mixed"].wait()
    ins["datt"].wait()
    g_out[...] = tn(mixed[...], datt[...])
    put(g_out, grad_out, pl.ds(0, width), 4)
    ins["act"].wait()
    ins["douter"].wait()
    for j in range(4):
        these = pl.ds(j * width, width)
        g_down[these, :] = tn(act[:, these], douter[...])
        put(g_down, grad_down, these, 2)
    ins["normed"].wait()
    ins["dinner"].wait()
    for j in range(3):
        these = pl.ds(j * 256, 256)
        g_up[these, :] = tn(normed[:, these], dinner[...])
        put(g_up, grad_up, these, 3)
    ins["xcls"].wait()
    ins["dq"].wait()
    ins["kv"].wait()
    for j in range(3):
        these = pl.ds(j * 256, 256)
        g_qkv[these, pl.ds(0, width)] = tn(xcls[:, these], dq[...])
        for m in range(2):
            g_qkv[these, pl.ds((m + 1) * width, width)] = kv[m, :, these].astype(F32).T
        put(g_qkv, grad_qkv, these, 5)
    through = [
        pltpu.make_async_copy(h_out, hidden_out, out_sem.at[0]),
        pltpu.make_async_copy(h_grad, hidden_grad, out_sem.at[1]),
    ]
    for name, copy in zip(("h_out", "h_grad"), through):
        ins[name].wait()
        copy.start()
    grad_down_bias[...] = column_sum(douter[...])
    grad_up_bias[...] = column_sum(dinner[...])
    grad_out_bias[...] = column_sum(datt[...])
    grad_query_bias[...] = column_sum(dq[...])
    pltpu.make_async_copy(g_down, grad_down.at[0], out_sem.at[2]).wait()
    pltpu.make_async_copy(g_up, grad_up.at[0], out_sem.at[3]).wait()
    pltpu.make_async_copy(g_out, grad_out.at[0], out_sem.at[4]).wait()
    pltpu.make_async_copy(g_qkv, grad_qkv.at[0], out_sem.at[5]).wait()
    for copy in through:
        copy.wait()


def fused_on_device(n, *args):
    (
        hidden_in,
        starts,
        positives,
        qkv_weight,
        query_bias,
        value_bias,
        out_weight,
        out_bias,
        first_gain,
        first_shift,
        up_weight,
        up_bias,
        down_weight,
        down_bias,
        second_gain,
        second_shift,
    ) = args
    rows, length, width = hidden_in.shape[1:]
    tokens = rows * length
    ff = up_weight.shape[-1]
    wide = n * PAD
    side = wide // 2
    spreads = H * PAD
    planes = n // 4
    shape = jax.ShapeDtypeStruct
    hbm = pl.BlockSpec(memory_space=pl.ANY)
    vmem = pl.BlockSpec(memory_space=pltpu.VMEM)
    smem = pl.BlockSpec(memory_space=pltpu.SMEM)
    dma = pltpu.SemaphoreType.DMA
    limit = 60 * 1024 * 1024
    outs = pl.pallas_call(
        functools.partial(main_kernel, n),
        out_shape=[
            shape((tokens, width), BF),
            shape((tokens, width), BF),
            shape((wide, width), BF),
            shape((wide, width), BF),
            shape((wide, width), BF),
            shape((wide, ff), BF),
            shape((wide, width), BF),
            shape((wide, ff), BF),
            shape((wide, width), BF),
            shape((wide, width), BF),
            shape((2, 8, width), F32),
            shape((2, width, width), BF),
        ],
        in_specs=[smem, smem, hbm, hbm, vmem, vmem, hbm, vmem, vmem, vmem, hbm, vmem, hbm, vmem, vmem, vmem],
        out_specs=[hbm] * 12,
        scratch_shapes=[
            pltpu.VMEM((tokens, width), BF),
            pltpu.VMEM((width, 3 * width), BF),
            pltpu.VMEM((width, width), BF),
            pltpu.VMEM((width, ff), BF),
            pltpu.VMEM((ff, width), BF),
            pltpu.VMEM((tokens, 2 * width), BF),
            pltpu.VMEM((tokens, width), BF),
            pltpu.VMEM((tokens, width), BF),
            pltpu.VMEM((length, length), F32),
            pltpu.VMEM((spreads, width), BF),
            pltpu.VMEM((spreads, width), BF),
            pltpu.VMEM((spreads, width), BF),
            pltpu.VMEM((spreads, width), BF),
            pltpu.VMEM((spreads, tokens), F32),
            pltpu.VMEM((spreads, tokens), BF),
            pltpu.VMEM((spreads, tokens), BF),
            pltpu.VMEM((spreads, width), BF),
            pltpu.VMEM((spreads, width), BF),
            pltpu.VMEM((2, side, width), BF),
            pltpu.VMEM((side, width), BF),
            pltpu.VMEM((2, 2, side, width), BF),
            pltpu.VMEM((side, width), F32),
            pltpu.VMEM((side, 128), F32),
            pltpu.VMEM((side, width), F32),
            pltpu.VMEM((side, 128), F32),
            pltpu.VMEM((side, width), BF),
            pltpu.VMEM((side, ff), BF),
            pltpu.VMEM((side, ff), F32),
            pltpu.VMEM((side, ff), BF),
            pltpu.VMEM((side, width), BF),
            pltpu.VMEM((side, width), BF),
            pltpu.VMEM((2, side, width), BF),
            pltpu.VMEM((side, width), F32),
            pltpu.VMEM((side, width), F32),
            pltpu.VMEM((side, width), F32),
            pltpu.VMEM((8, width), F32),
            pltpu.VMEM((width, wide), BF),
            pltpu.VMEM((n, H // 4 * PAD, width // 2), BF),
            pltpu.VMEM((width // 4, width // 2), BF),
            pltpu.VMEM((PAD, width), BF),
            pltpu.VMEM((length, width), BF),
            pltpu.VMEM((length, width), F32),
            pltpu.VMEM((tokens, width), BF),
            pltpu.VMEM((tokens, width), BF),
            dma((7,)),
            dma((18,)),
            dma((n // 2,)),
            dma((n,)),
            dma((n // 2,)),
            dma((n,)),
            dma((n // 2,)),
            dma((n,)),
            dma((3,)),
            dma((3,)),
            dma((4 * planes,)),
            dma((n,)),
            dma((n // 2,)),
            dma((4 * planes,)),
            dma((n,)),
            dma((13,)),
            dma((13,)),
        ],
        compiler_params=pltpu.CompilerParams(
            collective_id=0, has_side_effects=True, vmem_limit_bytes=limit
        ),
        name="layer",
    )(
        starts,
        positives,
        hidden_in.reshape(tokens, width),
        qkv_weight.reshape(width, 3 * width),
        query_bias,
        value_bias,
        out_weight.reshape(width, width),
        out_bias,
        first_gain,
        first_shift,
        up_weight.reshape(width, ff),
        up_bias,
        down_weight.reshape(ff, width),
        down_bias,
        second_gain,
        second_shift,
    )
    h_out, h_grad, xcls, mixed, normed, act, douter, dinner, datt, dq, vecs, kv = outs
    row = shape((1, width), F32)
    grads = pl.pallas_call(
        grad_kernel,
        out_shape=[
            shape((1, 1), F32),
            shape((tokens, width), BF),
            shape((tokens, width), BF),
            shape((1, width, 3 * width), F32),
            row,
            row,
            shape((1, width, width), F32),
            row,
            row,
            row,
            shape((1, width, ff), F32),
            shape((1, ff), F32),
            shape((1, ff, width), F32),
            row,
            row,
            row,
        ],
        in_specs=[hbm] * 11 + [vmem],
        out_specs=[vmem, hbm, hbm, hbm, vmem, vmem, hbm, vmem, vmem, vmem, hbm, vmem, hbm, vmem, vmem, vmem],
        scratch_shapes=[
            pltpu.VMEM((wide, width), BF),
            pltpu.VMEM((wide, width), BF),
            pltpu.VMEM((wide, width), BF),
            pltpu.VMEM((wide, ff), BF),
            pltpu.VMEM((wide, width), BF),
            pltpu.VMEM((wide, ff), BF),
            pltpu.VMEM((wide, width), BF),
            pltpu.VMEM((wide, width), BF),
            pltpu.VMEM((2, width, width), BF),
            pltpu.VMEM((width, 3 * width), F32),
            pltpu.VMEM((width, width), F32),
            pltpu.VMEM((width, ff), F32),
            pltpu.VMEM((ff, width), F32),
            pltpu.VMEM((tokens, width), BF),
            pltpu.VMEM((tokens, width), BF),
            dma((11,)),
            dma((6,)),
        ],
        compiler_params=pltpu.CompilerParams(vmem_limit_bytes=limit),
        name="gradients",
    )(xcls, mixed, normed, act, douter, dinner, datt, dq, kv, h_out, h_grad, vecs)
    place = (1, rows, length, width)
    return (
        grads[0].reshape(()),
        grads[1].reshape(place),
        grads[2].reshape(place),
        *grads[3:],
    )


def solution(mesh):
    placed = (
        P("enc", "dp", None, None),
        P("enc", "dp", None),
        P(),
        P("enc", None, None),
        P("enc", None),
        P("enc", None),
        P("enc", None, None),
        P("enc", None),
        P("enc", None),
        P("enc", None),
        P("enc", None, None),
        P("enc", None),
        P("enc", None, None),
        P("enc", None),
        P("enc", None),
        P("enc", None),
    )
    n = mesh.shape["dp"]
    body = functools.partial(fused_on_device, n) if n == OWNERS else on_device
    return jax.shard_map(
        body,
        mesh=mesh,
        in_specs=placed,
        out_specs=(
            P(),
            P("enc", "dp", None, None),
            P("enc", "dp", None, None),
            P("enc", None, None),
            P("enc", None),
            P("enc", None),
            P("enc", None, None),
            P("enc", None),
            P("enc", None),
            P("enc", None),
            P("enc", None, None),
            P("enc", None),
            P("enc", None, None),
            P("enc", None),
            P("enc", None),
            P("enc", None),
        ),
        check_vma=False,
    )
```

```python
import functools

import jax
import jax.numpy as jnp
from jax import lax
from jax.experimental import pallas as pl
from jax.experimental.pallas import tpu as pltpu
from jax.sharding import PartitionSpec as P

OWNERS = 16
H = 12
DOCS = 4


EPS_NORM = 1e-12


def partner(value, axis, distance):
    mask = 2**distance
    pairs = [(source, source ^ mask) for source in range(lax.axis_size(axis))]
    return lax.ppermute(value, axis, pairs)


def product(left, right):
    return jnp.dot(left, right, preferred_element_type=jnp.float32)


def layer_stats(hidden):
    centred = hidden - jnp.mean(hidden, -1, keepdims=True)
    inverse = lax.rsqrt(jnp.mean(centred * centred, -1, keepdims=True) + EPS_NORM)
    return (centred * inverse, inverse)


def norm_back(upstream, normal, inverse, gain):
    scaled = upstream * gain
    return inverse * (
        scaled
        - jnp.mean(scaled, -1, keepdims=True)
        - normal * jnp.mean(scaled * normal, -1, keepdims=True)
    )


def on_device(
    hidden_in,
    starts,
    positives,
    qkv_weight,
    query_bias,
    value_bias,
    out_weight,
    out_bias,
    first_gain,
    first_shift,
    up_weight,
    up_bias,
    down_weight,
    down_bias,
    second_gain,
    second_shift,
):
    rows, length, width = (hidden_in.shape[1], hidden_in.shape[2], hidden_in.shape[3])
    heads = H
    head_size = width // heads
    tokens = rows * length
    flat = hidden_in.reshape(tokens, width)
    w_qkv = qkv_weight[0]
    w_out = out_weight[0]
    w_up = up_weight[0]
    w_down = down_weight[0]
    row_starts = starts[0]
    qkv_shift = jnp.concatenate([query_bias[0], jnp.zeros_like(query_bias[0]), value_bias[0]])
    qkv = (product(flat, w_qkv) + qkv_shift).astype(jnp.bfloat16)
    split = qkv.reshape(rows, length, 3, heads, head_size)
    query, key, value = (split[:, :, 0], split[:, :, 1], split[:, :, 2])
    places = jnp.arange(length, dtype=jnp.int32)
    segment = jnp.sum((places[None, :, None] >= row_starts[:, None, :]).astype(jnp.int32), -1)
    allowed = (segment[:, :, None] == segment[:, None, :])[:, None]
    head_scale = head_size ** (-0.5)

    def attention_scores(left, right):
        raw = jnp.einsum("rqhe,rkhe->rhqk", left, right, preferred_element_type=jnp.float32)
        return jnp.where(allowed, head_scale * raw, -1e30)

    scores = attention_scores(query, key)
    peak = jnp.max(scores, -1, keepdims=True)
    log_total = peak + jnp.log(jnp.sum(jnp.exp(scores - peak), -1, keepdims=True))
    weights_low = jnp.exp(scores - log_total).astype(jnp.bfloat16)
    mixed = jnp.einsum("rhqk,rkhe->rqhe", weights_low, value, preferred_element_type=jnp.float32)
    mixed = mixed.astype(jnp.bfloat16).reshape(tokens, width)
    attended = product(mixed, w_out) + out_bias[0]
    first_normal, first_inverse = layer_stats(flat.astype(jnp.float32) + attended)
    normed = first_normal * first_gain[0] + first_shift[0]
    normed_low = normed.astype(jnp.bfloat16)
    inner = product(normed_low, w_up) + up_bias[0]
    activated_low = jax.nn.gelu(inner, approximate=False).astype(jnp.bfloat16)
    outer = product(activated_low, w_down) + down_bias[0]
    second_normal, second_inverse = layer_stats(normed + outer)
    encoded = second_normal * second_gain[0] + second_shift[0]
    hidden_out = encoded.astype(jnp.bfloat16).reshape(1, rows, length, width)
    picker = (places[None, None, :] == row_starts[:, :, None]).astype(jnp.float32)
    cls = jnp.einsum(
        "rdl,rlw->rdw",
        picker,
        encoded.reshape(rows, length, width),
        precision=lax.Precision.HIGHEST,
    )
    local_count = rows * DOCS
    cls_low = cls.reshape(local_count, width).astype(jnp.bfloat16)
    first_half = lax.axis_index("enc") == 0
    mine = lax.all_gather(cls_low, "dp", axis=0, tiled=True)
    other = partner(mine, "enc", 0)
    questions = jnp.where(first_half, mine, other)
    passages = jnp.where(first_half, other, mine)
    count = questions.shape[0]
    sim_scale = width ** (-0.5)
    sims = sim_scale * jnp.einsum(
        "qw,pw->qp", questions, passages, preferred_element_type=jnp.float32
    )
    sim_peak = jnp.max(sims, -1, keepdims=True)
    sim_total = sim_peak + jnp.log(jnp.sum(jnp.exp(sims - sim_peak), -1, keepdims=True))
    target = (jnp.arange(count, dtype=jnp.int32)[None, :] == positives[:, None]).astype(jnp.float32)
    total = jnp.sum(sim_total[:, 0] - jnp.sum(sims * target, -1)) / local_count
    loss_mean = total / lax.axis_size("dp")
    d_sims_low = (sim_scale * (jnp.exp(sims - sim_total) - target) / local_count).astype(
        jnp.bfloat16
    )
    own_start = lax.axis_index("dp") * local_count
    own_rows = lax.dynamic_slice_in_dim(d_sims_low, own_start, local_count, 0)
    own_columns = lax.dynamic_slice_in_dim(d_sims_low, own_start, local_count, 1)
    d_questions = jnp.einsum("qp,pw->qw", own_rows, passages, preferred_element_type=jnp.float32)
    d_passages = jnp.einsum("qp,qw->pw", own_columns, questions, preferred_element_type=jnp.float32)
    d_cls = jnp.where(first_half, d_questions, d_passages).reshape(rows, DOCS, width)
    d_encoded = jnp.einsum("rdl,rdw->rlw", picker, d_cls, precision=lax.Precision.HIGHEST).reshape(
        tokens, width
    )
    grad_second_gain = jnp.sum(d_encoded * second_normal, 0)
    grad_second_shift = jnp.sum(d_encoded, 0)
    d_second = norm_back(d_encoded, second_normal, second_inverse, second_gain[0])
    d_outer_low = d_second.astype(jnp.bfloat16)
    grad_down_bias = jnp.sum(d_outer_low.astype(jnp.float32), 0)
    grad_down_weight = jnp.einsum(
        "tf,tw->fw", activated_low, d_outer_low, preferred_element_type=jnp.float32
    )
    d_activated = jnp.einsum("tw,fw->tf", d_outer_low, w_down, preferred_element_type=jnp.float32)
    normal_cdf = 0.5 * (1.0 + lax.erf(inner * 0.7071067811865476))
    slope = normal_cdf + inner * jnp.exp(-0.5 * inner * inner) * 0.3989422804014327
    d_inner_low = (d_activated * slope).astype(jnp.bfloat16)
    grad_up_bias = jnp.sum(d_inner_low.astype(jnp.float32), 0)
    grad_up_weight = jnp.einsum(
        "tw,tf->wf", normed_low, d_inner_low, preferred_element_type=jnp.float32
    )
    d_normed = d_second + jnp.einsum(
        "tf,wf->tw", d_inner_low, w_up, preferred_element_type=jnp.float32
    )
    grad_first_gain = jnp.sum(d_normed * first_normal, 0)
    grad_first_shift = jnp.sum(d_normed, 0)
    d_first = norm_back(d_normed, first_normal, first_inverse, first_gain[0])
    d_attended_low = d_first.astype(jnp.bfloat16)
    grad_out_bias = jnp.sum(d_attended_low.astype(jnp.float32), 0)
    grad_out_weight = jnp.einsum(
        "tv,tw->vw", mixed, d_attended_low, preferred_element_type=jnp.float32
    )
    d_mixed_low = jnp.einsum(
        "tw,vw->tv", d_attended_low, w_out, preferred_element_type=jnp.float32
    ).astype(jnp.bfloat16)
    d_mixed_heads = d_mixed_low.reshape(rows, length, heads, head_size)
    probs_again = jnp.exp(attention_scores(query, key) - log_total)
    weights_again = probs_again.astype(jnp.bfloat16)
    grad_value = jnp.einsum(
        "rhqk,rqhe->rkhe", weights_again, d_mixed_heads, preferred_element_type=jnp.float32
    )
    d_weights = jnp.einsum(
        "rqhe,rkhe->rhqk", d_mixed_heads, value, preferred_element_type=jnp.float32
    )
    d_scores = probs_again * (d_weights - jnp.sum(d_weights * probs_again, -1, keepdims=True))
    d_raw_low = (head_scale * d_scores).astype(jnp.bfloat16)
    grad_query = jnp.einsum("rhqk,rkhe->rqhe", d_raw_low, key, preferred_element_type=jnp.float32)
    grad_key = jnp.einsum("rhqk,rqhe->rkhe", d_raw_low, query, preferred_element_type=jnp.float32)
    d_qkv_low = (
        jnp.stack([grad_query, grad_key, grad_value], 2)
        .reshape(tokens, 3 * width)
        .astype(jnp.bfloat16)
    )
    grad_qkv_local = jnp.einsum("tw,tv->wv", flat, d_qkv_low, preferred_element_type=jnp.float32)
    bias_sums = jnp.sum(d_qkv_low.astype(jnp.float32), 0)
    grad_query_local = bias_sums[:width]
    grad_value_local = bias_sums[2 * width :]
    d_input = d_first + jnp.einsum(
        "tv,wv->tw", d_qkv_low, w_qkv, preferred_element_type=jnp.float32
    )
    hidden_grad = d_input.astype(jnp.bfloat16).reshape(1, rows, length, width)
    (
        share_qkv,
        share_query_bias,
        share_value_bias,
        share_out_weight,
        share_out_bias,
        share_first_gain,
        share_first_shift,
        share_up_weight,
        share_up_bias,
        share_down_weight,
        share_down_bias,
        share_second_gain,
        share_second_shift,
    ) = (
        lax.psum_scatter(grad_qkv_local[None], "dp", scatter_dimension=1, tiled=True),
        lax.psum_scatter(grad_query_local[None], "dp", scatter_dimension=1, tiled=True),
        lax.psum_scatter(grad_value_local[None], "dp", scatter_dimension=1, tiled=True),
        lax.psum_scatter(grad_out_weight[None], "dp", scatter_dimension=1, tiled=True),
        lax.psum_scatter(grad_out_bias[None], "dp", scatter_dimension=1, tiled=True),
        lax.psum_scatter(grad_first_gain[None], "dp", scatter_dimension=1, tiled=True),
        lax.psum_scatter(grad_first_shift[None], "dp", scatter_dimension=1, tiled=True),
        lax.psum_scatter(grad_up_weight[None], "dp", scatter_dimension=1, tiled=True),
        lax.psum_scatter(grad_up_bias[None], "dp", scatter_dimension=1, tiled=True),
        lax.psum_scatter(grad_down_weight[None], "dp", scatter_dimension=1, tiled=True),
        lax.psum_scatter(grad_down_bias[None], "dp", scatter_dimension=1, tiled=True),
        lax.psum_scatter(grad_second_gain[None], "dp", scatter_dimension=1, tiled=True),
        lax.psum_scatter(grad_second_shift[None], "dp", scatter_dimension=1, tiled=True),
    )
    summed = (
        lax.all_gather(share_qkv.astype(jnp.bfloat16), "dp", axis=1, tiled=True).astype(
            share_qkv.dtype
        ),
        lax.all_gather(share_query_bias.astype(jnp.bfloat16), "dp", axis=1, tiled=True).astype(
            share_query_bias.dtype
        ),
        lax.all_gather(share_value_bias.astype(jnp.bfloat16), "dp", axis=1, tiled=True).astype(
            share_value_bias.dtype
        ),
        lax.all_gather(share_out_weight.astype(jnp.bfloat16), "dp", axis=1, tiled=True).astype(
            share_out_weight.dtype
        ),
        lax.all_gather(share_out_bias.astype(jnp.bfloat16), "dp", axis=1, tiled=True).astype(
            share_out_bias.dtype
        ),
        lax.all_gather(share_first_gain.astype(jnp.bfloat16), "dp", axis=1, tiled=True).astype(
            share_first_gain.dtype
        ),
        lax.all_gather(share_first_shift.astype(jnp.bfloat16), "dp", axis=1, tiled=True).astype(
            share_first_shift.dtype
        ),
        lax.all_gather(share_up_weight.astype(jnp.bfloat16), "dp", axis=1, tiled=True).astype(
            share_up_weight.dtype
        ),
        lax.all_gather(share_up_bias.astype(jnp.bfloat16), "dp", axis=1, tiled=True).astype(
            share_up_bias.dtype
        ),
        lax.all_gather(share_down_weight.astype(jnp.bfloat16), "dp", axis=1, tiled=True).astype(
            share_down_weight.dtype
        ),
        lax.all_gather(share_down_bias.astype(jnp.bfloat16), "dp", axis=1, tiled=True).astype(
            share_down_bias.dtype
        ),
        lax.all_gather(share_second_gain.astype(jnp.bfloat16), "dp", axis=1, tiled=True).astype(
            share_second_gain.dtype
        ),
        lax.all_gather(share_second_shift.astype(jnp.bfloat16), "dp", axis=1, tiled=True).astype(
            share_second_shift.dtype
        ),
    )
    return (
        loss_mean,
        hidden_out,
        hidden_grad,
        summed[0],
        summed[1],
        summed[2],
        summed[3],
        summed[4],
        summed[5],
        summed[6],
        summed[7],
        summed[8],
        summed[9],
        summed[10],
        summed[11],
        summed[12],
    )


PAD = 16
BF = jnp.bfloat16
F32 = jnp.float32
MESH = pl.DeviceIdType.MESH
NEG = -1e30
ROOT_HALF = 0.7071067811865476
PEAK = 0.3989422804014327


def nn(left, right):
    return jnp.dot(left, right, preferred_element_type=F32)


def nt(left, right):
    return lax.dot_general(left, right, (((1,), (1,)), ((), ())), preferred_element_type=F32)


def tn(left, right):
    return lax.dot_general(left, right, (((0,), (0,)), ((), ())), preferred_element_type=F32)


def iota(shape, dim):
    return lax.broadcasted_iota(jnp.int32, shape, dim)


def gelu_parts(inner):
    cdf = 0.5 * (1.0 + lax.erf(inner * ROOT_HALF))
    return cdf, jnp.exp(-0.5 * inner * inner) * PEAK


def chunk(index, size):
    return pl.ds(pl.multiple_of(index * size, size), size)


def loop(count, body):
    def step(index, carry):
        body(index)
        return carry

    lax.fori_loop(0, count, step, 0)


def main_kernel(
    n,
    starts,
    positives,
    x_hbm,
    qkv_hbm,
    q_bias,
    v_bias,
    out_hbm,
    o_bias,
    gain1,
    shift1,
    up_hbm,
    u_bias,
    down_hbm,
    d_bias,
    gain2,
    shift2,
    hidden_out,
    hidden_grad,
    xcls_o,
    mixed_o,
    normed_o,
    act_o,
    douter_o,
    dinner_o,
    datt_o,
    dq_o,
    vecs_o,
    kv_o,
    x,
    w_qkv,
    w_out,
    w_up,
    w_down,
    kv,
    q,
    mix,
    seg_bias,
    qbd,
    dbd,
    qk,
    dv,
    probs,
    p_low,
    ds_low,
    px,
    dx,
    xcls,
    mixed,
    cls,
    norm1,
    inv1,
    norm2,
    inv2,
    normed,
    act,
    slope,
    dinner,
    douter,
    datt,
    dmix,
    d_cls,
    dfirst,
    acc,
    vecs,
    turned,
    recv,
    piece,
    turned_v,
    recv_v,
    piece_v,
    dq_own,
    low_t,
    acc_t,
    hout,
    hgrad,
    load_sem,
    save_sem,
    xs_sem,
    xr_sem,
    ms_sem,
    mr_sem,
    ks_sem,
    kr_sem,
    cs_sem,
    cr_sem,
    qs_sem,
    qr_sem,
    vs_sem,
    vr_sem,
    gs_sem,
    gr_sem,
    hs_sem,
    hr_sem,
    fs_sem,
    fr_sem,
):
    enc = lax.axis_index("enc")
    me = lax.axis_index("dp")
    other = 1 - enc
    core = lax.rem(me, 2)
    which = lax.div(me, 2)
    sibling = me + 1 - 2 * core
    across = me + 2 - 4 * lax.rem(which, 2)
    tokens, width = x.shape
    ff = w_up.shape[1]
    side = n // 2 * PAD
    rows = starts.shape[0]
    length = tokens // rows
    local = rows * DOCS
    head = width // H
    pairs = H // 2
    head_scale = head ** (-0.5)
    group_cols = width // 4
    half_feats = width // 2
    group_rows = H // 4 * PAD
    query_w = pl.ds(0, width)
    key_w = pl.ds(width, width)
    value_w = pl.ds(2 * width, width)

    def weight_load(cols, index):
        return pltpu.make_async_copy(qkv_hbm.at[:, cols], w_qkv.at[:, cols], load_sem.at[index])

    loads = [
        pltpu.make_async_copy(x_hbm, x, load_sem.at[0]),
        weight_load(key_w, 1),
        weight_load(query_w, 2),
        weight_load(value_w, 3),
        pltpu.make_async_copy(out_hbm, w_out, load_sem.at[4]),
        pltpu.make_async_copy(up_hbm, w_up, load_sem.at[5]),
        pltpu.make_async_copy(down_hbm, w_down, load_sem.at[6]),
    ]
    for copy in loads:
        copy.start()

    barrier = pltpu.get_barrier_semaphore()

    def greet(j):
        peer = lax.rem(me + j + 1, n)
        pl.semaphore_signal(barrier, inc=1, device_id=(enc, peer), device_id_type=MESH)

    loop(n - 1, greet)
    pl.semaphore_signal(barrier, inc=1, device_id=(other, me), device_id_type=MESH)

    def remote(source, target, send, receive, device):
        return pltpu.make_async_remote_copy(
            src_ref=source,
            dst_ref=target,
            send_sem=send,
            recv_sem=receive,
            device_id=device,
            device_id_type=MESH,
        )

    def same_core(j):
        return lax.rem(me + 2 * j + 2, n)

    def cousin(j):
        return lax.rem(same_core(j) + 1 - 2 * core + n, n)

    def block(index):
        return pl.ds(pl.multiple_of(index * PAD, PAD), PAD)

    own = block(which)

    def share(source, place, send, receive):
        def go(j):
            remote(source, place(me), send.at[j], receive.at[me], (enc, same_core(j))).start()

        loop(n // 2 - 1, go)

    def shared(source, place, send, receive):
        def came(j):
            peer = same_core(j)
            copy = remote(source, place(peer), send.at[j], receive.at[peer], (enc, peer))
            copy.wait_send()
            copy.wait_recv()

        loop(n // 2 - 1, came)

    class Relay:
        def __init__(self, source, place, send, receive, group):
            self.source, self.place, self.send, self.receive = source, place, send, receive
            self.base = me - lax.rem(me, group)
            self.group = group
            self.ups = group // 4 - 1

        def up(self, device, j):
            return self.base + lax.rem(device - self.base + 4 * j, self.group)

        def copy(self, slot, source, owner, device):
            return remote(
                source, self.place(owner), self.send.at[slot], self.receive.at[owner], (enc, device)
            )

        def start(self):
            for j in range(self.ups):
                self.copy(j, self.source, me, self.up(me, j + 1)).start()
            self.copy(self.ups, self.source, me, across).start()
            self.copy(self.ups + 1, self.source, me, sibling).start()

        def plane(self):
            for j in range(self.ups):
                peer = self.up(me, j + 1)
                self.copy(0, self.place(peer), peer, peer).wait_recv()
                self.copy(self.ups + 2 + 2 * j, self.place(peer), peer, across).start()
                self.copy(self.ups + 3 + 2 * j, self.place(peer), peer, sibling).start()

        def over(self):
            for j in range(self.ups + 1):
                peer = self.up(across, j)
                self.copy(0, self.place(peer), peer, across).wait_recv()
                self.copy(3 * self.ups + 2 + j, self.place(peer), peer, sibling).start()

        def sent(self):
            def wait(j):
                self.copy(j, self.source, me, sibling).wait_send()

            loop(4 * self.ups + 3, wait)

        def came(self):
            for j in range(self.ups + 1):
                for peer in (self.up(sibling, j), self.up(across + sibling - me, j)):
                    self.copy(0, self.place(peer), peer, sibling).wait_recv()

    saves = []

    def save(source, target, index):
        copy = pltpu.make_async_copy(source, target, save_sem.at[index])
        copy.start()
        saves.append(copy)

    halves = [pl.ds(pl.multiple_of(core * side, side), side)]
    halves.append(pl.ds(pl.multiple_of((1 - core) * side, side), side))
    given = []

    def give(source, target, index):
        save(source, target.at[halves[0]], index)
        copy = remote(source, target.at[halves[0]], fs_sem.at[index], fr_sem.at[index], (enc, sibling))
        copy.start()
        given.append(
            remote(source, target.at[halves[1]], fs_sem.at[index], fr_sem.at[index], (enc, sibling))
        )

    first_col = jnp.full((PAD, 1), -1, jnp.int32)
    seg_col = jnp.full((PAD, 1), -1, jnp.int32)
    place_col = iota((PAD, 1), 0)
    segs = []
    for r in range(rows):
        place = iota((1, length), 1)
        count = jnp.zeros((1, length), jnp.int32)
        for k in range(DOCS):
            start = starts[r, 0, k]
            count = count + (place >= start).astype(jnp.int32)
            order = jnp.int32(0)
            for m in range(DOCS):
                order = order + jnp.where(starts[r, 0, m] <= start, 1, 0)
            here = place_col == r * DOCS + k
            first_col = jnp.where(here, r * length + start, first_col)
            seg_col = jnp.where(here, r * 8 + order, seg_col)
        segs.append(count + r * 8)
    seg_row = jnp.concatenate(segs, axis=1)
    pick = (iota((PAD, tokens), 1) == first_col).astype(F32).astype(BF)
    allowed = seg_row == seg_col

    low_half = iota((1, 128), 1) < head

    def block_diagonal(target, block_rows):
        for p in range(pairs):
            part = block_rows[:, p * 128 : (p + 1) * 128]
            even = jnp.where(low_half, part, 0.0).astype(BF)
            odd = jnp.where(low_half, 0.0, part).astype(BF)
            target[pl.ds(2 * p * PAD, PAD), pl.ds(p * 128, 128)] = even
            target[pl.ds((2 * p + 1) * PAD, PAD), pl.ds(p * 128, 128)] = odd

    def own_lanes(full):
        parts = []
        for p in range(pairs):
            lanes = slice(p * 128, (p + 1) * 128)
            even = full[2 * p * PAD : (2 * p + 1) * PAD, lanes]
            odd = full[(2 * p + 1) * PAD : (2 * p + 2) * PAD, lanes]
            parts.append(jnp.where(low_half, even, odd))
        return jnp.concatenate(parts, axis=1)

    qbd[...] = jnp.zeros_like(qbd)
    dbd[...] = jnp.zeros_like(dbd)
    loads[0].wait()
    xcls[core, own, :] = nn(pick, x[...]).astype(BF)
    pl.semaphore_wait(barrier, n)

    def xcls_place(peer):
        return xcls.at[core, block(lax.div(peer, 2))]

    share(xcls.at[core, own], xcls_place, xs_sem, xr_sem)

    loads[1].wait()
    kv[:, pl.ds(0, width)] = nn(x[...], w_qkv[:, key_w]).astype(BF)
    loads[2].wait()
    q_own = (nn(xcls[core, own, :], w_qkv[:, query_w]) + q_bias[...]).astype(BF).astype(F32)
    block_diagonal(qbd, q_own)
    loads[3].wait()
    kv[:, pl.ds(width, width)] = (nn(x[...], w_qkv[:, value_w]) + v_bias[...]).astype(BF)
    allowed_all = jnp.concatenate([allowed] * H, axis=0)
    scores = jnp.where(allowed_all, head_scale * nt(qbd[...], kv[:, pl.ds(0, width)]), NEG)
    peak = jnp.max(scores, -1, keepdims=True)
    raw = jnp.where(allowed_all, jnp.exp(scores - peak), 0.0)
    total = jnp.sum(raw, -1, keepdims=True)
    weights = raw / jnp.where(total > 0.0, total, 1.0)
    probs[...] = weights
    p_low[...] = weights.astype(BF)
    mixed[own, :] = own_lanes(nn(p_low[...], kv[:, pl.ds(width, width)])).astype(BF)

    def mixed_place(peer):
        return mixed.at[block(lax.div(peer, 2))]

    share(mixed.at[own], mixed_place, ms_sem, mr_sem)

    half_n = n // 2

    def slot_of(peer):
        return lax.rem(peer, 2) * half_n + lax.div(peer, 2)

    def send_pieces(source, into, owners, send, receive):
        for j, owner in enumerate(owners):
            i = j % half_n
            part = source.at[
                pl.ds((i % 4) * group_rows, group_rows), pl.ds((i // 4) * half_feats, half_feats)
            ]

            @pl.when(me != owner)
            def _():
                remote(part, into.at[slot_of(me)], send.at[j], receive.at[me], (enc, owner)).start()

            @pl.when(me == owner)
            def _():
                into[slot_of(me)] = part[...]

    def sent_pieces(source, into, owners, send, receive):
        part = source.at[pl.ds(0, group_rows), pl.ds(0, half_feats)]
        for j, owner in enumerate(owners):

            @pl.when(me != owner)
            def _():
                remote(
                    part, into.at[slot_of(me)], send.at[j], receive.at[me], (enc, owner)
                ).wait_send()

    def pieces_came(into, receive):
        def came(j):
            peer = lax.rem(me + j + 1, n)
            place = into.at[slot_of(peer)]
            remote(place, place, ks_sem.at[0], receive.at[peer], (enc, peer)).wait_recv()

        loop(n - 1, came)

    key_owners = range(0, n, 2)
    px[...] = nn(p_low[...], x[...]).astype(BF)
    def attend_row(r):
        place0 = iota((length, 1), 0)
        place1 = iota((1, length), 1)
        count0 = jnp.zeros((length, 1), jnp.int32)
        count1 = jnp.zeros((1, length), jnp.int32)
        for k in range(DOCS):
            start = starts[r, 0, k]
            count0 = count0 + (place0 >= start).astype(jnp.int32)
            count1 = count1 + (place1 >= start).astype(jnp.int32)
        seg_bias[...] = jnp.where(count0 == count1, 0.0, NEG)
        these = pl.ds(r * length, length)
        mask_even = jnp.where(low_half, 1.0, 0.0).astype(BF)
        mask_odd = jnp.where(low_half, 0.0, 1.0).astype(BF)

        for p in range(pairs):
            lanes = pl.ds(p * 128, 128)
            query = q[these, lanes]
            key = kv[these, lanes]
            value = kv[these, pl.ds(width + p * 128, 128)]
            ext = jnp.concatenate([value, jnp.ones_like(value)], axis=1)
            outs = []
            for mask in (mask_even, mask_odd):
                s = nt(query * mask, key) + seg_bias[...]
                e = jnp.exp(s - jnp.max(s, -1, keepdims=True)).astype(BF)
                outs.append(nn(e, ext))
            even, odd = outs
            top = jnp.where(low_half, even[:, :128], odd[:, :128])
            low = jnp.where(low_half, even[:, 128:], odd[:, 128:])
            mix[these, lanes] = (top / low).astype(BF)

    shared(xcls.at[core, own], xcls_place, xs_sem, xr_sem)
    xcls_over = remote(xcls.at[core], xcls.at[core], fs_sem.at[10], fr_sem.at[10], (enc, sibling))
    xcls_over.start()
    xcls_back = remote(xcls.at[core], xcls.at[1 - core], fs_sem.at[10], fr_sem.at[10], (enc, sibling))
    shared(mixed.at[own], mixed_place, ms_sem, mr_sem)
    send_pieces(px, recv_v, range(n), vs_sem, vr_sem)
    loads[4].wait()

    acc[...] = nn(mixed[...], w_out[...]) + o_bias[...] + xcls[core].astype(F32)

    def stats(h):
        centred = h - jnp.mean(h, -1, keepdims=True)
        inverse = lax.rsqrt(jnp.mean(centred * centred, -1, keepdims=True) + EPS_NORM)
        return centred * inverse, inverse

    unit, inverse = stats(acc[...])
    norm1[...] = unit
    inv1[...] = jnp.broadcast_to(inverse, inv1.shape)
    level = unit * gain1[...] + shift1[...]
    normed[...] = level.astype(BF)
    loads[5].wait()
    loads[6].wait()
    inner = nn(normed[...], w_up[...]) + u_bias[...]
    cdf, pdf = gelu_parts(inner)
    slope[...] = cdf + inner * pdf
    act[...] = (inner * cdf).astype(BF)
    unit, inverse = stats(level + d_bias[...] + nn(act[...], w_down[...]))
    norm2[...] = unit
    inv2[...] = jnp.broadcast_to(inverse, inv2.shape)
    cls[enc, core] = (unit * gain2[...] + shift2[...]).astype(BF)

    def cls_copy(half_of, to_core, index, device):
        return remote(
            cls.at[half_of, core], cls.at[half_of, to_core], cs_sem.at[index], cr_sem.at[index], device
        )

    cls_copy(enc, core, 0, (other, me)).start()
    cls_copy(enc, core, 1, (enc, sibling)).start()
    give(mixed, mixed_o, 1)
    give(normed, normed_o, 2)
    give(act, act_o, 3)

    def padded(question):
        device = lax.div(question, local)
        place = lax.rem(device, 2) * side + lax.div(device, 2) * PAD
        return place + question - device * local

    count = n * local
    spot = padded(iota((count, 1), 0)) == iota((count, 2 * side), 1)
    goal = padded(positives[...].reshape(1, count)) + 1
    pos_row = nn(goal.astype(F32).astype(BF), spot.astype(F32).astype(BF)).astype(jnp.int32) - 1

    xcls_back.wait_recv()

    @pl.when(core == 0)
    def _():
        for c in range(2):
            y = (nn(xcls[c], w_qkv[:, query_w]) + q_bias[...]).astype(BF).astype(F32)
            turned[:, pl.ds(c * side, side)] = y.T.astype(BF)

    save(xcls.at[0], xcls_o.at[pl.ds(0, side)], 4)
    save(xcls.at[1], xcls_o.at[pl.ds(side, side)], 5)

    cls_copy(enc, core, 0, (other, me)).wait_send()
    cls_in = remote(cls.at[enc, core], cls.at[other, core], cs_sem.at[0], cr_sem.at[0], (other, me))
    cls_in.wait_recv()
    cls_pass = cls_copy(other, core, 2, (enc, sibling))
    cls_pass.start()
    cls_copy(enc, core, 1, (enc, sibling)).wait_send()
    remote(
        cls.at[enc, core], cls.at[enc, 1 - core], cs_sem.at[1], cr_sem.at[1], (enc, sibling)
    ).wait_recv()
    cls_pass.wait_send()
    remote(
        cls.at[other, core], cls.at[other, 1 - core], cs_sem.at[2], cr_sem.at[2], (enc, sibling)
    ).wait_recv()

    sim_scale = width ** (-0.5)
    good_col = lax.rem(iota((2 * side, 1), 0), PAD) < local
    good_row = lax.rem(iota((1, 2 * side), 1), PAD) < local
    questions = cls[0].reshape(2 * side, width)
    passages = cls[1].reshape(2 * side, width)
    raw_sims = sim_scale * nt(passages, questions)
    sims = jnp.where(good_col, raw_sims, NEG)
    sim_peak = jnp.max(sims, 0, keepdims=True)
    sim_total = sim_peak + jnp.log(jnp.sum(jnp.exp(sims - sim_peak), 0, keepdims=True))
    target = (iota((2 * side, 2 * side), 0) == pos_row).astype(F32)
    losses = sim_total - jnp.sum(raw_sims * target, 0, keepdims=True)
    loss = jnp.sum(jnp.where(good_row, losses, 0.0), -1, keepdims=True) / (local * n)
    d_sims = sim_scale * (jnp.exp(sims - sim_total) - target) / local
    d_sims = jnp.where(good_row, d_sims, 0.0).astype(BF)

    for c in range(2):
        these = slice(c * side, (c + 1) * side)

        @pl.when((enc == 0) & (core == c))
        def _():
            d_cls[...] = tn(d_sims[:, these], passages)

        @pl.when((enc == 1) & (core == c))
        def _():
            d_cls[...] = nn(d_sims[these, :], questions)

    def column_sum(value):
        return jnp.sum(value, 0, keepdims=True)

    def back(upstream, unit, inverse, gain):
        scaled = upstream * gain
        return inverse[:, :1] * (
            scaled
            - jnp.mean(scaled, -1, keepdims=True)
            - unit * jnp.mean(scaled * unit, -1, keepdims=True)
        )

    vecs[pl.ds(0, 1), :] = column_sum(d_cls[...] * norm2[...])
    vecs[pl.ds(1, 1), :] = column_sum(d_cls[...])
    d_second = back(d_cls[...], norm2[...], inv2[...], gain2[...])
    douter[...] = d_second.astype(BF)
    d_active = nt(douter[...], w_down[...])
    dinner[...] = (d_active * slope[...]).astype(BF)
    acc[...] = d_second + nt(dinner[...], w_up[...])
    vecs[pl.ds(2, 1), :] = column_sum(acc[...] * norm1[...])
    vecs[pl.ds(3, 1), :] = column_sum(acc[...])
    vecs[pl.ds(4, 1), :] = jnp.broadcast_to(loss, (1, width))
    vecs[pl.ds(6, 2), :] = jnp.zeros((2, width), F32)
    d_first = back(acc[...], norm1[...], inv1[...], gain1[...])
    dfirst[...] = d_first
    datt[...] = d_first.astype(BF)

    dmix[core] = nt(datt[...], w_out[...]).astype(BF)
    dmix_over = remote(dmix.at[core], dmix.at[core], fs_sem.at[11], fr_sem.at[11], (enc, sibling))
    dmix_back = remote(dmix.at[core], dmix.at[1 - core], fs_sem.at[11], fr_sem.at[11], (enc, sibling))

    dmix_over.start()

    block_diagonal(dbd, dmix[core, own, :].astype(F32))
    d_weights = nt(dbd[...], kv[:, pl.ds(width, width)])
    weights = probs[...]
    inner_sum = jnp.sum(d_weights * weights, -1, keepdims=True)
    ds_low[...] = (head_scale * weights * (d_weights - inner_sum)).astype(BF)
    dx[...] = nn(ds_low[...], x[...]).astype(BF)
    send_pieces(dx, recv, key_owners, ks_sem, kr_sem)
    dq_own[...] = own_lanes(nn(ds_low[...], kv[:, pl.ds(0, width)])).astype(BF)

    def dq_place(peer):
        return dq_o.at[block(slot_of(peer))]

    save(dq_own, dq_place(me), 6)
    give(douter, douter_o, 7)
    give(dinner, dinner_o, 8)
    give(datt, datt_o, 9)
    vecs[pl.ds(5, 1), :] = column_sum(dmix[core].astype(F32))

    def layer_tile(r):
        these = pl.ds(r * length, length)

        acc_t[...] = nn(mix[these, :], w_out[...]) + o_bias[...] + x[these, :].astype(F32)
        unit, _ = stats(acc_t[...])
        level = unit * gain1[...] + shift1[...]
        low_t[...] = level.astype(BF)
        inner = nn(low_t[...], w_up[...]) + u_bias[...]
        active = (0.5 * inner * (1.0 + lax.erf(inner * ROOT_HALF))).astype(BF)
        unit, _ = stats(level + d_bias[...] + nn(active, w_down[...]))
        hout[these, :] = (unit * gain2[...] + shift2[...]).astype(BF)
        save(hout.at[these], hidden_out.at[these], 13 + r)

    def piece_place(matrix, i):
        return kv_o.at[
            matrix,
            pl.ds(pl.multiple_of(lax.rem(i, 4) * group_cols, group_cols), group_cols),
            pl.ds(pl.multiple_of(lax.div(i, 4) * half_feats, half_feats), half_feats),
        ]

    def key_place(peer):
        return piece_place(0, lax.div(peer, 2))

    def value_place(peer):
        return piece_place(1, lax.rem(peer, half_n))

    keys = Relay(piece, key_place, gs_sem, gr_sem, n)
    values = Relay(piece_v, value_place, hs_sem, hr_sem, half_n)
    key_save = pltpu.make_async_copy(piece, key_place(me), save_sem.at[16])

    def sum_pieces(i, left, right, target):
        for a in range(H // 4):
            rows_a = right[:, pl.ds(a * PAD, PAD), :].reshape(2 * side, half_feats)
            start = lax.rem(i, 4) * group_cols + a * head
            cols_a = left[pl.ds(pl.multiple_of(start, head), head), :]
            target[pl.ds(a * head, head), :] = nn(cols_a, rows_a).astype(BF)

    pieces_came(recv_v, vr_sem)
    dmix_back.wait_recv()
    for c in range(2):
        turned_v[:, pl.ds(c * side, side)] = dmix[c].astype(F32).T.astype(BF)
    sum_pieces(lax.rem(me, half_n), turned_v, recv_v, piece_v)
    values.start()
    save(piece_v, value_place(me), 10)

    y = nn(x[...], w_qkv[:, query_w]) + q_bias[...]
    q[...] = (y.astype(BF).astype(F32) * head_scale).astype(BF)
    for r in range(rows):
        attend_row(r)
    values.plane()

    @pl.when(core == 0)
    def _():
        pieces_came(recv, kr_sem)
        sum_pieces(which, turned, recv, piece)
        keys.start()
        key_save.start()

    layer_tile(0)
    values.over()
    layer_tile(1)
    share(dq_own, dq_place, qs_sem, qr_sem)
    remote(dq_own, dq_place(me), qs_sem.at[n - 2], qr_sem.at[me], (enc, sibling)).start()

    @pl.when(core == 0)
    def _():
        keys.plane()

    layer_tile(2)

    base = dfirst[own, :] + nt(dq_own[...], w_qkv[:, query_w])
    base = base.astype(BF)
    qk[...] = nt(qbd[...], w_qkv[:, key_w]).astype(BF)
    dv[...] = nt(dbd[...], w_qkv[:, value_w]).astype(BF)
    y = tn(ds_low[...], qk[...]) + tn(p_low[...], dv[...]) + tn(pick, base)
    hgrad[...] = y.astype(BF)
    save(hgrad, hidden_grad, 17)
    vecs_give = remote(vecs, vecs_o.at[core], fs_sem.at[12], fr_sem.at[12], (enc, sibling))
    vecs_give.start()
    vecs_take = remote(vecs, vecs_o.at[1 - core], fs_sem.at[12], fr_sem.at[12], (enc, sibling))
    save(vecs, vecs_o.at[core], 12)

    def dq_pass(j):
        peer = same_core(j)
        remote(dq_own, dq_place(peer), qs_sem.at[j], qr_sem.at[peer], (enc, peer)).wait_recv()
        send = qs_sem.at[n // 2 - 1 + j]
        remote(dq_place(peer), dq_place(peer), send, qr_sem.at[peer], (enc, sibling)).start()

    loop(n // 2 - 1, dq_pass)

    @pl.when(core == 0)
    def _():
        keys.over()

    sent_pieces(px, recv_v, range(n), vs_sem, vr_sem)
    sent_pieces(dx, recv, key_owners, ks_sem, kr_sem)

    def dq_came(j):
        peer = cousin(j)
        remote(dq_own, dq_place(peer), qs_sem.at[0], qr_sem.at[peer], (enc, sibling)).wait_recv()

    loop(n // 2, dq_came)

    def dq_sent(j):
        remote(dq_own, dq_place(me), qs_sem.at[j], qr_sem.at[me], (enc, sibling)).wait_send()

    loop(n - 1, dq_sent)
    xcls_back.wait_send()

    dmix_over.wait_send()
    for copy in [*given, vecs_take]:
        copy.wait_send()
        copy.wait_recv()
    values.sent()
    values.came()

    @pl.when(core == 0)
    def _():
        keys.sent()
        key_save.wait()

    @pl.when(core == 1)
    def _():
        keys.came()

    for copy in saves:
        copy.wait()


def grad_kernel(
    xcls_i,
    mixed_i,
    normed_i,
    act_i,
    douter_i,
    dinner_i,
    datt_i,
    dq_i,
    kv_i,
    hidden_out_i,
    hidden_grad_i,
    vecs,
    loss,
    hidden_out,
    hidden_grad,
    grad_qkv,
    grad_query_bias,
    grad_value_bias,
    grad_out,
    grad_out_bias,
    grad_first_gain,
    grad_first_shift,
    grad_up,
    grad_up_bias,
    grad_down,
    grad_down_bias,
    grad_second_gain,
    grad_second_shift,
    xcls,
    mixed,
    normed,
    act,
    douter,
    dinner,
    datt,
    dq,
    kv,
    g_qkv,
    g_out,
    g_up,
    g_down,
    h_out,
    h_grad,
    in_sem,
    out_sem,
):
    width = xcls.shape[1]
    ins = {}
    loads = [
        ("mixed", mixed_i, mixed),
        ("datt", datt_i, datt),
        ("act", act_i, act),
        ("douter", douter_i, douter),
        ("normed", normed_i, normed),
        ("dinner", dinner_i, dinner),
        ("xcls", xcls_i, xcls),
        ("dq", dq_i, dq),
        ("kv", kv_i, kv),
        ("h_out", hidden_out_i, h_out),
        ("h_grad", hidden_grad_i, h_grad),
    ]
    for index, (name, source, target) in enumerate(loads):
        ins[name] = pltpu.make_async_copy(source, target, in_sem.at[index])
        ins[name].start()

    def column_sum(value):
        return jnp.sum(value.astype(F32), 0, keepdims=True)

    def vector(row):
        return vecs[0, pl.ds(row, 1), :] + vecs[1, pl.ds(row, 1), :]

    def put(source, target, rows, index):
        pltpu.make_async_copy(source.at[rows], target.at[0, rows], out_sem.at[index]).start()

    loss[...] = vecs[0, pl.ds(4, 1), pl.ds(0, 1)]
    grad_second_gain[...] = vector(0)
    grad_second_shift[...] = vector(1)
    grad_first_gain[...] = vector(2)
    grad_first_shift[...] = vector(3)
    grad_value_bias[...] = vector(5)

    ins["mixed"].wait()
    ins["datt"].wait()
    g_out[...] = tn(mixed[...], datt[...])
    put(g_out, grad_out, pl.ds(0, width), 4)
    ins["act"].wait()
    ins["douter"].wait()
    for j in range(4):
        these = pl.ds(j * width, width)
        g_down[these, :] = tn(act[:, these], douter[...])
        put(g_down, grad_down, these, 2)
    ins["normed"].wait()
    ins["dinner"].wait()
    for j in range(3):
        these = pl.ds(j * 256, 256)
        g_up[these, :] = tn(normed[:, these], dinner[...])
        put(g_up, grad_up, these, 3)
    ins["xcls"].wait()
    ins["dq"].wait()
    ins["kv"].wait()
    for j in range(3):
        these = pl.ds(j * 256, 256)
        g_qkv[these, pl.ds(0, width)] = tn(xcls[:, these], dq[...])
        for m in range(2):
            g_qkv[these, pl.ds((m + 1) * width, width)] = kv[m, :, these].astype(F32).T
        put(g_qkv, grad_qkv, these, 5)
    through = [
        pltpu.make_async_copy(h_out, hidden_out, out_sem.at[0]),
        pltpu.make_async_copy(h_grad, hidden_grad, out_sem.at[1]),
    ]
    for name, copy in zip(("h_out", "h_grad"), through):
        ins[name].wait()
        copy.start()
    grad_down_bias[...] = column_sum(douter[...])
    grad_up_bias[...] = column_sum(dinner[...])
    grad_out_bias[...] = column_sum(datt[...])
    grad_query_bias[...] = column_sum(dq[...])
    pltpu.make_async_copy(g_down, grad_down.at[0], out_sem.at[2]).wait()
    pltpu.make_async_copy(g_up, grad_up.at[0], out_sem.at[3]).wait()
    pltpu.make_async_copy(g_out, grad_out.at[0], out_sem.at[4]).wait()
    pltpu.make_async_copy(g_qkv, grad_qkv.at[0], out_sem.at[5]).wait()
    for copy in through:
        copy.wait()


def fused_on_device(n, *args):
    (
        hidden_in,
        starts,
        positives,
        qkv_weight,
        query_bias,
        value_bias,
        out_weight,
        out_bias,
        first_gain,
        first_shift,
        up_weight,
        up_bias,
        down_weight,
        down_bias,
        second_gain,
        second_shift,
    ) = args
    rows, length, width = hidden_in.shape[1:]
    tokens = rows * length
    ff = up_weight.shape[-1]
    wide = n * PAD
    side = wide // 2
    spreads = H * PAD
    planes = n // 4
    shape = jax.ShapeDtypeStruct
    hbm = pl.BlockSpec(memory_space=pl.ANY)
    vmem = pl.BlockSpec(memory_space=pltpu.VMEM)
    smem = pl.BlockSpec(memory_space=pltpu.SMEM)
    dma = pltpu.SemaphoreType.DMA
    limit = 60 * 1024 * 1024
    outs = pl.pallas_call(
        functools.partial(main_kernel, n),
        out_shape=[
            shape((tokens, width), BF),
            shape((tokens, width), BF),
            shape((wide, width), BF),
            shape((wide, width), BF),
            shape((wide, width), BF),
            shape((wide, ff), BF),
            shape((wide, width), BF),
            shape((wide, ff), BF),
            shape((wide, width), BF),
            shape((wide, width), BF),
            shape((2, 8, width), F32),
            shape((2, width, width), BF),
        ],
        in_specs=[smem, vmem, hbm, hbm, vmem, vmem, hbm, vmem, vmem, vmem, hbm, vmem, hbm, vmem, vmem, vmem],
        out_specs=[hbm] * 12,
        scratch_shapes=[
            pltpu.VMEM((tokens, width), BF),
            pltpu.VMEM((width, 3 * width), BF),
            pltpu.VMEM((width, width), BF),
            pltpu.VMEM((width, ff), BF),
            pltpu.VMEM((ff, width), BF),
            pltpu.VMEM((tokens, 2 * width), BF),
            pltpu.VMEM((tokens, width), BF),
            pltpu.VMEM((tokens, width), BF),
            pltpu.VMEM((length, length), F32),
            pltpu.VMEM((spreads, width), BF),
            pltpu.VMEM((spreads, width), BF),
            pltpu.VMEM((spreads, width), BF),
            pltpu.VMEM((spreads, width), BF),
            pltpu.VMEM((spreads, tokens), F32),
            pltpu.VMEM((spreads, tokens), BF),
            pltpu.VMEM((spreads, tokens), BF),
            pltpu.VMEM((spreads, width), BF),
            pltpu.VMEM((spreads, width), BF),
            pltpu.VMEM((2, side, width), BF),
            pltpu.VMEM((side, width), BF),
            pltpu.VMEM((2, 2, side, width), BF),
            pltpu.VMEM((side, width), F32),
            pltpu.VMEM((side, 128), F32),
            pltpu.VMEM((side, width), F32),
            pltpu.VMEM((side, 128), F32),
            pltpu.VMEM((side, width), BF),
            pltpu.VMEM((side, ff), BF),
            pltpu.VMEM((side, ff), F32),
            pltpu.VMEM((side, ff), BF),
            pltpu.VMEM((side, width), BF),
            pltpu.VMEM((side, width), BF),
            pltpu.VMEM((2, side, width), BF),
            pltpu.VMEM((side, width), F32),
            pltpu.VMEM((side, width), F32),
            pltpu.VMEM((side, width), F32),
            pltpu.VMEM((8, width), F32),
            pltpu.VMEM((width, wide), BF),
            pltpu.VMEM((n, H // 4 * PAD, width // 2), BF),
            pltpu.VMEM((width // 4, width // 2), BF),
            pltpu.VMEM((width, wide), BF),
            pltpu.VMEM((n, H // 4 * PAD, width // 2), BF),
            pltpu.VMEM((width // 4, width // 2), BF),
            pltpu.VMEM((PAD, width), BF),
            pltpu.VMEM((length, width), BF),
            pltpu.VMEM((length, width), F32),
            pltpu.VMEM((tokens, width), BF),
            pltpu.VMEM((tokens, width), BF),
            dma((7,)),
            dma((18,)),
            dma((n // 2,)),
            dma((n,)),
            dma((n // 2,)),
            dma((n,)),
            dma((n // 2,)),
            dma((n,)),
            dma((3,)),
            dma((3,)),
            dma((n - 1,)),
            dma((n,)),
            dma((n,)),
            dma((n,)),
            dma((n,)),
            dma((n,)),
            dma((n,)),
            dma((n,)),
            dma((13,)),
            dma((13,)),
        ],
        compiler_params=pltpu.CompilerParams(
            collective_id=0, has_side_effects=True, vmem_limit_bytes=limit
        ),
        name="layer",
    )(
        jnp.transpose(starts, (1, 0, 2)),
        positives,
        hidden_in.reshape(tokens, width),
        qkv_weight.reshape(width, 3 * width),
        query_bias,
        value_bias,
        out_weight.reshape(width, width),
        out_bias,
        first_gain,
        first_shift,
        up_weight.reshape(width, ff),
        up_bias,
        down_weight.reshape(ff, width),
        down_bias,
        second_gain,
        second_shift,
    )
    h_out, h_grad, xcls, mixed, normed, act, douter, dinner, datt, dq, vecs, kv = outs
    row = shape((1, width), F32)
    grads = pl.pallas_call(
        grad_kernel,
        out_shape=[
            shape((1, 1), F32),
            shape((tokens, width), BF),
            shape((tokens, width), BF),
            shape((1, width, 3 * width), F32),
            row,
            row,
            shape((1, width, width), F32),
            row,
            row,
            row,
            shape((1, width, ff), F32),
            shape((1, ff), F32),
            shape((1, ff, width), F32),
            row,
            row,
            row,
        ],
        in_specs=[hbm] * 11 + [vmem],
        out_specs=[vmem, hbm, hbm, hbm, vmem, vmem, hbm, vmem, vmem, vmem, hbm, vmem, hbm, vmem, vmem, vmem],
        scratch_shapes=[
            pltpu.VMEM((wide, width), BF),
            pltpu.VMEM((wide, width), BF),
            pltpu.VMEM((wide, width), BF),
            pltpu.VMEM((wide, ff), BF),
            pltpu.VMEM((wide, width), BF),
            pltpu.VMEM((wide, ff), BF),
            pltpu.VMEM((wide, width), BF),
            pltpu.VMEM((wide, width), BF),
            pltpu.VMEM((2, width, width), BF),
            pltpu.VMEM((width, 3 * width), F32),
            pltpu.VMEM((width, width), F32),
            pltpu.VMEM((width, ff), F32),
            pltpu.VMEM((ff, width), F32),
            pltpu.VMEM((tokens, width), BF),
            pltpu.VMEM((tokens, width), BF),
            dma((11,)),
            dma((6,)),
        ],
        compiler_params=pltpu.CompilerParams(vmem_limit_bytes=limit),
        name="gradients",
    )(xcls, mixed, normed, act, douter, dinner, datt, dq, kv, h_out, h_grad, vecs)
    place = (1, rows, length, width)
    return (
        grads[0].reshape(()),
        grads[1].reshape(place),
        grads[2].reshape(place),
        *grads[3:],
    )


def solution(mesh):
    placed = (
        P("enc", "dp", None, None),
        P("enc", "dp", None),
        P(),
        P("enc", None, None),
        P("enc", None),
        P("enc", None),
        P("enc", None, None),
        P("enc", None),
        P("enc", None),
        P("enc", None),
        P("enc", None, None),
        P("enc", None),
        P("enc", None, None),
        P("enc", None),
        P("enc", None),
        P("enc", None),
    )
    n = mesh.shape["dp"]
    body = functools.partial(fused_on_device, n) if n == OWNERS else on_device
    return jax.shard_map(
        body,
        mesh=mesh,
        in_specs=placed,
        out_specs=(
            P(),
            P("enc", "dp", None, None),
            P("enc", "dp", None, None),
            P("enc", None, None),
            P("enc", None),
            P("enc", None),
            P("enc", None, None),
            P("enc", None),
            P("enc", None),
            P("enc", None),
            P("enc", None, None),
            P("enc", None),
            P("enc", None, None),
            P("enc", None),
            P("enc", None),
            P("enc", None),
        ),
        check_vma=False,
    )
```

```python
import functools

import jax
import jax.numpy as jnp
from jax import lax
from jax.experimental import pallas as pl
from jax.experimental.pallas import tpu as pltpu
from jax.sharding import PartitionSpec as P

OWNERS = 16
H = 12
DOCS = 4


EPS_NORM = 1e-12


def partner(value, axis, distance):
    mask = 2**distance
    pairs = [(source, source ^ mask) for source in range(lax.axis_size(axis))]
    return lax.ppermute(value, axis, pairs)


def product(left, right):
    return jnp.dot(left, right, preferred_element_type=jnp.float32)


def layer_stats(hidden):
    centred = hidden - jnp.mean(hidden, -1, keepdims=True)
    inverse = lax.rsqrt(jnp.mean(centred * centred, -1, keepdims=True) + EPS_NORM)
    return (centred * inverse, inverse)


def norm_back(upstream, normal, inverse, gain):
    scaled = upstream * gain
    return inverse * (
        scaled
        - jnp.mean(scaled, -1, keepdims=True)
        - normal * jnp.mean(scaled * normal, -1, keepdims=True)
    )


def on_device(
    hidden_in,
    starts,
    positives,
    qkv_weight,
    query_bias,
    value_bias,
    out_weight,
    out_bias,
    first_gain,
    first_shift,
    up_weight,
    up_bias,
    down_weight,
    down_bias,
    second_gain,
    second_shift,
):
    rows, length, width = (hidden_in.shape[1], hidden_in.shape[2], hidden_in.shape[3])
    heads = H
    head_size = width // heads
    tokens = rows * length
    flat = hidden_in.reshape(tokens, width)
    w_qkv = qkv_weight[0]
    w_out = out_weight[0]
    w_up = up_weight[0]
    w_down = down_weight[0]
    row_starts = starts[0]
    qkv_shift = jnp.concatenate([query_bias[0], jnp.zeros_like(query_bias[0]), value_bias[0]])
    qkv = (product(flat, w_qkv) + qkv_shift).astype(jnp.bfloat16)
    split = qkv.reshape(rows, length, 3, heads, head_size)
    query, key, value = (split[:, :, 0], split[:, :, 1], split[:, :, 2])
    places = jnp.arange(length, dtype=jnp.int32)
    segment = jnp.sum((places[None, :, None] >= row_starts[:, None, :]).astype(jnp.int32), -1)
    allowed = (segment[:, :, None] == segment[:, None, :])[:, None]
    head_scale = head_size ** (-0.5)

    def attention_scores(left, right):
        raw = jnp.einsum("rqhe,rkhe->rhqk", left, right, preferred_element_type=jnp.float32)
        return jnp.where(allowed, head_scale * raw, -1e30)

    scores = attention_scores(query, key)
    peak = jnp.max(scores, -1, keepdims=True)
    log_total = peak + jnp.log(jnp.sum(jnp.exp(scores - peak), -1, keepdims=True))
    weights_low = jnp.exp(scores - log_total).astype(jnp.bfloat16)
    mixed = jnp.einsum("rhqk,rkhe->rqhe", weights_low, value, preferred_element_type=jnp.float32)
    mixed = mixed.astype(jnp.bfloat16).reshape(tokens, width)
    attended = product(mixed, w_out) + out_bias[0]
    first_normal, first_inverse = layer_stats(flat.astype(jnp.float32) + attended)
    normed = first_normal * first_gain[0] + first_shift[0]
    normed_low = normed.astype(jnp.bfloat16)
    inner = product(normed_low, w_up) + up_bias[0]
    activated_low = jax.nn.gelu(inner, approximate=False).astype(jnp.bfloat16)
    outer = product(activated_low, w_down) + down_bias[0]
    second_normal, second_inverse = layer_stats(normed + outer)
    encoded = second_normal * second_gain[0] + second_shift[0]
    hidden_out = encoded.astype(jnp.bfloat16).reshape(1, rows, length, width)
    picker = (places[None, None, :] == row_starts[:, :, None]).astype(jnp.float32)
    cls = jnp.einsum(
        "rdl,rlw->rdw",
        picker,
        encoded.reshape(rows, length, width),
        precision=lax.Precision.HIGHEST,
    )
    local_count = rows * DOCS
    cls_low = cls.reshape(local_count, width).astype(jnp.bfloat16)
    first_half = lax.axis_index("enc") == 0
    mine = lax.all_gather(cls_low, "dp", axis=0, tiled=True)
    other = partner(mine, "enc", 0)
    questions = jnp.where(first_half, mine, other)
    passages = jnp.where(first_half, other, mine)
    count = questions.shape[0]
    sim_scale = width ** (-0.5)
    sims = sim_scale * jnp.einsum(
        "qw,pw->qp", questions, passages, preferred_element_type=jnp.float32
    )
    sim_peak = jnp.max(sims, -1, keepdims=True)
    sim_total = sim_peak + jnp.log(jnp.sum(jnp.exp(sims - sim_peak), -1, keepdims=True))
    target = (jnp.arange(count, dtype=jnp.int32)[None, :] == positives[:, None]).astype(jnp.float32)
    total = jnp.sum(sim_total[:, 0] - jnp.sum(sims * target, -1)) / local_count
    loss_mean = total / lax.axis_size("dp")
    d_sims_low = (sim_scale * (jnp.exp(sims - sim_total) - target) / local_count).astype(
        jnp.bfloat16
    )
    own_start = lax.axis_index("dp") * local_count
    own_rows = lax.dynamic_slice_in_dim(d_sims_low, own_start, local_count, 0)
    own_columns = lax.dynamic_slice_in_dim(d_sims_low, own_start, local_count, 1)
    d_questions = jnp.einsum("qp,pw->qw", own_rows, passages, preferred_element_type=jnp.float32)
    d_passages = jnp.einsum("qp,qw->pw", own_columns, questions, preferred_element_type=jnp.float32)
    d_cls = jnp.where(first_half, d_questions, d_passages).reshape(rows, DOCS, width)
    d_encoded = jnp.einsum("rdl,rdw->rlw", picker, d_cls, precision=lax.Precision.HIGHEST).reshape(
        tokens, width
    )
    grad_second_gain = jnp.sum(d_encoded * second_normal, 0)
    grad_second_shift = jnp.sum(d_encoded, 0)
    d_second = norm_back(d_encoded, second_normal, second_inverse, second_gain[0])
    d_outer_low = d_second.astype(jnp.bfloat16)
    grad_down_bias = jnp.sum(d_outer_low.astype(jnp.float32), 0)
    grad_down_weight = jnp.einsum(
        "tf,tw->fw", activated_low, d_outer_low, preferred_element_type=jnp.float32
    )
    d_activated = jnp.einsum("tw,fw->tf", d_outer_low, w_down, preferred_element_type=jnp.float32)
    normal_cdf = 0.5 * (1.0 + lax.erf(inner * 0.7071067811865476))
    slope = normal_cdf + inner * jnp.exp(-0.5 * inner * inner) * 0.3989422804014327
    d_inner_low = (d_activated * slope).astype(jnp.bfloat16)
    grad_up_bias = jnp.sum(d_inner_low.astype(jnp.float32), 0)
    grad_up_weight = jnp.einsum(
        "tw,tf->wf", normed_low, d_inner_low, preferred_element_type=jnp.float32
    )
    d_normed = d_second + jnp.einsum(
        "tf,wf->tw", d_inner_low, w_up, preferred_element_type=jnp.float32
    )
    grad_first_gain = jnp.sum(d_normed * first_normal, 0)
    grad_first_shift = jnp.sum(d_normed, 0)
    d_first = norm_back(d_normed, first_normal, first_inverse, first_gain[0])
    d_attended_low = d_first.astype(jnp.bfloat16)
    grad_out_bias = jnp.sum(d_attended_low.astype(jnp.float32), 0)
    grad_out_weight = jnp.einsum(
        "tv,tw->vw", mixed, d_attended_low, preferred_element_type=jnp.float32
    )
    d_mixed_low = jnp.einsum(
        "tw,vw->tv", d_attended_low, w_out, preferred_element_type=jnp.float32
    ).astype(jnp.bfloat16)
    d_mixed_heads = d_mixed_low.reshape(rows, length, heads, head_size)
    probs_again = jnp.exp(attention_scores(query, key) - log_total)
    weights_again = probs_again.astype(jnp.bfloat16)
    grad_value = jnp.einsum(
        "rhqk,rqhe->rkhe", weights_again, d_mixed_heads, preferred_element_type=jnp.float32
    )
    d_weights = jnp.einsum(
        "rqhe,rkhe->rhqk", d_mixed_heads, value, preferred_element_type=jnp.float32
    )
    d_scores = probs_again * (d_weights - jnp.sum(d_weights * probs_again, -1, keepdims=True))
    d_raw_low = (head_scale * d_scores).astype(jnp.bfloat16)
    grad_query = jnp.einsum("rhqk,rkhe->rqhe", d_raw_low, key, preferred_element_type=jnp.float32)
    grad_key = jnp.einsum("rhqk,rqhe->rkhe", d_raw_low, query, preferred_element_type=jnp.float32)
    d_qkv_low = (
        jnp.stack([grad_query, grad_key, grad_value], 2)
        .reshape(tokens, 3 * width)
        .astype(jnp.bfloat16)
    )
    grad_qkv_local = jnp.einsum("tw,tv->wv", flat, d_qkv_low, preferred_element_type=jnp.float32)
    bias_sums = jnp.sum(d_qkv_low.astype(jnp.float32), 0)
    grad_query_local = bias_sums[:width]
    grad_value_local = bias_sums[2 * width :]
    d_input = d_first + jnp.einsum(
        "tv,wv->tw", d_qkv_low, w_qkv, preferred_element_type=jnp.float32
    )
    hidden_grad = d_input.astype(jnp.bfloat16).reshape(1, rows, length, width)
    (
        share_qkv,
        share_query_bias,
        share_value_bias,
        share_out_weight,
        share_out_bias,
        share_first_gain,
        share_first_shift,
        share_up_weight,
        share_up_bias,
        share_down_weight,
        share_down_bias,
        share_second_gain,
        share_second_shift,
    ) = (
        lax.psum_scatter(grad_qkv_local[None], "dp", scatter_dimension=1, tiled=True),
        lax.psum_scatter(grad_query_local[None], "dp", scatter_dimension=1, tiled=True),
        lax.psum_scatter(grad_value_local[None], "dp", scatter_dimension=1, tiled=True),
        lax.psum_scatter(grad_out_weight[None], "dp", scatter_dimension=1, tiled=True),
        lax.psum_scatter(grad_out_bias[None], "dp", scatter_dimension=1, tiled=True),
        lax.psum_scatter(grad_first_gain[None], "dp", scatter_dimension=1, tiled=True),
        lax.psum_scatter(grad_first_shift[None], "dp", scatter_dimension=1, tiled=True),
        lax.psum_scatter(grad_up_weight[None], "dp", scatter_dimension=1, tiled=True),
        lax.psum_scatter(grad_up_bias[None], "dp", scatter_dimension=1, tiled=True),
        lax.psum_scatter(grad_down_weight[None], "dp", scatter_dimension=1, tiled=True),
        lax.psum_scatter(grad_down_bias[None], "dp", scatter_dimension=1, tiled=True),
        lax.psum_scatter(grad_second_gain[None], "dp", scatter_dimension=1, tiled=True),
        lax.psum_scatter(grad_second_shift[None], "dp", scatter_dimension=1, tiled=True),
    )
    summed = (
        lax.all_gather(share_qkv.astype(jnp.bfloat16), "dp", axis=1, tiled=True).astype(
            share_qkv.dtype
        ),
        lax.all_gather(share_query_bias.astype(jnp.bfloat16), "dp", axis=1, tiled=True).astype(
            share_query_bias.dtype
        ),
        lax.all_gather(share_value_bias.astype(jnp.bfloat16), "dp", axis=1, tiled=True).astype(
            share_value_bias.dtype
        ),
        lax.all_gather(share_out_weight.astype(jnp.bfloat16), "dp", axis=1, tiled=True).astype(
            share_out_weight.dtype
        ),
        lax.all_gather(share_out_bias.astype(jnp.bfloat16), "dp", axis=1, tiled=True).astype(
            share_out_bias.dtype
        ),
        lax.all_gather(share_first_gain.astype(jnp.bfloat16), "dp", axis=1, tiled=True).astype(
            share_first_gain.dtype
        ),
        lax.all_gather(share_first_shift.astype(jnp.bfloat16), "dp", axis=1, tiled=True).astype(
            share_first_shift.dtype
        ),
        lax.all_gather(share_up_weight.astype(jnp.bfloat16), "dp", axis=1, tiled=True).astype(
            share_up_weight.dtype
        ),
        lax.all_gather(share_up_bias.astype(jnp.bfloat16), "dp", axis=1, tiled=True).astype(
            share_up_bias.dtype
        ),
        lax.all_gather(share_down_weight.astype(jnp.bfloat16), "dp", axis=1, tiled=True).astype(
            share_down_weight.dtype
        ),
        lax.all_gather(share_down_bias.astype(jnp.bfloat16), "dp", axis=1, tiled=True).astype(
            share_down_bias.dtype
        ),
        lax.all_gather(share_second_gain.astype(jnp.bfloat16), "dp", axis=1, tiled=True).astype(
            share_second_gain.dtype
        ),
        lax.all_gather(share_second_shift.astype(jnp.bfloat16), "dp", axis=1, tiled=True).astype(
            share_second_shift.dtype
        ),
    )
    return (
        loss_mean,
        hidden_out,
        hidden_grad,
        summed[0],
        summed[1],
        summed[2],
        summed[3],
        summed[4],
        summed[5],
        summed[6],
        summed[7],
        summed[8],
        summed[9],
        summed[10],
        summed[11],
        summed[12],
    )


PAD = 16
BF = jnp.bfloat16
F32 = jnp.float32
MESH = pl.DeviceIdType.MESH
NEG = -1e30
ROOT_HALF = 0.7071067811865476
PEAK = 0.3989422804014327


def nn(left, right):
    return jnp.dot(left, right, preferred_element_type=F32)


def nt(left, right):
    return lax.dot_general(left, right, (((1,), (1,)), ((), ())), preferred_element_type=F32)


def tn(left, right):
    return lax.dot_general(left, right, (((0,), (0,)), ((), ())), preferred_element_type=F32)


def iota(shape, dim):
    return lax.broadcasted_iota(jnp.int32, shape, dim)


def gelu_parts(inner):
    cdf = 0.5 * (1.0 + lax.erf(inner * ROOT_HALF))
    return cdf, jnp.exp(-0.5 * inner * inner) * PEAK


def chunk(index, size):
    return pl.ds(pl.multiple_of(index * size, size), size)


def loop(count, body):
    def step(index, carry):
        body(index)
        return carry

    lax.fori_loop(0, count, step, 0)


def main_kernel(
    n,
    starts,
    positives,
    x_hbm,
    qkv_hbm,
    q_bias,
    v_bias,
    out_hbm,
    o_bias,
    gain1,
    shift1,
    up_hbm,
    u_bias,
    down_hbm,
    d_bias,
    gain2,
    shift2,
    hidden_out,
    hidden_grad,
    xcls_o,
    mixed_o,
    normed_o,
    act_o,
    douter_o,
    dinner_o,
    datt_o,
    dq_o,
    vecs_o,
    kv_o,
    x,
    w_qkv,
    w_out,
    w_up,
    w_down,
    out_turned,
    up_turned,
    down_turned,
    v_turned,
    kv,
    q,
    mix,
    seg_bias,
    qbd,
    dbd,
    qk,
    dv,
    probs,
    p_low,
    ds_low,
    px,
    dx,
    xcls,
    mixed,
    cls,
    norm1,
    inv1,
    norm2,
    inv2,
    normed,
    act,
    slope,
    dinner,
    douter,
    datt,
    dmix,
    d_cls,
    dfirst,
    acc,
    vecs,
    turned,
    recv,
    piece,
    turned_v,
    recv_v,
    piece_v,
    dq_own,
    low_t,
    acc_t,
    hout,
    hgrad,
    load_sem,
    save_sem,
    xs_sem,
    xr_sem,
    ms_sem,
    mr_sem,
    ks_sem,
    kr_sem,
    cs_sem,
    cr_sem,
    qs_sem,
    qr_sem,
    vs_sem,
    vr_sem,
    gs_sem,
    gr_sem,
    hs_sem,
    hr_sem,
    fs_sem,
    fr_sem,
):
    enc = lax.axis_index("enc")
    me = lax.axis_index("dp")
    other = 1 - enc
    core = lax.rem(me, 2)
    which = lax.div(me, 2)
    sibling = me + 1 - 2 * core
    across = me + 2 - 4 * lax.rem(which, 2)
    tokens, width = x.shape
    ff = w_up.shape[1]
    side = n // 2 * PAD
    rows = starts.shape[0]
    length = tokens // rows
    local = rows * DOCS
    head = width // H
    pairs = H // 2
    head_scale = head ** (-0.5)
    group_cols = width // 4
    half_feats = width // 2
    group_rows = H // 4 * PAD
    query_w = pl.ds(0, width)
    key_w = pl.ds(width, width)
    value_w = pl.ds(2 * width, width)

    def weight_load(cols, index):
        return pltpu.make_async_copy(qkv_hbm.at[:, cols], w_qkv.at[:, cols], load_sem.at[index])

    loads = [
        pltpu.make_async_copy(x_hbm, x, load_sem.at[0]),
        weight_load(key_w, 1),
        weight_load(query_w, 2),
        weight_load(value_w, 3),
        pltpu.make_async_copy(out_hbm, w_out, load_sem.at[4]),
        pltpu.make_async_copy(up_hbm, w_up, load_sem.at[5]),
        pltpu.make_async_copy(down_hbm, w_down, load_sem.at[6]),
    ]
    for copy in loads:
        copy.start()

    barrier = pltpu.get_barrier_semaphore()

    def greet(j):
        peer = lax.rem(me + j + 1, n)
        pl.semaphore_signal(barrier, inc=1, device_id=(enc, peer), device_id_type=MESH)

    loop(n - 1, greet)
    pl.semaphore_signal(barrier, inc=1, device_id=(other, me), device_id_type=MESH)

    def remote(source, target, send, receive, device):
        return pltpu.make_async_remote_copy(
            src_ref=source,
            dst_ref=target,
            send_sem=send,
            recv_sem=receive,
            device_id=device,
            device_id_type=MESH,
        )

    def same_core(j):
        return lax.rem(me + 2 * j + 2, n)

    def cousin(j):
        return lax.rem(same_core(j) + 1 - 2 * core + n, n)

    def block(index):
        return pl.ds(pl.multiple_of(index * PAD, PAD), PAD)

    own = block(which)

    def share(source, place, send, receive):
        def go(j):
            remote(source, place(me), send.at[j], receive.at[me], (enc, same_core(j))).start()

        loop(n // 2 - 1, go)

    def shared(source, place, send, receive):
        def came(j):
            peer = same_core(j)
            copy = remote(source, place(peer), send.at[j], receive.at[peer], (enc, peer))
            copy.wait_send()
            copy.wait_recv()

        loop(n // 2 - 1, came)

    class Relay:
        def __init__(self, source, place, send, receive, group):
            self.source, self.place, self.send, self.receive = source, place, send, receive
            self.base = me - lax.rem(me, group)
            self.group = group
            self.ups = group // 4 - 1

        def up(self, device, j):
            return self.base + lax.rem(device - self.base + 4 * j, self.group)

        def copy(self, slot, source, owner, device):
            return remote(
                source, self.place(owner), self.send.at[slot], self.receive.at[owner], (enc, device)
            )

        def start(self):
            for j in range(self.ups):
                self.copy(j, self.source, me, self.up(me, j + 1)).start()
            self.copy(self.ups, self.source, me, across).start()
            self.copy(self.ups + 1, self.source, me, sibling).start()

        def plane(self):
            for j in range(self.ups):
                peer = self.up(me, j + 1)
                self.copy(0, self.place(peer), peer, peer).wait_recv()
                self.copy(self.ups + 2 + 2 * j, self.place(peer), peer, across).start()
                self.copy(self.ups + 3 + 2 * j, self.place(peer), peer, sibling).start()

        def over(self):
            for j in range(self.ups + 1):
                peer = self.up(across, j)
                self.copy(0, self.place(peer), peer, across).wait_recv()
                self.copy(3 * self.ups + 2 + j, self.place(peer), peer, sibling).start()

        def sent(self):
            def wait(j):
                self.copy(j, self.source, me, sibling).wait_send()

            loop(4 * self.ups + 3, wait)

        def came(self):
            for j in range(self.ups + 1):
                for peer in (self.up(sibling, j), self.up(across + sibling - me, j)):
                    self.copy(0, self.place(peer), peer, sibling).wait_recv()

    saves = []

    def save(source, target, index):
        copy = pltpu.make_async_copy(source, target, save_sem.at[index])
        copy.start()
        saves.append(copy)

    halves = [pl.ds(pl.multiple_of(core * side, side), side)]
    halves.append(pl.ds(pl.multiple_of((1 - core) * side, side), side))
    given = []

    def give(source, target, index):
        save(source, target.at[halves[0]], index)
        copy = remote(source, target.at[halves[0]], fs_sem.at[index], fr_sem.at[index], (enc, sibling))
        copy.start()
        given.append(
            remote(source, target.at[halves[1]], fs_sem.at[index], fr_sem.at[index], (enc, sibling))
        )

    first_col = jnp.full((PAD, 1), -1, jnp.int32)
    seg_col = jnp.full((PAD, 1), -1, jnp.int32)
    place_col = iota((PAD, 1), 0)
    segs = []
    for r in range(rows):
        place = iota((1, length), 1)
        count = jnp.zeros((1, length), jnp.int32)
        for k in range(DOCS):
            start = starts[r, 0, k]
            count = count + (place >= start).astype(jnp.int32)
            order = jnp.int32(0)
            for m in range(DOCS):
                order = order + jnp.where(starts[r, 0, m] <= start, 1, 0)
            here = place_col == r * DOCS + k
            first_col = jnp.where(here, r * length + start, first_col)
            seg_col = jnp.where(here, r * 8 + order, seg_col)
        segs.append(count + r * 8)
    seg_row = jnp.concatenate(segs, axis=1)
    pick = (iota((PAD, tokens), 1) == first_col).astype(F32).astype(BF)
    allowed = seg_row == seg_col

    low_half = iota((1, 128), 1) < head

    def block_diagonal(target, block_rows):
        for p in range(pairs):
            part = block_rows[:, p * 128 : (p + 1) * 128]
            even = jnp.where(low_half, part, 0.0).astype(BF)
            odd = jnp.where(low_half, 0.0, part).astype(BF)
            target[pl.ds(2 * p * PAD, PAD), pl.ds(p * 128, 128)] = even
            target[pl.ds((2 * p + 1) * PAD, PAD), pl.ds(p * 128, 128)] = odd

    def own_lanes(full):
        parts = []
        for p in range(pairs):
            lanes = slice(p * 128, (p + 1) * 128)
            even = full[2 * p * PAD : (2 * p + 1) * PAD, lanes]
            odd = full[(2 * p + 1) * PAD : (2 * p + 2) * PAD, lanes]
            parts.append(jnp.where(low_half, even, odd))
        return jnp.concatenate(parts, axis=1)

    qbd[...] = jnp.zeros_like(qbd)
    dbd[...] = jnp.zeros_like(dbd)
    loads[0].wait()
    xcls[core, own, :] = nn(pick, x[...]).astype(BF)
    pl.semaphore_wait(barrier, n)

    def xcls_place(peer):
        return xcls.at[core, block(lax.div(peer, 2))]

    share(xcls.at[core, own], xcls_place, xs_sem, xr_sem)

    loads[1].wait()
    kv[:, pl.ds(0, width)] = nn(x[...], w_qkv[:, key_w]).astype(BF)
    loads[2].wait()
    q_own = (nn(xcls[core, own, :], w_qkv[:, query_w]) + q_bias[...]).astype(BF).astype(F32)
    block_diagonal(qbd, q_own)
    loads[3].wait()
    kv[:, pl.ds(width, width)] = (nn(x[...], w_qkv[:, value_w]) + v_bias[...]).astype(BF)
    allowed_all = jnp.concatenate([allowed] * H, axis=0)
    scores = jnp.where(allowed_all, head_scale * nt(qbd[...], kv[:, pl.ds(0, width)]), NEG)
    peak = jnp.max(scores, -1, keepdims=True)
    raw = jnp.where(allowed_all, jnp.exp(scores - peak), 0.0)
    total = jnp.sum(raw, -1, keepdims=True)
    weights = raw / jnp.where(total > 0.0, total, 1.0)
    probs[...] = weights
    p_low[...] = weights.astype(BF)
    mixed[own, :] = own_lanes(nn(p_low[...], kv[:, pl.ds(width, width)])).astype(BF)

    def mixed_place(peer):
        return mixed.at[block(lax.div(peer, 2))]

    share(mixed.at[own], mixed_place, ms_sem, mr_sem)

    half_n = n // 2

    def slot_of(peer):
        return lax.rem(peer, 2) * half_n + lax.div(peer, 2)

    def send_pieces(source, into, owners, send, receive):
        for j, owner in enumerate(owners):
            i = j % half_n
            part = source.at[
                pl.ds((i % 4) * group_rows, group_rows), pl.ds((i // 4) * half_feats, half_feats)
            ]

            @pl.when(me != owner)
            def _():
                remote(part, into.at[slot_of(me)], send.at[j], receive.at[me], (enc, owner)).start()

            @pl.when(me == owner)
            def _():
                into[slot_of(me)] = part[...]

    def sent_pieces(source, into, owners, send, receive):
        part = source.at[pl.ds(0, group_rows), pl.ds(0, half_feats)]
        for j, owner in enumerate(owners):

            @pl.when(me != owner)
            def _():
                remote(
                    part, into.at[slot_of(me)], send.at[j], receive.at[me], (enc, owner)
                ).wait_send()

    def pieces_came(into, receive):
        def came(j):
            peer = lax.rem(me + j + 1, n)
            place = into.at[slot_of(peer)]
            remote(place, place, ks_sem.at[0], receive.at[peer], (enc, peer)).wait_recv()

        loop(n - 1, came)

    key_owners = range(0, n, 2)
    px[...] = nn(p_low[...], x[...]).astype(BF)
    v_turned[...] = kv[:, pl.ds(width, width)].T
    y = nn(x[...], w_qkv[:, query_w]) + q_bias[...]
    q[...] = (y.astype(BF).astype(F32) * head_scale).astype(BF)
    loads[5].wait()
    up_turned[...] = w_up[...].T
    def attend_row(r):
        place0 = iota((length, 1), 0)
        place1 = iota((1, length), 1)
        count0 = jnp.zeros((length, 1), jnp.int32)
        count1 = jnp.zeros((1, length), jnp.int32)
        for k in range(DOCS):
            start = starts[r, 0, k]
            count0 = count0 + (place0 >= start).astype(jnp.int32)
            count1 = count1 + (place1 >= start).astype(jnp.int32)
        seg_bias[...] = jnp.where(count0 == count1, 0.0, NEG)
        these = pl.ds(r * length, length)
        mask_even = jnp.where(low_half, 1.0, 0.0).astype(BF)
        mask_odd = jnp.where(low_half, 0.0, 1.0).astype(BF)

        for p in range(pairs):
            lanes = pl.ds(p * 128, 128)
            query = q[these, lanes]
            key = kv[these, lanes]
            value = kv[these, pl.ds(width + p * 128, 128)]
            ext = jnp.concatenate([value, jnp.ones_like(value)], axis=1)
            outs = []
            for mask in (mask_even, mask_odd):
                s = nt(query * mask, key) + seg_bias[...]
                e = jnp.exp(s - jnp.max(s, -1, keepdims=True)).astype(BF)
                outs.append(nn(e, ext))
            even, odd = outs
            top = jnp.where(low_half, even[:, :128], odd[:, :128])
            low = jnp.where(low_half, even[:, 128:], odd[:, 128:])
            mix[these, lanes] = (top / low).astype(BF)

    attend_row(0)

    shared(xcls.at[core, own], xcls_place, xs_sem, xr_sem)
    xcls_over = remote(xcls.at[core], xcls.at[core], fs_sem.at[10], fr_sem.at[10], (enc, sibling))
    xcls_over.start()
    xcls_back = remote(xcls.at[core], xcls.at[1 - core], fs_sem.at[10], fr_sem.at[10], (enc, sibling))
    shared(mixed.at[own], mixed_place, ms_sem, mr_sem)
    send_pieces(px, recv_v, range(n), vs_sem, vr_sem)
    loads[4].wait()

    acc[...] = nn(mixed[...], w_out[...]) + o_bias[...] + xcls[core].astype(F32)

    def stats(h):
        centred = h - jnp.mean(h, -1, keepdims=True)
        inverse = lax.rsqrt(jnp.mean(centred * centred, -1, keepdims=True) + EPS_NORM)
        return centred * inverse, inverse

    unit, inverse = stats(acc[...])
    norm1[...] = unit
    inv1[...] = jnp.broadcast_to(inverse, inv1.shape)
    level = unit * gain1[...] + shift1[...]
    normed[...] = level.astype(BF)
    loads[6].wait()
    inner = nn(normed[...], w_up[...]) + u_bias[...]
    cdf, pdf = gelu_parts(inner)
    slope[...] = cdf + inner * pdf
    act[...] = (inner * cdf).astype(BF)
    unit, inverse = stats(level + d_bias[...] + nn(act[...], w_down[...]))
    norm2[...] = unit
    inv2[...] = jnp.broadcast_to(inverse, inv2.shape)
    cls[enc, core] = (unit * gain2[...] + shift2[...]).astype(BF)

    def cls_copy(half_of, to_core, index, device):
        return remote(
            cls.at[half_of, core], cls.at[half_of, to_core], cs_sem.at[index], cr_sem.at[index], device
        )

    cls_copy(enc, core, 0, (other, me)).start()
    cls_copy(enc, core, 1, (enc, sibling)).start()
    give(mixed, mixed_o, 1)
    give(normed, normed_o, 2)
    give(act, act_o, 3)

    def padded(question):
        device = lax.div(question, local)
        place = lax.rem(device, 2) * side + lax.div(device, 2) * PAD
        return place + question - device * local

    count = n * local
    spot = padded(iota((count, 1), 0)) == iota((count, 2 * side), 1)
    goal = padded(positives[...].reshape(1, count)) + 1
    pos_row = nn(goal.astype(F32).astype(BF), spot.astype(F32).astype(BF)).astype(jnp.int32) - 1

    down_turned[...] = w_down[...].T
    out_turned[...] = w_out[...].T
    attend_row(1)

    xcls_back.wait_recv()

    @pl.when(core == 0)
    def _():
        for c in range(2):
            y = (nn(xcls[c], w_qkv[:, query_w]) + q_bias[...]).astype(BF).astype(F32)
            turned[:, pl.ds(c * side, side)] = y.T.astype(BF)

    save(xcls.at[0], xcls_o.at[pl.ds(0, side)], 4)
    save(xcls.at[1], xcls_o.at[pl.ds(side, side)], 5)

    cls_copy(enc, core, 0, (other, me)).wait_send()
    cls_in = remote(cls.at[enc, core], cls.at[other, core], cs_sem.at[0], cr_sem.at[0], (other, me))
    cls_in.wait_recv()
    cls_pass = cls_copy(other, core, 2, (enc, sibling))
    cls_pass.start()
    cls_copy(enc, core, 1, (enc, sibling)).wait_send()
    remote(
        cls.at[enc, core], cls.at[enc, 1 - core], cs_sem.at[1], cr_sem.at[1], (enc, sibling)
    ).wait_recv()
    cls_pass.wait_send()
    remote(
        cls.at[other, core], cls.at[other, 1 - core], cs_sem.at[2], cr_sem.at[2], (enc, sibling)
    ).wait_recv()

    sim_scale = width ** (-0.5)
    good_col = lax.rem(iota((2 * side, 1), 0), PAD) < local
    good_row = lax.rem(iota((1, 2 * side), 1), PAD) < local
    questions = cls[0].reshape(2 * side, width)
    passages = cls[1].reshape(2 * side, width)
    raw_sims = sim_scale * nt(passages, questions)
    sims = jnp.where(good_col, raw_sims, NEG)
    sim_peak = jnp.max(sims, 0, keepdims=True)
    sim_total = sim_peak + jnp.log(jnp.sum(jnp.exp(sims - sim_peak), 0, keepdims=True))
    target = (iota((2 * side, 2 * side), 0) == pos_row).astype(F32)
    losses = sim_total - jnp.sum(raw_sims * target, 0, keepdims=True)
    loss = jnp.sum(jnp.where(good_row, losses, 0.0), -1, keepdims=True) / (local * n)
    d_sims = sim_scale * (jnp.exp(sims - sim_total) - target) / local
    d_sims = jnp.where(good_row, d_sims, 0.0).astype(BF)

    for c in range(2):
        these = slice(c * side, (c + 1) * side)

        @pl.when((enc == 0) & (core == c))
        def _():
            d_cls[...] = tn(d_sims[:, these], passages)

        @pl.when((enc == 1) & (core == c))
        def _():
            d_cls[...] = nn(d_sims[these, :], questions)

    def column_sum(value):
        return jnp.sum(value, 0, keepdims=True)

    def back(upstream, unit, inverse, gain):
        scaled = upstream * gain
        return inverse[:, :1] * (
            scaled
            - jnp.mean(scaled, -1, keepdims=True)
            - unit * jnp.mean(scaled * unit, -1, keepdims=True)
        )

    vecs[pl.ds(0, 1), :] = column_sum(d_cls[...] * norm2[...])
    vecs[pl.ds(1, 1), :] = column_sum(d_cls[...])
    d_second = back(d_cls[...], norm2[...], inv2[...], gain2[...])
    douter[...] = d_second.astype(BF)
    d_active = nn(douter[...], down_turned[...])
    dinner[...] = (d_active * slope[...]).astype(BF)
    acc[...] = d_second + nn(dinner[...], up_turned[...])
    vecs[pl.ds(2, 1), :] = column_sum(acc[...] * norm1[...])
    vecs[pl.ds(3, 1), :] = column_sum(acc[...])
    vecs[pl.ds(4, 1), :] = jnp.broadcast_to(loss, (1, width))
    vecs[pl.ds(6, 2), :] = jnp.zeros((2, width), F32)
    d_first = back(acc[...], norm1[...], inv1[...], gain1[...])
    dfirst[...] = d_first
    datt[...] = d_first.astype(BF)

    dmix[core] = nn(datt[...], out_turned[...]).astype(BF)
    dmix_over = remote(dmix.at[core], dmix.at[core], fs_sem.at[11], fr_sem.at[11], (enc, sibling))
    dmix_back = remote(dmix.at[core], dmix.at[1 - core], fs_sem.at[11], fr_sem.at[11], (enc, sibling))

    dmix_over.start()

    block_diagonal(dbd, dmix[core, own, :].astype(F32))
    d_weights = nn(dbd[...], v_turned[...])
    weights = probs[...]
    inner_sum = jnp.sum(d_weights * weights, -1, keepdims=True)
    ds_low[...] = (head_scale * weights * (d_weights - inner_sum)).astype(BF)
    dx[...] = nn(ds_low[...], x[...]).astype(BF)
    send_pieces(dx, recv, key_owners, ks_sem, kr_sem)
    dq_own[...] = own_lanes(nn(ds_low[...], kv[:, pl.ds(0, width)])).astype(BF)

    def dq_place(peer):
        return dq_o.at[block(slot_of(peer))]

    save(dq_own, dq_place(me), 6)
    vecs[pl.ds(5, 1), :] = column_sum(dmix[core].astype(F32))

    def layer_tile(r):
        these = pl.ds(r * length, length)

        acc_t[...] = nn(mix[these, :], w_out[...]) + o_bias[...] + x[these, :].astype(F32)
        unit, _ = stats(acc_t[...])
        level = unit * gain1[...] + shift1[...]
        low_t[...] = level.astype(BF)
        inner = nn(low_t[...], w_up[...]) + u_bias[...]
        active = (0.5 * inner * (1.0 + lax.erf(inner * ROOT_HALF))).astype(BF)
        unit, _ = stats(level + d_bias[...] + nn(active, w_down[...]))
        hout[these, :] = (unit * gain2[...] + shift2[...]).astype(BF)
        save(hout.at[these], hidden_out.at[these], 13 + r)

    def piece_place(matrix, i):
        return kv_o.at[
            matrix,
            pl.ds(pl.multiple_of(lax.rem(i, 4) * group_cols, group_cols), group_cols),
            pl.ds(pl.multiple_of(lax.div(i, 4) * half_feats, half_feats), half_feats),
        ]

    def key_place(peer):
        return piece_place(0, lax.div(peer, 2))

    def value_place(peer):
        return piece_place(1, lax.rem(peer, half_n))

    keys = Relay(piece, key_place, gs_sem, gr_sem, n)
    values = Relay(piece_v, value_place, hs_sem, hr_sem, half_n)
    key_save = pltpu.make_async_copy(piece, key_place(me), save_sem.at[16])

    def sum_pieces(i, left, right, target):
        for a in range(H // 4):
            rows_a = right[:, pl.ds(a * PAD, PAD), :].reshape(2 * side, half_feats)
            start = lax.rem(i, 4) * group_cols + a * head
            cols_a = left[pl.ds(pl.multiple_of(start, head), head), :]
            target[pl.ds(a * head, head), :] = nn(cols_a, rows_a).astype(BF)

    pieces_came(recv_v, vr_sem)
    dmix_back.wait_recv()
    for c in range(2):
        turned_v[:, pl.ds(c * side, side)] = dmix[c].astype(F32).T.astype(BF)
    sum_pieces(lax.rem(me, half_n), turned_v, recv_v, piece_v)
    values.start()
    save(piece_v, value_place(me), 10)

    for r in range(2, rows):
        attend_row(r)

    @pl.when(core == 0)
    def _():
        pieces_came(recv, kr_sem)
        sum_pieces(which, turned, recv, piece)
        keys.start()
        key_save.start()

    give(douter, douter_o, 7)
    give(dinner, dinner_o, 8)
    give(datt, datt_o, 9)
    values.plane()
    layer_tile(0)
    layer_tile(1)
    values.over()
    share(dq_own, dq_place, qs_sem, qr_sem)
    remote(dq_own, dq_place(me), qs_sem.at[n - 2], qr_sem.at[me], (enc, sibling)).start()

    @pl.when(core == 0)
    def _():
        keys.plane()

    layer_tile(2)

    base = dfirst[own, :] + nt(dq_own[...], w_qkv[:, query_w])
    base = base.astype(BF)
    qk[...] = nt(qbd[...], w_qkv[:, key_w]).astype(BF)
    dv[...] = nt(dbd[...], w_qkv[:, value_w]).astype(BF)
    y = tn(ds_low[...], qk[...]) + tn(p_low[...], dv[...]) + tn(pick, base)
    hgrad[...] = y.astype(BF)
    save(hgrad, hidden_grad, 17)
    vecs_give = remote(vecs, vecs_o.at[core], fs_sem.at[12], fr_sem.at[12], (enc, sibling))
    vecs_give.start()
    vecs_take = remote(vecs, vecs_o.at[1 - core], fs_sem.at[12], fr_sem.at[12], (enc, sibling))
    save(vecs, vecs_o.at[core], 12)

    def dq_pass(j):
        peer = same_core(j)
        remote(dq_own, dq_place(peer), qs_sem.at[j], qr_sem.at[peer], (enc, peer)).wait_recv()
        send = qs_sem.at[n // 2 - 1 + j]
        remote(dq_place(peer), dq_place(peer), send, qr_sem.at[peer], (enc, sibling)).start()

    loop(n // 2 - 1, dq_pass)
    sent_pieces(px, recv_v, range(n), vs_sem, vr_sem)
    sent_pieces(dx, recv, key_owners, ks_sem, kr_sem)
    xcls_back.wait_send()
    dmix_over.wait_send()
    for copy in [*given, vecs_take]:
        copy.wait_send()
        copy.wait_recv()
    values.sent()
    values.came()
    for copy in saves[:-1]:
        copy.wait()

    @pl.when(core == 0)
    def _():
        key_save.wait()
        keys.over()

    def dq_came(j):
        peer = cousin(j)
        remote(dq_own, dq_place(peer), qs_sem.at[0], qr_sem.at[peer], (enc, sibling)).wait_recv()

    loop(n // 2, dq_came)

    def dq_sent(j):
        remote(dq_own, dq_place(me), qs_sem.at[j], qr_sem.at[me], (enc, sibling)).wait_send()

    loop(n - 1, dq_sent)

    @pl.when(core == 0)
    def _():
        keys.sent()

    @pl.when(core == 1)
    def _():
        keys.came()

    saves[-1].wait()


def grad_kernel(
    xcls_i,
    mixed_i,
    normed_i,
    act_i,
    douter_i,
    dinner_i,
    datt_i,
    dq_i,
    kv_i,
    hidden_out_i,
    hidden_grad_i,
    vecs,
    loss,
    hidden_out,
    hidden_grad,
    grad_qkv,
    grad_query_bias,
    grad_value_bias,
    grad_out,
    grad_out_bias,
    grad_first_gain,
    grad_first_shift,
    grad_up,
    grad_up_bias,
    grad_down,
    grad_down_bias,
    grad_second_gain,
    grad_second_shift,
    xcls,
    mixed,
    normed,
    act,
    douter,
    dinner,
    datt,
    dq,
    kv,
    g_qkv,
    g_out,
    g_up,
    g_down,
    h_out,
    h_grad,
    in_sem,
    out_sem,
):
    width = xcls.shape[1]
    ins = {}
    loads = [
        ("mixed", mixed_i, mixed),
        ("datt", datt_i, datt),
        ("act", act_i, act),
        ("douter", douter_i, douter),
        ("normed", normed_i, normed),
        ("dinner", dinner_i, dinner),
        ("xcls", xcls_i, xcls),
        ("dq", dq_i, dq),
        ("kv", kv_i, kv),
        ("h_out", hidden_out_i, h_out),
        ("h_grad", hidden_grad_i, h_grad),
    ]
    for index, (name, source, target) in enumerate(loads):
        ins[name] = pltpu.make_async_copy(source, target, in_sem.at[index])
        ins[name].start()

    def column_sum(value):
        return jnp.sum(value.astype(F32), 0, keepdims=True)

    def vector(row):
        return vecs[0, pl.ds(row, 1), :] + vecs[1, pl.ds(row, 1), :]

    def put(source, target, rows, index):
        pltpu.make_async_copy(source.at[rows], target.at[0, rows], out_sem.at[index]).start()

    loss[...] = vecs[0, pl.ds(4, 1), pl.ds(0, 1)]
    grad_second_gain[...] = vector(0)
    grad_second_shift[...] = vector(1)
    grad_first_gain[...] = vector(2)
    grad_first_shift[...] = vector(3)
    grad_value_bias[...] = vector(5)

    ins["mixed"].wait()
    ins["datt"].wait()
    g_out[...] = tn(mixed[...], datt[...])
    put(g_out, grad_out, pl.ds(0, width), 4)
    ins["act"].wait()
    ins["douter"].wait()
    for j in range(4):
        these = pl.ds(j * width, width)
        g_down[these, :] = tn(act[:, these], douter[...])
        put(g_down, grad_down, these, 2)
    ins["normed"].wait()
    ins["dinner"].wait()
    for j in range(3):
        these = pl.ds(j * 256, 256)
        g_up[these, :] = tn(normed[:, these], dinner[...])
        put(g_up, grad_up, these, 3)
    ins["xcls"].wait()
    ins["dq"].wait()
    ins["kv"].wait()
    for j in range(3):
        these = pl.ds(j * 256, 256)
        g_qkv[these, pl.ds(0, width)] = tn(xcls[:, these], dq[...])
        for m in range(2):
            g_qkv[these, pl.ds((m + 1) * width, width)] = kv[m, :, these].astype(F32).T
        put(g_qkv, grad_qkv, these, 5)
    through = [
        pltpu.make_async_copy(h_out, hidden_out, out_sem.at[0]),
        pltpu.make_async_copy(h_grad, hidden_grad, out_sem.at[1]),
    ]
    for name, copy in zip(("h_out", "h_grad"), through):
        ins[name].wait()
        copy.start()
    grad_down_bias[...] = column_sum(douter[...])
    grad_up_bias[...] = column_sum(dinner[...])
    grad_out_bias[...] = column_sum(datt[...])
    grad_query_bias[...] = column_sum(dq[...])
    pltpu.make_async_copy(g_down, grad_down.at[0], out_sem.at[2]).wait()
    pltpu.make_async_copy(g_up, grad_up.at[0], out_sem.at[3]).wait()
    pltpu.make_async_copy(g_out, grad_out.at[0], out_sem.at[4]).wait()
    pltpu.make_async_copy(g_qkv, grad_qkv.at[0], out_sem.at[5]).wait()
    for copy in through:
        copy.wait()


def fused_on_device(n, *args):
    (
        hidden_in,
        starts,
        positives,
        qkv_weight,
        query_bias,
        value_bias,
        out_weight,
        out_bias,
        first_gain,
        first_shift,
        up_weight,
        up_bias,
        down_weight,
        down_bias,
        second_gain,
        second_shift,
    ) = args
    rows, length, width = hidden_in.shape[1:]
    tokens = rows * length
    ff = up_weight.shape[-1]
    wide = n * PAD
    side = wide // 2
    spreads = H * PAD
    planes = n // 4
    shape = jax.ShapeDtypeStruct
    hbm = pl.BlockSpec(memory_space=pl.ANY)
    vmem = pl.BlockSpec(memory_space=pltpu.VMEM)
    smem = pl.BlockSpec(memory_space=pltpu.SMEM)
    dma = pltpu.SemaphoreType.DMA
    limit = 60 * 1024 * 1024
    outs = pl.pallas_call(
        functools.partial(main_kernel, n),
        out_shape=[
            shape((tokens, width), BF),
            shape((tokens, width), BF),
            shape((wide, width), BF),
            shape((wide, width), BF),
            shape((wide, width), BF),
            shape((wide, ff), BF),
            shape((wide, width), BF),
            shape((wide, ff), BF),
            shape((wide, width), BF),
            shape((wide, width), BF),
            shape((2, 8, width), F32),
            shape((2, width, width), BF),
        ],
        in_specs=[smem, vmem, hbm, hbm, vmem, vmem, hbm, vmem, vmem, vmem, hbm, vmem, hbm, vmem, vmem, vmem],
        out_specs=[hbm] * 12,
        scratch_shapes=[
            pltpu.VMEM((tokens, width), BF),
            pltpu.VMEM((width, 3 * width), BF),
            pltpu.VMEM((width, width), BF),
            pltpu.VMEM((width, ff), BF),
            pltpu.VMEM((ff, width), BF),
            pltpu.VMEM((width, width), BF),
            pltpu.VMEM((ff, width), BF),
            pltpu.VMEM((width, ff), BF),
            pltpu.VMEM((width, tokens), BF),
            pltpu.VMEM((tokens, 2 * width), BF),
            pltpu.VMEM((tokens, width), BF),
            pltpu.VMEM((tokens, width), BF),
            pltpu.VMEM((length, length), F32),
            pltpu.VMEM((spreads, width), BF),
            pltpu.VMEM((spreads, width), BF),
            pltpu.VMEM((spreads, width), BF),
            pltpu.VMEM((spreads, width), BF),
            pltpu.VMEM((spreads, tokens), F32),
            pltpu.VMEM((spreads, tokens), BF),
            pltpu.VMEM((spreads, tokens), BF),
            pltpu.VMEM((spreads, width), BF),
            pltpu.VMEM((spreads, width), BF),
            pltpu.VMEM((2, side, width), BF),
            pltpu.VMEM((side, width), BF),
            pltpu.VMEM((2, 2, side, width), BF),
            pltpu.VMEM((side, width), F32),
            pltpu.VMEM((side, 128), F32),
            pltpu.VMEM((side, width), F32),
            pltpu.VMEM((side, 128), F32),
            pltpu.VMEM((side, width), BF),
            pltpu.VMEM((side, ff), BF),
            pltpu.VMEM((side, ff), F32),
            pltpu.VMEM((side, ff), BF),
            pltpu.VMEM((side, width), BF),
            pltpu.VMEM((side, width), BF),
            pltpu.VMEM((2, side, width), BF),
            pltpu.VMEM((side, width), F32),
            pltpu.VMEM((side, width), F32),
            pltpu.VMEM((side, width), F32),
            pltpu.VMEM((8, width), F32),
            pltpu.VMEM((width, wide), BF),
            pltpu.VMEM((n, H // 4 * PAD, width // 2), BF),
            pltpu.VMEM((width // 4, width // 2), BF),
            pltpu.VMEM((width, wide), BF),
            pltpu.VMEM((n, H // 4 * PAD, width // 2), BF),
            pltpu.VMEM((width // 4, width // 2), BF),
            pltpu.VMEM((PAD, width), BF),
            pltpu.VMEM((length, width), BF),
            pltpu.VMEM((length, width), F32),
            pltpu.VMEM((tokens, width), BF),
            pltpu.VMEM((tokens, width), BF),
            dma((7,)),
            dma((18,)),
            dma((n // 2,)),
            dma((n,)),
            dma((n // 2,)),
            dma((n,)),
            dma((n // 2,)),
            dma((n,)),
            dma((3,)),
            dma((3,)),
            dma((n - 1,)),
            dma((n,)),
            dma((n,)),
            dma((n,)),
            dma((n,)),
            dma((n,)),
            dma((n,)),
            dma((n,)),
            dma((13,)),
            dma((13,)),
        ],
        compiler_params=pltpu.CompilerParams(
            collective_id=0, has_side_effects=True, vmem_limit_bytes=limit
        ),
        name="layer",
    )(
        jnp.transpose(starts, (1, 0, 2)),
        positives,
        hidden_in.reshape(tokens, width),
        qkv_weight.reshape(width, 3 * width),
        query_bias,
        value_bias,
        out_weight.reshape(width, width),
        out_bias,
        first_gain,
        first_shift,
        up_weight.reshape(width, ff),
        up_bias,
        down_weight.reshape(ff, width),
        down_bias,
        second_gain,
        second_shift,
    )
    h_out, h_grad, xcls, mixed, normed, act, douter, dinner, datt, dq, vecs, kv = outs
    row = shape((1, width), F32)
    grads = pl.pallas_call(
        grad_kernel,
        out_shape=[
            shape((1, 1), F32),
            shape((tokens, width), BF),
            shape((tokens, width), BF),
            shape((1, width, 3 * width), F32),
            row,
            row,
            shape((1, width, width), F32),
            row,
            row,
            row,
            shape((1, width, ff), F32),
            shape((1, ff), F32),
            shape((1, ff, width), F32),
            row,
            row,
            row,
        ],
        in_specs=[hbm] * 11 + [vmem],
        out_specs=[vmem, hbm, hbm, hbm, vmem, vmem, hbm, vmem, vmem, vmem, hbm, vmem, hbm, vmem, vmem, vmem],
        scratch_shapes=[
            pltpu.VMEM((wide, width), BF),
            pltpu.VMEM((wide, width), BF),
            pltpu.VMEM((wide, width), BF),
            pltpu.VMEM((wide, ff), BF),
            pltpu.VMEM((wide, width), BF),
            pltpu.VMEM((wide, ff), BF),
            pltpu.VMEM((wide, width), BF),
            pltpu.VMEM((wide, width), BF),
            pltpu.VMEM((2, width, width), BF),
            pltpu.VMEM((width, 3 * width), F32),
            pltpu.VMEM((width, width), F32),
            pltpu.VMEM((width, ff), F32),
            pltpu.VMEM((ff, width), F32),
            pltpu.VMEM((tokens, width), BF),
            pltpu.VMEM((tokens, width), BF),
            dma((11,)),
            dma((6,)),
        ],
        compiler_params=pltpu.CompilerParams(vmem_limit_bytes=limit),
        name="gradients",
    )(xcls, mixed, normed, act, douter, dinner, datt, dq, kv, h_out, h_grad, vecs)
    place = (1, rows, length, width)
    return (
        grads[0].reshape(()),
        grads[1].reshape(place),
        grads[2].reshape(place),
        *grads[3:],
    )


def solution(mesh):
    placed = (
        P("enc", "dp", None, None),
        P("enc", "dp", None),
        P(),
        P("enc", None, None),
        P("enc", None),
        P("enc", None),
        P("enc", None, None),
        P("enc", None),
        P("enc", None),
        P("enc", None),
        P("enc", None, None),
        P("enc", None),
        P("enc", None, None),
        P("enc", None),
        P("enc", None),
        P("enc", None),
    )
    n = mesh.shape["dp"]
    body = functools.partial(fused_on_device, n) if n == OWNERS else on_device
    return jax.shard_map(
        body,
        mesh=mesh,
        in_specs=placed,
        out_specs=(
            P(),
            P("enc", "dp", None, None),
            P("enc", "dp", None, None),
            P("enc", None, None),
            P("enc", None),
            P("enc", None),
            P("enc", None, None),
            P("enc", None),
            P("enc", None),
            P("enc", None),
            P("enc", None, None),
            P("enc", None),
            P("enc", None, None),
            P("enc", None),
            P("enc", None),
            P("enc", None),
        ),
        check_vma=False,
    )
```

```python
import functools

import jax
import jax.numpy as jnp
from jax import lax
from jax.experimental import pallas as pl
from jax.experimental.pallas import tpu as pltpu
from jax.sharding import PartitionSpec as P

OWNERS = 16
H = 12
DOCS = 4


EPS_NORM = 1e-12


def partner(value, axis, distance):
    mask = 2**distance
    pairs = [(source, source ^ mask) for source in range(lax.axis_size(axis))]
    return lax.ppermute(value, axis, pairs)


def product(left, right):
    return jnp.dot(left, right, preferred_element_type=jnp.float32)


def layer_stats(hidden):
    centred = hidden - jnp.mean(hidden, -1, keepdims=True)
    inverse = lax.rsqrt(jnp.mean(centred * centred, -1, keepdims=True) + EPS_NORM)
    return (centred * inverse, inverse)


def norm_back(upstream, normal, inverse, gain):
    scaled = upstream * gain
    return inverse * (
        scaled
        - jnp.mean(scaled, -1, keepdims=True)
        - normal * jnp.mean(scaled * normal, -1, keepdims=True)
    )


def on_device(
    hidden_in,
    starts,
    positives,
    qkv_weight,
    query_bias,
    value_bias,
    out_weight,
    out_bias,
    first_gain,
    first_shift,
    up_weight,
    up_bias,
    down_weight,
    down_bias,
    second_gain,
    second_shift,
):
    rows, length, width = (hidden_in.shape[1], hidden_in.shape[2], hidden_in.shape[3])
    heads = H
    head_size = width // heads
    tokens = rows * length
    flat = hidden_in.reshape(tokens, width)
    w_qkv = qkv_weight[0]
    w_out = out_weight[0]
    w_up = up_weight[0]
    w_down = down_weight[0]
    row_starts = starts[0]
    qkv_shift = jnp.concatenate([query_bias[0], jnp.zeros_like(query_bias[0]), value_bias[0]])
    qkv = (product(flat, w_qkv) + qkv_shift).astype(jnp.bfloat16)
    split = qkv.reshape(rows, length, 3, heads, head_size)
    query, key, value = (split[:, :, 0], split[:, :, 1], split[:, :, 2])
    places = jnp.arange(length, dtype=jnp.int32)
    segment = jnp.sum((places[None, :, None] >= row_starts[:, None, :]).astype(jnp.int32), -1)
    allowed = (segment[:, :, None] == segment[:, None, :])[:, None]
    head_scale = head_size ** (-0.5)

    def attention_scores(left, right):
        raw = jnp.einsum("rqhe,rkhe->rhqk", left, right, preferred_element_type=jnp.float32)
        return jnp.where(allowed, head_scale * raw, -1e30)

    scores = attention_scores(query, key)
    peak = jnp.max(scores, -1, keepdims=True)
    log_total = peak + jnp.log(jnp.sum(jnp.exp(scores - peak), -1, keepdims=True))
    weights_low = jnp.exp(scores - log_total).astype(jnp.bfloat16)
    mixed = jnp.einsum("rhqk,rkhe->rqhe", weights_low, value, preferred_element_type=jnp.float32)
    mixed = mixed.astype(jnp.bfloat16).reshape(tokens, width)
    attended = product(mixed, w_out) + out_bias[0]
    first_normal, first_inverse = layer_stats(flat.astype(jnp.float32) + attended)
    normed = first_normal * first_gain[0] + first_shift[0]
    normed_low = normed.astype(jnp.bfloat16)
    inner = product(normed_low, w_up) + up_bias[0]
    activated_low = jax.nn.gelu(inner, approximate=False).astype(jnp.bfloat16)
    outer = product(activated_low, w_down) + down_bias[0]
    second_normal, second_inverse = layer_stats(normed + outer)
    encoded = second_normal * second_gain[0] + second_shift[0]
    hidden_out = encoded.astype(jnp.bfloat16).reshape(1, rows, length, width)
    picker = (places[None, None, :] == row_starts[:, :, None]).astype(jnp.float32)
    cls = jnp.einsum(
        "rdl,rlw->rdw",
        picker,
        encoded.reshape(rows, length, width),
        precision=lax.Precision.HIGHEST,
    )
    local_count = rows * DOCS
    cls_low = cls.reshape(local_count, width).astype(jnp.bfloat16)
    first_half = lax.axis_index("enc") == 0
    mine = lax.all_gather(cls_low, "dp", axis=0, tiled=True)
    other = partner(mine, "enc", 0)
    questions = jnp.where(first_half, mine, other)
    passages = jnp.where(first_half, other, mine)
    count = questions.shape[0]
    sim_scale = width ** (-0.5)
    sims = sim_scale * jnp.einsum(
        "qw,pw->qp", questions, passages, preferred_element_type=jnp.float32
    )
    sim_peak = jnp.max(sims, -1, keepdims=True)
    sim_total = sim_peak + jnp.log(jnp.sum(jnp.exp(sims - sim_peak), -1, keepdims=True))
    target = (jnp.arange(count, dtype=jnp.int32)[None, :] == positives[:, None]).astype(jnp.float32)
    total = jnp.sum(sim_total[:, 0] - jnp.sum(sims * target, -1)) / local_count
    loss_mean = total / lax.axis_size("dp")
    d_sims_low = (sim_scale * (jnp.exp(sims - sim_total) - target) / local_count).astype(
        jnp.bfloat16
    )
    own_start = lax.axis_index("dp") * local_count
    own_rows = lax.dynamic_slice_in_dim(d_sims_low, own_start, local_count, 0)
    own_columns = lax.dynamic_slice_in_dim(d_sims_low, own_start, local_count, 1)
    d_questions = jnp.einsum("qp,pw->qw", own_rows, passages, preferred_element_type=jnp.float32)
    d_passages = jnp.einsum("qp,qw->pw", own_columns, questions, preferred_element_type=jnp.float32)
    d_cls = jnp.where(first_half, d_questions, d_passages).reshape(rows, DOCS, width)
    d_encoded = jnp.einsum("rdl,rdw->rlw", picker, d_cls, precision=lax.Precision.HIGHEST).reshape(
        tokens, width
    )
    grad_second_gain = jnp.sum(d_encoded * second_normal, 0)
    grad_second_shift = jnp.sum(d_encoded, 0)
    d_second = norm_back(d_encoded, second_normal, second_inverse, second_gain[0])
    d_outer_low = d_second.astype(jnp.bfloat16)
    grad_down_bias = jnp.sum(d_outer_low.astype(jnp.float32), 0)
    grad_down_weight = jnp.einsum(
        "tf,tw->fw", activated_low, d_outer_low, preferred_element_type=jnp.float32
    )
    d_activated = jnp.einsum("tw,fw->tf", d_outer_low, w_down, preferred_element_type=jnp.float32)
    normal_cdf = 0.5 * (1.0 + lax.erf(inner * 0.7071067811865476))
    slope = normal_cdf + inner * jnp.exp(-0.5 * inner * inner) * 0.3989422804014327
    d_inner_low = (d_activated * slope).astype(jnp.bfloat16)
    grad_up_bias = jnp.sum(d_inner_low.astype(jnp.float32), 0)
    grad_up_weight = jnp.einsum(
        "tw,tf->wf", normed_low, d_inner_low, preferred_element_type=jnp.float32
    )
    d_normed = d_second + jnp.einsum(
        "tf,wf->tw", d_inner_low, w_up, preferred_element_type=jnp.float32
    )
    grad_first_gain = jnp.sum(d_normed * first_normal, 0)
    grad_first_shift = jnp.sum(d_normed, 0)
    d_first = norm_back(d_normed, first_normal, first_inverse, first_gain[0])
    d_attended_low = d_first.astype(jnp.bfloat16)
    grad_out_bias = jnp.sum(d_attended_low.astype(jnp.float32), 0)
    grad_out_weight = jnp.einsum(
        "tv,tw->vw", mixed, d_attended_low, preferred_element_type=jnp.float32
    )
    d_mixed_low = jnp.einsum(
        "tw,vw->tv", d_attended_low, w_out, preferred_element_type=jnp.float32
    ).astype(jnp.bfloat16)
    d_mixed_heads = d_mixed_low.reshape(rows, length, heads, head_size)
    probs_again = jnp.exp(attention_scores(query, key) - log_total)
    weights_again = probs_again.astype(jnp.bfloat16)
    grad_value = jnp.einsum(
        "rhqk,rqhe->rkhe", weights_again, d_mixed_heads, preferred_element_type=jnp.float32
    )
    d_weights = jnp.einsum(
        "rqhe,rkhe->rhqk", d_mixed_heads, value, preferred_element_type=jnp.float32
    )
    d_scores = probs_again * (d_weights - jnp.sum(d_weights * probs_again, -1, keepdims=True))
    d_raw_low = (head_scale * d_scores).astype(jnp.bfloat16)
    grad_query = jnp.einsum("rhqk,rkhe->rqhe", d_raw_low, key, preferred_element_type=jnp.float32)
    grad_key = jnp.einsum("rhqk,rqhe->rkhe", d_raw_low, query, preferred_element_type=jnp.float32)
    d_qkv_low = (
        jnp.stack([grad_query, grad_key, grad_value], 2)
        .reshape(tokens, 3 * width)
        .astype(jnp.bfloat16)
    )
    grad_qkv_local = jnp.einsum("tw,tv->wv", flat, d_qkv_low, preferred_element_type=jnp.float32)
    bias_sums = jnp.sum(d_qkv_low.astype(jnp.float32), 0)
    grad_query_local = bias_sums[:width]
    grad_value_local = bias_sums[2 * width :]
    d_input = d_first + jnp.einsum(
        "tv,wv->tw", d_qkv_low, w_qkv, preferred_element_type=jnp.float32
    )
    hidden_grad = d_input.astype(jnp.bfloat16).reshape(1, rows, length, width)
    (
        share_qkv,
        share_query_bias,
        share_value_bias,
        share_out_weight,
        share_out_bias,
        share_first_gain,
        share_first_shift,
        share_up_weight,
        share_up_bias,
        share_down_weight,
        share_down_bias,
        share_second_gain,
        share_second_shift,
    ) = (
        lax.psum_scatter(grad_qkv_local[None], "dp", scatter_dimension=1, tiled=True),
        lax.psum_scatter(grad_query_local[None], "dp", scatter_dimension=1, tiled=True),
        lax.psum_scatter(grad_value_local[None], "dp", scatter_dimension=1, tiled=True),
        lax.psum_scatter(grad_out_weight[None], "dp", scatter_dimension=1, tiled=True),
        lax.psum_scatter(grad_out_bias[None], "dp", scatter_dimension=1, tiled=True),
        lax.psum_scatter(grad_first_gain[None], "dp", scatter_dimension=1, tiled=True),
        lax.psum_scatter(grad_first_shift[None], "dp", scatter_dimension=1, tiled=True),
        lax.psum_scatter(grad_up_weight[None], "dp", scatter_dimension=1, tiled=True),
        lax.psum_scatter(grad_up_bias[None], "dp", scatter_dimension=1, tiled=True),
        lax.psum_scatter(grad_down_weight[None], "dp", scatter_dimension=1, tiled=True),
        lax.psum_scatter(grad_down_bias[None], "dp", scatter_dimension=1, tiled=True),
        lax.psum_scatter(grad_second_gain[None], "dp", scatter_dimension=1, tiled=True),
        lax.psum_scatter(grad_second_shift[None], "dp", scatter_dimension=1, tiled=True),
    )
    summed = (
        lax.all_gather(share_qkv.astype(jnp.bfloat16), "dp", axis=1, tiled=True).astype(
            share_qkv.dtype
        ),
        lax.all_gather(share_query_bias.astype(jnp.bfloat16), "dp", axis=1, tiled=True).astype(
            share_query_bias.dtype
        ),
        lax.all_gather(share_value_bias.astype(jnp.bfloat16), "dp", axis=1, tiled=True).astype(
            share_value_bias.dtype
        ),
        lax.all_gather(share_out_weight.astype(jnp.bfloat16), "dp", axis=1, tiled=True).astype(
            share_out_weight.dtype
        ),
        lax.all_gather(share_out_bias.astype(jnp.bfloat16), "dp", axis=1, tiled=True).astype(
            share_out_bias.dtype
        ),
        lax.all_gather(share_first_gain.astype(jnp.bfloat16), "dp", axis=1, tiled=True).astype(
            share_first_gain.dtype
        ),
        lax.all_gather(share_first_shift.astype(jnp.bfloat16), "dp", axis=1, tiled=True).astype(
            share_first_shift.dtype
        ),
        lax.all_gather(share_up_weight.astype(jnp.bfloat16), "dp", axis=1, tiled=True).astype(
            share_up_weight.dtype
        ),
        lax.all_gather(share_up_bias.astype(jnp.bfloat16), "dp", axis=1, tiled=True).astype(
            share_up_bias.dtype
        ),
        lax.all_gather(share_down_weight.astype(jnp.bfloat16), "dp", axis=1, tiled=True).astype(
            share_down_weight.dtype
        ),
        lax.all_gather(share_down_bias.astype(jnp.bfloat16), "dp", axis=1, tiled=True).astype(
            share_down_bias.dtype
        ),
        lax.all_gather(share_second_gain.astype(jnp.bfloat16), "dp", axis=1, tiled=True).astype(
            share_second_gain.dtype
        ),
        lax.all_gather(share_second_shift.astype(jnp.bfloat16), "dp", axis=1, tiled=True).astype(
            share_second_shift.dtype
        ),
    )
    return (
        loss_mean,
        hidden_out,
        hidden_grad,
        summed[0],
        summed[1],
        summed[2],
        summed[3],
        summed[4],
        summed[5],
        summed[6],
        summed[7],
        summed[8],
        summed[9],
        summed[10],
        summed[11],
        summed[12],
    )


PAD = 16
BF = jnp.bfloat16
F32 = jnp.float32
MESH = pl.DeviceIdType.MESH
NEG = -1e30
ROOT_HALF = 0.7071067811865476
PEAK = 0.3989422804014327


def nn(left, right):
    return jnp.dot(left, right, preferred_element_type=F32)


def nt(left, right):
    return lax.dot_general(left, right, (((1,), (1,)), ((), ())), preferred_element_type=F32)


def tn(left, right):
    return lax.dot_general(left, right, (((0,), (0,)), ((), ())), preferred_element_type=F32)


def iota(shape, dim):
    return lax.broadcasted_iota(jnp.int32, shape, dim)


def gelu_parts(inner):
    cdf = 0.5 * (1.0 + lax.erf(inner * ROOT_HALF))
    return cdf, jnp.exp(-0.5 * inner * inner) * PEAK


def chunk(index, size):
    return pl.ds(pl.multiple_of(index * size, size), size)


def loop(count, body):
    def step(index, carry):
        body(index)
        return carry

    lax.fori_loop(0, count, step, 0)


def main_kernel(
    n,
    starts,
    positives,
    x_hbm,
    qkv_hbm,
    q_bias,
    v_bias,
    out_hbm,
    o_bias,
    gain1,
    shift1,
    up_hbm,
    u_bias,
    down_hbm,
    d_bias,
    gain2,
    shift2,
    hidden_out,
    hidden_grad,
    xcls_o,
    mixed_o,
    normed_o,
    act_o,
    douter_o,
    dinner_o,
    datt_o,
    dq_o,
    vecs_o,
    kv_o,
    x,
    w_qkv,
    w_out,
    w_up,
    w_down,
    out_turned,
    up_turned,
    down_turned,
    v_turned,
    kv,
    q,
    mix,
    seg_bias,
    qbd,
    dbd,
    qk,
    dv,
    probs,
    p_low,
    ds_low,
    px,
    dx,
    xcls,
    mixed,
    cls,
    packed,
    norm1,
    inv1,
    norm2,
    inv2,
    normed,
    act,
    slope,
    dinner,
    douter,
    datt,
    dmix,
    d_cls,
    dfirst,
    acc,
    vecs,
    turned,
    recv,
    piece,
    turned_v,
    recv_v,
    piece_v,
    dq_own,
    low_t,
    acc_t,
    hout,
    hgrad,
    load_sem,
    save_sem,
    xs_sem,
    xr_sem,
    ms_sem,
    mr_sem,
    ks_sem,
    kr_sem,
    cs_sem,
    cr_sem,
    qs_sem,
    qr_sem,
    vs_sem,
    vr_sem,
    gs_sem,
    gr_sem,
    hs_sem,
    hr_sem,
    fs_sem,
    fr_sem,
):
    enc = lax.axis_index("enc")
    me = lax.axis_index("dp")
    other = 1 - enc
    core = lax.rem(me, 2)
    which = lax.div(me, 2)
    sibling = me + 1 - 2 * core
    across = me + 2 - 4 * lax.rem(which, 2)
    tokens, width = x.shape
    ff = w_up.shape[1]
    side = n // 2 * PAD
    rows = starts.shape[0]
    length = tokens // rows
    local = rows * DOCS
    head = width // H
    pairs = H // 2
    head_scale = head ** (-0.5)
    group_cols = width // 4
    half_feats = width // 2
    group_rows = H // 4 * PAD
    query_w = pl.ds(0, width)
    key_w = pl.ds(width, width)
    value_w = pl.ds(2 * width, width)

    def weight_load(cols, index):
        return pltpu.make_async_copy(qkv_hbm.at[:, cols], w_qkv.at[:, cols], load_sem.at[index])

    loads = [
        pltpu.make_async_copy(x_hbm, x, load_sem.at[0]),
        weight_load(key_w, 1),
        weight_load(query_w, 2),
        weight_load(value_w, 3),
        pltpu.make_async_copy(out_hbm, w_out, load_sem.at[4]),
        pltpu.make_async_copy(up_hbm, w_up, load_sem.at[5]),
        pltpu.make_async_copy(down_hbm, w_down, load_sem.at[6]),
    ]
    for copy in loads:
        copy.start()

    barrier = pltpu.get_barrier_semaphore()

    def greet(j):
        peer = lax.rem(me + j + 1, n)
        pl.semaphore_signal(barrier, inc=1, device_id=(enc, peer), device_id_type=MESH)

    loop(n - 1, greet)
    pl.semaphore_signal(barrier, inc=1, device_id=(other, me), device_id_type=MESH)

    def remote(source, target, send, receive, device):
        return pltpu.make_async_remote_copy(
            src_ref=source,
            dst_ref=target,
            send_sem=send,
            recv_sem=receive,
            device_id=device,
            device_id_type=MESH,
        )

    def same_core(j):
        return lax.rem(me + 2 * j + 2, n)

    def cousin(j):
        return lax.rem(same_core(j) + 1 - 2 * core + n, n)

    def block(index):
        return pl.ds(pl.multiple_of(index * PAD, PAD), PAD)

    own = block(which)

    def share(source, place, send, receive):
        def go(j):
            remote(source, place(me), send.at[j], receive.at[me], (enc, same_core(j))).start()

        loop(n // 2 - 1, go)

    def shared(source, place, send, receive):
        def came(j):
            peer = same_core(j)
            copy = remote(source, place(peer), send.at[j], receive.at[peer], (enc, peer))
            copy.wait_send()
            copy.wait_recv()

        loop(n // 2 - 1, came)

    class Relay:
        def __init__(self, source, place, send, receive, group):
            self.source, self.place, self.send, self.receive = source, place, send, receive
            self.base = me - lax.rem(me, group)
            self.group = group
            self.ups = group // 4 - 1

        def up(self, device, j):
            return self.base + lax.rem(device - self.base + 4 * j, self.group)

        def copy(self, slot, source, owner, device):
            return remote(
                source, self.place(owner), self.send.at[slot], self.receive.at[owner], (enc, device)
            )

        def start(self):
            for j in range(self.ups):
                self.copy(j, self.source, me, self.up(me, j + 1)).start()
            self.copy(self.ups, self.source, me, across).start()
            self.copy(self.ups + 1, self.source, me, sibling).start()

        def plane(self):
            for j in range(self.ups):
                peer = self.up(me, j + 1)
                self.copy(0, self.place(peer), peer, peer).wait_recv()
                self.copy(self.ups + 2 + 2 * j, self.place(peer), peer, across).start()
                self.copy(self.ups + 3 + 2 * j, self.place(peer), peer, sibling).start()

        def over(self):
            for j in range(self.ups + 1):
                peer = self.up(across, j)
                self.copy(0, self.place(peer), peer, across).wait_recv()
                self.copy(3 * self.ups + 2 + j, self.place(peer), peer, sibling).start()

        def sent(self):
            def wait(j):
                self.copy(j, self.source, me, sibling).wait_send()

            loop(4 * self.ups + 3, wait)

        def came(self):
            for j in range(self.ups + 1):
                for peer in (self.up(sibling, j), self.up(across + sibling - me, j)):
                    self.copy(0, self.place(peer), peer, sibling).wait_recv()

    saves = []

    def save(source, target, index):
        copy = pltpu.make_async_copy(source, target, save_sem.at[index])
        copy.start()
        saves.append(copy)

    halves = [pl.ds(pl.multiple_of(core * side, side), side)]
    halves.append(pl.ds(pl.multiple_of((1 - core) * side, side), side))
    given = []

    def give(source, target, index):
        save(source, target.at[halves[0]], index)
        copy = remote(source, target.at[halves[0]], fs_sem.at[index], fr_sem.at[index], (enc, sibling))
        copy.start()
        given.append(
            remote(source, target.at[halves[1]], fs_sem.at[index], fr_sem.at[index], (enc, sibling))
        )

    first_col = jnp.full((PAD, 1), -1, jnp.int32)
    seg_col = jnp.full((PAD, 1), -1, jnp.int32)
    place_col = iota((PAD, 1), 0)
    segs = []
    for r in range(rows):
        place = iota((1, length), 1)
        count = jnp.zeros((1, length), jnp.int32)
        for k in range(DOCS):
            start = starts[r, 0, k]
            count = count + (place >= start).astype(jnp.int32)
            order = jnp.int32(0)
            for m in range(DOCS):
                order = order + jnp.where(starts[r, 0, m] <= start, 1, 0)
            here = place_col == r * DOCS + k
            first_col = jnp.where(here, r * length + start, first_col)
            seg_col = jnp.where(here, r * 8 + order, seg_col)
        segs.append(count + r * 8)
    seg_row = jnp.concatenate(segs, axis=1)
    pick = (iota((PAD, tokens), 1) == first_col).astype(F32).astype(BF)
    allowed = seg_row == seg_col

    low_half = iota((1, 128), 1) < head

    def block_diagonal(target, block_rows):
        for p in range(pairs):
            part = block_rows[:, p * 128 : (p + 1) * 128]
            even = jnp.where(low_half, part, 0.0).astype(BF)
            odd = jnp.where(low_half, 0.0, part).astype(BF)
            target[pl.ds(2 * p * PAD, PAD), pl.ds(p * 128, 128)] = even
            target[pl.ds((2 * p + 1) * PAD, PAD), pl.ds(p * 128, 128)] = odd

    def own_lanes(full):
        parts = []
        for p in range(pairs):
            lanes = slice(p * 128, (p + 1) * 128)
            even = full[2 * p * PAD : (2 * p + 1) * PAD, lanes]
            odd = full[(2 * p + 1) * PAD : (2 * p + 2) * PAD, lanes]
            parts.append(jnp.where(low_half, even, odd))
        return jnp.concatenate(parts, axis=1)

    qbd[...] = jnp.zeros_like(qbd)
    dbd[...] = jnp.zeros_like(dbd)
    loads[0].wait()
    xcls[core, own, :] = nn(pick, x[...]).astype(BF)
    pl.semaphore_wait(barrier, n)

    def xcls_place(peer):
        return xcls.at[core, block(lax.div(peer, 2))]

    share(xcls.at[core, own], xcls_place, xs_sem, xr_sem)

    loads[1].wait()
    kv[:, pl.ds(0, width)] = nn(x[...], w_qkv[:, key_w]).astype(BF)
    loads[2].wait()
    q_own = (nn(xcls[core, own, :], w_qkv[:, query_w]) + q_bias[...]).astype(BF).astype(F32)
    block_diagonal(qbd, q_own)
    loads[3].wait()
    kv[:, pl.ds(width, width)] = (nn(x[...], w_qkv[:, value_w]) + v_bias[...]).astype(BF)
    allowed_all = jnp.concatenate([allowed] * H, axis=0)
    scores = jnp.where(allowed_all, head_scale * nt(qbd[...], kv[:, pl.ds(0, width)]), NEG)
    peak = jnp.max(scores, -1, keepdims=True)
    raw = jnp.where(allowed_all, jnp.exp(scores - peak), 0.0)
    total = jnp.sum(raw, -1, keepdims=True)
    weights = raw / jnp.where(total > 0.0, total, 1.0)
    probs[...] = weights
    p_low[...] = weights.astype(BF)
    mixed[own, :] = own_lanes(nn(p_low[...], kv[:, pl.ds(width, width)])).astype(BF)

    def mixed_place(peer):
        return mixed.at[block(lax.div(peer, 2))]

    share(mixed.at[own], mixed_place, ms_sem, mr_sem)

    half_n = n // 2

    def slot_of(peer):
        return lax.rem(peer, 2) * half_n + lax.div(peer, 2)

    def send_pieces(source, into, owners, send, receive):
        for j, owner in enumerate(owners):
            i = j % half_n
            part = source.at[
                pl.ds((i % 4) * group_rows, group_rows), pl.ds((i // 4) * half_feats, half_feats)
            ]

            @pl.when(me != owner)
            def _():
                remote(part, into.at[slot_of(me)], send.at[j], receive.at[me], (enc, owner)).start()

            @pl.when(me == owner)
            def _():
                into[slot_of(me)] = part[...]

    def sent_pieces(source, into, owners, send, receive):
        part = source.at[pl.ds(0, group_rows), pl.ds(0, half_feats)]
        for j, owner in enumerate(owners):

            @pl.when(me != owner)
            def _():
                remote(
                    part, into.at[slot_of(me)], send.at[j], receive.at[me], (enc, owner)
                ).wait_send()

    def pieces_came(into, receive):
        def came(j):
            peer = lax.rem(me + j + 1, n)
            place = into.at[slot_of(peer)]
            remote(place, place, ks_sem.at[0], receive.at[peer], (enc, peer)).wait_recv()

        loop(n - 1, came)

    key_owners = range(0, n, 2)
    px[...] = nn(p_low[...], x[...]).astype(BF)
    v_turned[...] = kv[:, pl.ds(width, width)].T
    y = nn(x[...], w_qkv[:, query_w]) + q_bias[...]
    q[...] = (y.astype(BF).astype(F32) * head_scale).astype(BF)
    loads[5].wait()
    up_turned[...] = w_up[...].T
    def attend_row(r):
        place0 = iota((length, 1), 0)
        place1 = iota((1, length), 1)
        count0 = jnp.zeros((length, 1), jnp.int32)
        count1 = jnp.zeros((1, length), jnp.int32)
        for k in range(DOCS):
            start = starts[r, 0, k]
            count0 = count0 + (place0 >= start).astype(jnp.int32)
            count1 = count1 + (place1 >= start).astype(jnp.int32)
        seg_bias[...] = jnp.where(count0 == count1, 0.0, NEG)
        these = pl.ds(r * length, length)
        mask_even = jnp.where(low_half, 1.0, 0.0).astype(BF)
        mask_odd = jnp.where(low_half, 0.0, 1.0).astype(BF)

        for p in range(pairs):
            lanes = pl.ds(p * 128, 128)
            query = q[these, lanes]
            key = kv[these, lanes]
            value = kv[these, pl.ds(width + p * 128, 128)]
            ext = jnp.concatenate([value, jnp.ones_like(value)], axis=1)
            outs = []
            for mask in (mask_even, mask_odd):
                s = nt(query * mask, key) + seg_bias[...]
                e = jnp.exp(s - jnp.max(s, -1, keepdims=True)).astype(BF)
                outs.append(nn(e, ext))
            even, odd = outs
            top = jnp.where(low_half, even[:, :128], odd[:, :128])
            low = jnp.where(low_half, even[:, 128:], odd[:, 128:])
            mix[these, lanes] = (top / low).astype(BF)

    attend_row(0)

    shared(xcls.at[core, own], xcls_place, xs_sem, xr_sem)
    xcls_over = remote(xcls.at[core], xcls.at[core], fs_sem.at[10], fr_sem.at[10], (enc, sibling))
    xcls_over.start()
    xcls_back = remote(xcls.at[core], xcls.at[1 - core], fs_sem.at[10], fr_sem.at[10], (enc, sibling))
    shared(mixed.at[own], mixed_place, ms_sem, mr_sem)
    send_pieces(px, recv_v, range(n), vs_sem, vr_sem)
    loads[4].wait()

    acc[...] = nn(mixed[...], w_out[...]) + o_bias[...] + xcls[core].astype(F32)

    def stats(h):
        centred = h - jnp.mean(h, -1, keepdims=True)
        inverse = lax.rsqrt(jnp.mean(centred * centred, -1, keepdims=True) + EPS_NORM)
        return centred * inverse, inverse

    unit, inverse = stats(acc[...])
    norm1[...] = unit
    inv1[...] = jnp.broadcast_to(inverse, inv1.shape)
    level = unit * gain1[...] + shift1[...]
    normed[...] = level.astype(BF)
    loads[6].wait()
    inner = nn(normed[...], w_up[...]) + u_bias[...]
    cdf, pdf = gelu_parts(inner)
    slope[...] = cdf + inner * pdf
    act[...] = (inner * cdf).astype(BF)
    unit, inverse = stats(level + d_bias[...] + nn(act[...], w_down[...]))
    norm2[...] = unit
    inv2[...] = jnp.broadcast_to(inverse, inv2.shape)
    cls[enc, core] = (unit * gain2[...] + shift2[...]).astype(BF)

    dense = packed.shape[2]
    order = iota((dense, 1), 0)
    keep = iota((dense, side), 1) == order + (PAD - local) * lax.div(order, local)
    keep = keep.astype(F32).astype(BF)
    packed[enc, core] = nn(keep, cls[enc, core]).astype(BF)

    def unpack(half_of, from_core):
        cls[half_of, from_core] = tn(keep, packed[half_of, from_core]).astype(BF)


    def cls_copy(half_of, to_core, index, device):
        return remote(
            packed.at[half_of, core], packed.at[half_of, to_core], cs_sem.at[index], cr_sem.at[index], device
        )

    cls_copy(enc, core, 0, (other, me)).start()
    cls_copy(enc, core, 1, (enc, sibling)).start()
    give(mixed, mixed_o, 1)
    give(normed, normed_o, 2)
    give(act, act_o, 3)

    def padded(question):
        device = lax.div(question, local)
        place = lax.rem(device, 2) * side + lax.div(device, 2) * PAD
        return place + question - device * local

    count = n * local
    spot = padded(iota((count, 1), 0)) == iota((count, 2 * side), 1)
    goal = padded(positives[...].reshape(1, count)) + 1
    pos_row = nn(goal.astype(F32).astype(BF), spot.astype(F32).astype(BF)).astype(jnp.int32) - 1

    down_turned[...] = w_down[...].T
    out_turned[...] = w_out[...].T
    attend_row(1)

    xcls_back.wait_recv()

    @pl.when(core == 0)
    def _():
        for c in range(2):
            y = (nn(xcls[c], w_qkv[:, query_w]) + q_bias[...]).astype(BF).astype(F32)
            turned[:, pl.ds(c * side, side)] = y.T.astype(BF)

    save(xcls.at[0], xcls_o.at[pl.ds(0, side)], 4)
    save(xcls.at[1], xcls_o.at[pl.ds(side, side)], 5)

    cls_copy(enc, core, 0, (other, me)).wait_send()
    cls_in = remote(
        packed.at[enc, core], packed.at[other, core], cs_sem.at[0], cr_sem.at[0], (other, me)
    )
    cls_in.wait_recv()
    cls_pass = cls_copy(other, core, 2, (enc, sibling))
    cls_pass.start()
    cls_copy(enc, core, 1, (enc, sibling)).wait_send()
    remote(
        packed.at[enc, core], packed.at[enc, 1 - core], cs_sem.at[1], cr_sem.at[1], (enc, sibling)
    ).wait_recv()
    unpack(enc, 1 - core)
    unpack(other, core)
    cls_pass.wait_send()
    remote(
        packed.at[other, core], packed.at[other, 1 - core], cs_sem.at[2], cr_sem.at[2], (enc, sibling)
    ).wait_recv()
    unpack(other, 1 - core)

    sim_scale = width ** (-0.5)
    good_col = lax.rem(iota((2 * side, 1), 0), PAD) < local
    good_row = lax.rem(iota((1, 2 * side), 1), PAD) < local
    questions = cls[0].reshape(2 * side, width)
    passages = cls[1].reshape(2 * side, width)
    raw_sims = sim_scale * nt(passages, questions)
    sims = jnp.where(good_col, raw_sims, NEG)
    sim_peak = jnp.max(sims, 0, keepdims=True)
    sim_total = sim_peak + jnp.log(jnp.sum(jnp.exp(sims - sim_peak), 0, keepdims=True))
    target = (iota((2 * side, 2 * side), 0) == pos_row).astype(F32)
    losses = sim_total - jnp.sum(raw_sims * target, 0, keepdims=True)
    loss = jnp.sum(jnp.where(good_row, losses, 0.0), -1, keepdims=True) / (local * n)
    d_sims = sim_scale * (jnp.exp(sims - sim_total) - target) / local
    d_sims = jnp.where(good_row, d_sims, 0.0).astype(BF)

    for c in range(2):
        these = slice(c * side, (c + 1) * side)

        @pl.when((enc == 0) & (core == c))
        def _():
            d_cls[...] = tn(d_sims[:, these], passages)

        @pl.when((enc == 1) & (core == c))
        def _():
            d_cls[...] = nn(d_sims[these, :], questions)

    def column_sum(value):
        return jnp.sum(value, 0, keepdims=True)

    def back(upstream, unit, inverse, gain):
        scaled = upstream * gain
        return inverse[:, :1] * (
            scaled
            - jnp.mean(scaled, -1, keepdims=True)
            - unit * jnp.mean(scaled * unit, -1, keepdims=True)
        )

    vecs[pl.ds(0, 1), :] = column_sum(d_cls[...] * norm2[...])
    vecs[pl.ds(1, 1), :] = column_sum(d_cls[...])
    d_second = back(d_cls[...], norm2[...], inv2[...], gain2[...])
    douter[...] = d_second.astype(BF)
    d_active = nn(douter[...], down_turned[...])
    dinner[...] = (d_active * slope[...]).astype(BF)
    acc[...] = d_second + nn(dinner[...], up_turned[...])
    vecs[pl.ds(2, 1), :] = column_sum(acc[...] * norm1[...])
    vecs[pl.ds(3, 1), :] = column_sum(acc[...])
    vecs[pl.ds(4, 1), :] = jnp.broadcast_to(loss, (1, width))
    vecs[pl.ds(6, 2), :] = jnp.zeros((2, width), F32)
    d_first = back(acc[...], norm1[...], inv1[...], gain1[...])
    dfirst[...] = d_first
    datt[...] = d_first.astype(BF)

    dmix[core] = nn(datt[...], out_turned[...]).astype(BF)
    dmix_over = remote(dmix.at[core], dmix.at[core], fs_sem.at[11], fr_sem.at[11], (enc, sibling))
    dmix_back = remote(dmix.at[core], dmix.at[1 - core], fs_sem.at[11], fr_sem.at[11], (enc, sibling))

    dmix_over.start()

    block_diagonal(dbd, dmix[core, own, :].astype(F32))
    d_weights = nn(dbd[...], v_turned[...])
    weights = probs[...]
    inner_sum = jnp.sum(d_weights * weights, -1, keepdims=True)
    ds_low[...] = (head_scale * weights * (d_weights - inner_sum)).astype(BF)
    dx[...] = nn(ds_low[...], x[...]).astype(BF)
    send_pieces(dx, recv, key_owners, ks_sem, kr_sem)
    dq_own[...] = own_lanes(nn(ds_low[...], kv[:, pl.ds(0, width)])).astype(BF)

    def dq_place(peer):
        return dq_o.at[block(slot_of(peer))]

    save(dq_own, dq_place(me), 6)
    vecs[pl.ds(5, 1), :] = column_sum(dmix[core].astype(F32))

    def layer_tile(r):
        these = pl.ds(r * length, length)

        acc_t[...] = nn(mix[these, :], w_out[...]) + o_bias[...] + x[these, :].astype(F32)
        unit, _ = stats(acc_t[...])
        level = unit * gain1[...] + shift1[...]
        low_t[...] = level.astype(BF)
        inner = nn(low_t[...], w_up[...]) + u_bias[...]
        active = (0.5 * inner * (1.0 + lax.erf(inner * ROOT_HALF))).astype(BF)
        unit, _ = stats(level + d_bias[...] + nn(active, w_down[...]))
        hout[these, :] = (unit * gain2[...] + shift2[...]).astype(BF)
        save(hout.at[these], hidden_out.at[these], 13 + r)

    def piece_place(matrix, i):
        return kv_o.at[
            matrix,
            pl.ds(pl.multiple_of(lax.rem(i, 4) * group_cols, group_cols), group_cols),
            pl.ds(pl.multiple_of(lax.div(i, 4) * half_feats, half_feats), half_feats),
        ]

    def key_place(peer):
        return piece_place(0, lax.div(peer, 2))

    def value_place(peer):
        return piece_place(1, lax.rem(peer, half_n))

    keys = Relay(piece, key_place, gs_sem, gr_sem, n)
    values = Relay(piece_v, value_place, hs_sem, hr_sem, half_n)
    key_save = pltpu.make_async_copy(piece, key_place(me), save_sem.at[16])

    def sum_pieces(i, left, right, target):
        for a in range(H // 4):
            rows_a = right[:, pl.ds(a * PAD, PAD), :].reshape(2 * side, half_feats)
            start = lax.rem(i, 4) * group_cols + a * head
            cols_a = left[pl.ds(pl.multiple_of(start, head), head), :]
            target[pl.ds(a * head, head), :] = nn(cols_a, rows_a).astype(BF)

    pieces_came(recv_v, vr_sem)
    dmix_back.wait_recv()
    for c in range(2):
        turned_v[:, pl.ds(c * side, side)] = dmix[c].astype(F32).T.astype(BF)
    sum_pieces(lax.rem(me, half_n), turned_v, recv_v, piece_v)
    values.start()
    save(piece_v, value_place(me), 10)

    for r in range(2, rows):
        attend_row(r)

    @pl.when(core == 0)
    def _():
        pieces_came(recv, kr_sem)
        sum_pieces(which, turned, recv, piece)
        keys.start()
        key_save.start()

    give(douter, douter_o, 7)
    give(dinner, dinner_o, 8)
    give(datt, datt_o, 9)
    values.plane()
    layer_tile(0)
    layer_tile(1)
    values.over()
    share(dq_own, dq_place, qs_sem, qr_sem)
    remote(dq_own, dq_place(me), qs_sem.at[n - 2], qr_sem.at[me], (enc, sibling)).start()

    @pl.when(core == 0)
    def _():
        keys.plane()

    layer_tile(2)

    base = dfirst[own, :] + nt(dq_own[...], w_qkv[:, query_w])
    base = base.astype(BF)
    qk[...] = nt(qbd[...], w_qkv[:, key_w]).astype(BF)
    dv[...] = nt(dbd[...], w_qkv[:, value_w]).astype(BF)
    y = tn(ds_low[...], qk[...]) + tn(p_low[...], dv[...]) + tn(pick, base)
    hgrad[...] = y.astype(BF)
    save(hgrad, hidden_grad, 17)
    vecs_give = remote(vecs, vecs_o.at[core], fs_sem.at[12], fr_sem.at[12], (enc, sibling))
    vecs_give.start()
    vecs_take = remote(vecs, vecs_o.at[1 - core], fs_sem.at[12], fr_sem.at[12], (enc, sibling))
    save(vecs, vecs_o.at[core], 12)

    def dq_pass(j):
        peer = same_core(j)
        remote(dq_own, dq_place(peer), qs_sem.at[j], qr_sem.at[peer], (enc, peer)).wait_recv()
        send = qs_sem.at[n // 2 - 1 + j]
        remote(dq_place(peer), dq_place(peer), send, qr_sem.at[peer], (enc, sibling)).start()

    loop(n // 2 - 1, dq_pass)
    sent_pieces(px, recv_v, range(n), vs_sem, vr_sem)
    sent_pieces(dx, recv, key_owners, ks_sem, kr_sem)
    xcls_back.wait_send()
    dmix_over.wait_send()
    for copy in [*given, vecs_take]:
        copy.wait_send()
        copy.wait_recv()
    values.sent()
    values.came()
    for copy in saves[:-1]:
        copy.wait()

    @pl.when(core == 0)
    def _():
        key_save.wait()
        keys.over()

    def dq_came(j):
        peer = cousin(j)
        remote(dq_own, dq_place(peer), qs_sem.at[0], qr_sem.at[peer], (enc, sibling)).wait_recv()

    loop(n // 2, dq_came)

    def dq_sent(j):
        remote(dq_own, dq_place(me), qs_sem.at[j], qr_sem.at[me], (enc, sibling)).wait_send()

    loop(n - 1, dq_sent)

    @pl.when(core == 0)
    def _():
        keys.sent()

    @pl.when(core == 1)
    def _():
        keys.came()

    saves[-1].wait()


def grad_kernel(
    xcls_i,
    mixed_i,
    normed_i,
    act_i,
    douter_i,
    dinner_i,
    datt_i,
    dq_i,
    kv_i,
    hidden_out_i,
    hidden_grad_i,
    vecs,
    loss,
    hidden_out,
    hidden_grad,
    grad_qkv,
    grad_query_bias,
    grad_value_bias,
    grad_out,
    grad_out_bias,
    grad_first_gain,
    grad_first_shift,
    grad_up,
    grad_up_bias,
    grad_down,
    grad_down_bias,
    grad_second_gain,
    grad_second_shift,
    xcls,
    mixed,
    normed,
    act,
    douter,
    dinner,
    datt,
    dq,
    kv,
    g_qkv,
    g_out,
    g_up,
    g_down,
    h_out,
    h_grad,
    in_sem,
    out_sem,
):
    width = xcls.shape[1]
    ins = {}
    loads = [
        ("mixed", mixed_i, mixed),
        ("datt", datt_i, datt),
        ("act", act_i, act),
        ("douter", douter_i, douter),
        ("normed", normed_i, normed),
        ("dinner", dinner_i, dinner),
        ("xcls", xcls_i, xcls),
        ("dq", dq_i, dq),
        ("kv", kv_i, kv),
        ("h_out", hidden_out_i, h_out),
        ("h_grad", hidden_grad_i, h_grad),
    ]
    for index, (name, source, target) in enumerate(loads):
        ins[name] = pltpu.make_async_copy(source, target, in_sem.at[index])
        ins[name].start()

    def column_sum(value):
        return jnp.sum(value.astype(F32), 0, keepdims=True)

    def vector(row):
        return vecs[0, pl.ds(row, 1), :] + vecs[1, pl.ds(row, 1), :]

    def put(source, target, rows, index):
        pltpu.make_async_copy(source.at[rows], target.at[0, rows], out_sem.at[index]).start()

    loss[...] = vecs[0, pl.ds(4, 1), pl.ds(0, 1)]
    grad_second_gain[...] = vector(0)
    grad_second_shift[...] = vector(1)
    grad_first_gain[...] = vector(2)
    grad_first_shift[...] = vector(3)
    grad_value_bias[...] = vector(5)

    ins["mixed"].wait()
    ins["datt"].wait()
    g_out[...] = tn(mixed[...], datt[...])
    put(g_out, grad_out, pl.ds(0, width), 4)
    ins["act"].wait()
    ins["douter"].wait()
    for j in range(4):
        these = pl.ds(j * width, width)
        g_down[these, :] = tn(act[:, these], douter[...])
        put(g_down, grad_down, these, 2)
    ins["normed"].wait()
    ins["dinner"].wait()
    for j in range(3):
        these = pl.ds(j * 256, 256)
        g_up[these, :] = tn(normed[:, these], dinner[...])
        put(g_up, grad_up, these, 3)
    ins["xcls"].wait()
    ins["dq"].wait()
    ins["kv"].wait()
    for j in range(3):
        these = pl.ds(j * 256, 256)
        g_qkv[these, pl.ds(0, width)] = tn(xcls[:, these], dq[...])
        for m in range(2):
            g_qkv[these, pl.ds((m + 1) * width, width)] = kv[m, :, these].astype(F32).T
        put(g_qkv, grad_qkv, these, 5)
    through = [
        pltpu.make_async_copy(h_out, hidden_out, out_sem.at[0]),
        pltpu.make_async_copy(h_grad, hidden_grad, out_sem.at[1]),
    ]
    for name, copy in zip(("h_out", "h_grad"), through):
        ins[name].wait()
        copy.start()
    grad_down_bias[...] = column_sum(douter[...])
    grad_up_bias[...] = column_sum(dinner[...])
    grad_out_bias[...] = column_sum(datt[...])
    grad_query_bias[...] = column_sum(dq[...])
    pltpu.make_async_copy(g_down, grad_down.at[0], out_sem.at[2]).wait()
    pltpu.make_async_copy(g_up, grad_up.at[0], out_sem.at[3]).wait()
    pltpu.make_async_copy(g_out, grad_out.at[0], out_sem.at[4]).wait()
    pltpu.make_async_copy(g_qkv, grad_qkv.at[0], out_sem.at[5]).wait()
    for copy in through:
        copy.wait()


def fused_on_device(n, *args):
    (
        hidden_in,
        starts,
        positives,
        qkv_weight,
        query_bias,
        value_bias,
        out_weight,
        out_bias,
        first_gain,
        first_shift,
        up_weight,
        up_bias,
        down_weight,
        down_bias,
        second_gain,
        second_shift,
    ) = args
    rows, length, width = hidden_in.shape[1:]
    tokens = rows * length
    ff = up_weight.shape[-1]
    wide = n * PAD
    side = wide // 2
    spreads = H * PAD
    planes = n // 4
    shape = jax.ShapeDtypeStruct
    hbm = pl.BlockSpec(memory_space=pl.ANY)
    vmem = pl.BlockSpec(memory_space=pltpu.VMEM)
    smem = pl.BlockSpec(memory_space=pltpu.SMEM)
    dma = pltpu.SemaphoreType.DMA
    limit = 60 * 1024 * 1024
    outs = pl.pallas_call(
        functools.partial(main_kernel, n),
        out_shape=[
            shape((tokens, width), BF),
            shape((tokens, width), BF),
            shape((wide, width), BF),
            shape((wide, width), BF),
            shape((wide, width), BF),
            shape((wide, ff), BF),
            shape((wide, width), BF),
            shape((wide, ff), BF),
            shape((wide, width), BF),
            shape((wide, width), BF),
            shape((2, 8, width), F32),
            shape((2, width, width), BF),
        ],
        in_specs=[smem, vmem, hbm, hbm, vmem, vmem, hbm, vmem, vmem, vmem, hbm, vmem, hbm, vmem, vmem, vmem],
        out_specs=[hbm] * 12,
        scratch_shapes=[
            pltpu.VMEM((tokens, width), BF),
            pltpu.VMEM((width, 3 * width), BF),
            pltpu.VMEM((width, width), BF),
            pltpu.VMEM((width, ff), BF),
            pltpu.VMEM((ff, width), BF),
            pltpu.VMEM((width, width), BF),
            pltpu.VMEM((ff, width), BF),
            pltpu.VMEM((width, ff), BF),
            pltpu.VMEM((width, tokens), BF),
            pltpu.VMEM((tokens, 2 * width), BF),
            pltpu.VMEM((tokens, width), BF),
            pltpu.VMEM((tokens, width), BF),
            pltpu.VMEM((length, length), F32),
            pltpu.VMEM((spreads, width), BF),
            pltpu.VMEM((spreads, width), BF),
            pltpu.VMEM((spreads, width), BF),
            pltpu.VMEM((spreads, width), BF),
            pltpu.VMEM((spreads, tokens), F32),
            pltpu.VMEM((spreads, tokens), BF),
            pltpu.VMEM((spreads, tokens), BF),
            pltpu.VMEM((spreads, width), BF),
            pltpu.VMEM((spreads, width), BF),
            pltpu.VMEM((2, side, width), BF),
            pltpu.VMEM((side, width), BF),
            pltpu.VMEM((2, 2, side, width), BF),
            pltpu.VMEM((2, 2, side // PAD * rows * DOCS, width), BF),
            pltpu.VMEM((side, width), F32),
            pltpu.VMEM((side, 128), F32),
            pltpu.VMEM((side, width), F32),
            pltpu.VMEM((side, 128), F32),
            pltpu.VMEM((side, width), BF),
            pltpu.VMEM((side, ff), BF),
            pltpu.VMEM((side, ff), F32),
            pltpu.VMEM((side, ff), BF),
            pltpu.VMEM((side, width), BF),
            pltpu.VMEM((side, width), BF),
            pltpu.VMEM((2, side, width), BF),
            pltpu.VMEM((side, width), F32),
            pltpu.VMEM((side, width), F32),
            pltpu.VMEM((side, width), F32),
            pltpu.VMEM((8, width), F32),
            pltpu.VMEM((width, wide), BF),
            pltpu.VMEM((n, H // 4 * PAD, width // 2), BF),
            pltpu.VMEM((width // 4, width // 2), BF),
            pltpu.VMEM((width, wide), BF),
            pltpu.VMEM((n, H // 4 * PAD, width // 2), BF),
            pltpu.VMEM((width // 4, width // 2), BF),
            pltpu.VMEM((PAD, width), BF),
            pltpu.VMEM((length, width), BF),
            pltpu.VMEM((length, width), F32),
            pltpu.VMEM((tokens, width), BF),
            pltpu.VMEM((tokens, width), BF),
            dma((7,)),
            dma((18,)),
            dma((n // 2,)),
            dma((n,)),
            dma((n // 2,)),
            dma((n,)),
            dma((n // 2,)),
            dma((n,)),
            dma((3,)),
            dma((3,)),
            dma((n - 1,)),
            dma((n,)),
            dma((n,)),
            dma((n,)),
            dma((n,)),
            dma((n,)),
            dma((n,)),
            dma((n,)),
            dma((13,)),
            dma((13,)),
        ],
        compiler_params=pltpu.CompilerParams(
            collective_id=0, has_side_effects=True, vmem_limit_bytes=limit
        ),
        name="layer",
    )(
        jnp.transpose(starts, (1, 0, 2)),
        positives,
        hidden_in.reshape(tokens, width),
        qkv_weight.reshape(width, 3 * width),
        query_bias,
        value_bias,
        out_weight.reshape(width, width),
        out_bias,
        first_gain,
        first_shift,
        up_weight.reshape(width, ff),
        up_bias,
        down_weight.reshape(ff, width),
        down_bias,
        second_gain,
        second_shift,
    )
    h_out, h_grad, xcls, mixed, normed, act, douter, dinner, datt, dq, vecs, kv = outs
    row = shape((1, width), F32)
    grads = pl.pallas_call(
        grad_kernel,
        out_shape=[
            shape((1, 1), F32),
            shape((tokens, width), BF),
            shape((tokens, width), BF),
            shape((1, width, 3 * width), F32),
            row,
            row,
            shape((1, width, width), F32),
            row,
            row,
            row,
            shape((1, width, ff), F32),
            shape((1, ff), F32),
            shape((1, ff, width), F32),
            row,
            row,
            row,
        ],
        in_specs=[hbm] * 11 + [vmem],
        out_specs=[vmem, hbm, hbm, hbm, vmem, vmem, hbm, vmem, vmem, vmem, hbm, vmem, hbm, vmem, vmem, vmem],
        scratch_shapes=[
            pltpu.VMEM((wide, width), BF),
            pltpu.VMEM((wide, width), BF),
            pltpu.VMEM((wide, width), BF),
            pltpu.VMEM((wide, ff), BF),
            pltpu.VMEM((wide, width), BF),
            pltpu.VMEM((wide, ff), BF),
            pltpu.VMEM((wide, width), BF),
            pltpu.VMEM((wide, width), BF),
            pltpu.VMEM((2, width, width), BF),
            pltpu.VMEM((width, 3 * width), F32),
            pltpu.VMEM((width, width), F32),
            pltpu.VMEM((width, ff), F32),
            pltpu.VMEM((ff, width), F32),
            pltpu.VMEM((tokens, width), BF),
            pltpu.VMEM((tokens, width), BF),
            dma((11,)),
            dma((6,)),
        ],
        compiler_params=pltpu.CompilerParams(vmem_limit_bytes=limit),
        name="gradients",
    )(xcls, mixed, normed, act, douter, dinner, datt, dq, kv, h_out, h_grad, vecs)
    place = (1, rows, length, width)
    return (
        grads[0].reshape(()),
        grads[1].reshape(place),
        grads[2].reshape(place),
        *grads[3:],
    )


def solution(mesh):
    placed = (
        P("enc", "dp", None, None),
        P("enc", "dp", None),
        P(),
        P("enc", None, None),
        P("enc", None),
        P("enc", None),
        P("enc", None, None),
        P("enc", None),
        P("enc", None),
        P("enc", None),
        P("enc", None, None),
        P("enc", None),
        P("enc", None, None),
        P("enc", None),
        P("enc", None),
        P("enc", None),
    )
    n = mesh.shape["dp"]
    body = functools.partial(fused_on_device, n) if n == OWNERS else on_device
    return jax.shard_map(
        body,
        mesh=mesh,
        in_specs=placed,
        out_specs=(
            P(),
            P("enc", "dp", None, None),
            P("enc", "dp", None, None),
            P("enc", None, None),
            P("enc", None),
            P("enc", None),
            P("enc", None, None),
            P("enc", None),
            P("enc", None),
            P("enc", None),
            P("enc", None, None),
            P("enc", None),
            P("enc", None, None),
            P("enc", None),
            P("enc", None),
            P("enc", None),
        ),
        check_vma=False,
    )
```
